512 devices in a mesh: gx: 16 (over y_hi, x, core), gy: 4 (over y_lo), gz: 8 (over z).
Axes of the slice: x: 4, y: 8 (y_hi: 2, y_lo: 4; y = y_hi * 4 + y_lo), z: 8, core: 2. Of those that a mesh axis runs over, the one named last changes fastest.
Arguments:
- velocity: float32 [3, 32, 4, 32, 512], P(None, 'gx', 'gy', 'gz'), may hold values from -4 to 4
- reaction: float32 [32, 4, 32, 512], P('gx', 'gy', 'gz'), may hold values from 10 to 100
Outputs:
- velocity_out: float32 [3, 32, 4, 32, 512], P(None, 'gx', 'gy', 'gz')
- pressure: float32 [32, 4, 32, 512], P('gx', 'gy', 'gz')
- residual: float32 [32, 4, 32, 512], P('gx', 'gy', 'gz')
The draws below stay inside these ranges and needn't reach their ends.
All inputs are finite; a program needn't handle non-finite values.
Results may differ from the reference program's by a relative error of at most 0.007.
Values sent between devices are 32-bit elements; how exact they have to be, the bound alone decides.
A program may use at most 64 MiB of HBM per device.

```python
import math
import jax
import jax.numpy as jnp
import numpy as np
from jax import lax

ELEMENT_NODES = 512
SUBSTEPS = 2
ITERS = 4
ELEMENTS_AXIAL = 32
ELEMENTS_CROSS = 4
ELEMENTS_DEPTH = 32


def level_of(stream_key, dims, pieces, low, largest):
    def one(dim, parts):
        steps = jax.random.uniform(jax.random.fold_in(jax.random.fold_in(stream_key, 6), dim), (parts,), jnp.float32, low / len(pieces), largest / len(pieces))
        return jnp.repeat(jnp.exp(steps), dims[dim] // parts).reshape((-1,) + (1,) * (len(dims) - dim - 1))

    level = one(*pieces[0])
    for cut in pieces[1:]:
        level = level * one(*cut)
    return level


def centred(rng, extent, width, reach, cuts=(), dtype=jnp.bfloat16):
    factor_of = level_of(rng, extent, cuts, -0.22, 0.18) if cuts else 1.0
    values = jax.random.normal(rng, extent, jnp.float32) * width * factor_of
    return jnp.minimum(jnp.maximum(values, -reach), reach).astype(dtype)


def setup_inputs(seed: int = 0) -> dict:
    key_of = jax.random.split(jax.random.key(seed), 3)
    return {
        "velocity": centred(key_of[0], (3, ELEMENTS_AXIAL, ELEMENTS_CROSS, ELEMENTS_DEPTH, ELEMENT_NODES), 1.0, 4.0, ((1, 16), (2, 4), (3, 8)), jnp.float32),
        "reaction": jnp.clip(jnp.exp(math.log(100.0) - 2.3025851 * jax.random.uniform(key_of[1], (ELEMENTS_AXIAL, ELEMENTS_CROSS, ELEMENTS_DEPTH, ELEMENT_NODES), jnp.float32) ** level_of(key_of[1], (ELEMENTS_AXIAL, ELEMENTS_CROSS, ELEMENTS_DEPTH, ELEMENT_NODES), ((0, 16), (1, 4), (2, 8)), -0.2, 0.2)), 10.0, 100.0),
    }


step_size = 0.02


def legendre_seven(points):
    earlier = points * 0.0 + 1.0
    current = points
    for degree in range(1, 7):
        earlier, current = current, ((2 * degree + 1) * points * current - degree * earlier) / (degree + 1)
    return current


def tables():
    half = np.array([0.2092992179024788687, 0.5917001814331423022, 0.8717401485096066153, 1.0])
    points = np.concatenate([-half[::-1], half])
    legendre = legendre_seven(points)
    weights = 2.0 / (56.0 * legendre ** 2)
    spacing = points[:, None] - points[None, :] + np.eye(8)
    derivative = (legendre[:, None] / legendre[None, :]) / spacing * (1.0 - np.eye(8))
    derivative[0, 0] = -14.0
    derivative[7, 7] = 14.0
    return jnp.asarray(weights, jnp.float32), jnp.asarray(derivative, jnp.float32)


def derive(values, derivative, along_dim, transposed):
    matrix = derivative.T if transposed else derivative
    layout = values.shape
    blocks = values.reshape(-1, 8, 8, 8)
    patterns = ("aq,nqbc->nabc", "bq,naqc->nabc", "cq,nabq->nabc")
    result = jnp.einsum(patterns[along_dim], matrix, blocks, precision=lax.Precision.HIGHEST)
    return result.reshape(layout)


def place_face(values, target_axis, position, update):
    selector = tuple(position if place == target_axis else slice(None) for place in range(values.ndim))
    return values.at[selector].set(update)


def join_faces(values, along_dim, periodic):
    lower_face = jnp.moveaxis(jnp.take(values, 0, axis=4 + along_dim), 1 + along_dim, 0)
    upper_face = jnp.moveaxis(jnp.take(values, 7, axis=4 + along_dim), 1 + along_dim, 0)
    elements = lower_face.shape[0]
    face_shape = lower_face.shape
    sequence = jnp.stack([lower_face, upper_face], axis=1).reshape(2 * elements, -1)
    if periodic:
        leading = sequence[-1:]
        trailing = sequence[:1]
    else:
        leading = jnp.zeros_like(sequence[:1])
        trailing = jnp.zeros_like(sequence[:1])
    padded = jnp.concatenate([leading, sequence, trailing], axis=0)
    paired = padded.reshape(elements + 1, 2, -1)
    totals = paired[:, 0] + paired[:, 1]
    new_lower = jnp.moveaxis(totals[:-1].reshape(face_shape), 0, 1 + along_dim)
    new_upper = jnp.moveaxis(totals[1:].reshape(face_shape), 0, 1 + along_dim)
    values = place_face(values, 4 + along_dim, 0, new_lower)
    return place_face(values, 4 + along_dim, 7, new_upper)


def assemble(values):
    values = join_faces(values, 0, True)
    values = join_faces(values, 1, False)
    return join_faces(values, 2, False)


def dim_factors(local_count, offset, total_count, bounded_by_walls):
    element_ids = offset + jnp.arange(local_count)
    node_ids = jnp.arange(8)
    at_end = (node_ids[None, :] == 0) | (node_ids[None, :] == 7)
    low_wall = (element_ids[:, None] == 0) & (node_ids[None, :] == 0)
    high_wall = (element_ids[:, None] == total_count - 1) & (node_ids[None, :] == 7)
    on_wall = (low_wall | high_wall) & bounded_by_walls
    shared = at_end & jnp.logical_not(on_wall)
    return jnp.where(shared, 2.0, 1.0).astype(jnp.float32), on_wall.astype(jnp.float32)


def reference(velocity, reaction):
    weights, derivative = tables()
    count_x, count_y, count_z = reaction.shape[0], reaction.shape[1], reaction.shape[2]
    speed = velocity.reshape(3, count_x, count_y, count_z, 8, 8, 8)
    react = reaction.reshape(1, count_x, count_y, count_z, 8, 8, 8)
    mass_matrix = weights[:, None, None] * weights[None, :, None] * weights[None, None, :]
    factor_x, wall_x = dim_factors(count_x, 0, count_x, False)
    factor_y, wall_y = dim_factors(count_y, 0, count_y, True)
    factor_z, wall_z = dim_factors(count_z, 0, count_z, True)
    multiplicity = (factor_x[None, :, None, None, :, None, None] * factor_y[None, None, :, None, None, :, None]
                    * factor_z[None, None, None, :, None, None, :])
    interior = ((1.0 - wall_y[None, None, :, None, None, :, None]) * (1.0 - wall_z[None, None, None, :, None, None, :]))
    speed = assemble(speed) / multiplicity
    for substep in range(SUBSTEPS):
        gradient_fields = [derive(speed, derivative, along_dim, False) for along_dim in range(3)]
        transport = speed[0:1] * gradient_fields[0] + speed[1:2] * gradient_fields[1] + speed[2:3] * gradient_fields[2]
        tendency = assemble(mass_matrix * transport) / (mass_matrix * multiplicity)
        speed = interior * (speed - step_size * tendency)
    spread = (derive(speed[0:1], derivative, 0, False) + derive(speed[1:2], derivative, 1, False)
              + derive(speed[2:3], derivative, 2, False))
    source = -assemble(mass_matrix * spread)
    stiff_sum = jnp.sum(weights[:, None] * derivative * derivative, axis=0)
    diag_local = (stiff_sum[:, None, None] * weights[None, :, None] * weights[None, None, :]
                  + weights[:, None, None] * stiff_sum[None, :, None] * weights[None, None, :]
                  + weights[:, None, None] * weights[None, :, None] * stiff_sum[None, None, :])
    diagonal = assemble(diag_local + react * mass_matrix)

    def apply_operator(search_vec):
        local_sum = react * mass_matrix * search_vec
        for along_dim in range(3):
            local_sum = local_sum + derive(mass_matrix * derive(search_vec, derivative, along_dim, False), derivative, along_dim, True)
        return assemble(local_sum)

    def inner_product(first, second):
        return jnp.sum(first * second / multiplicity)

    pressure = jnp.zeros_like(source)
    residual = source
    precond = residual / diagonal
    search = precond
    progress = inner_product(residual, precond)
    for sweep_index in range(ITERS):
        applied = apply_operator(search)
        step_length = progress / inner_product(search, applied)
        pressure = pressure + step_length * search
        residual = residual - step_length * applied
        precond = residual / diagonal
        progress_next = inner_product(residual, precond)
        search = precond + (progress_next / progress) * search
        progress = progress_next
    return (speed.reshape(3, count_x, count_y, count_z, 512),
            pressure.reshape(count_x, count_y, count_z, 512),
            residual.reshape(count_x, count_y, count_z, 512))
```

```python
import jax
import jax.numpy as jnp
import numpy as np
from jax import lax
from jax.experimental import pallas as pl
from jax.experimental.pallas import tpu as pltpu
from jax.sharding import PartitionSpec as P

MESH = pl.DeviceIdType.MESH
STEP = 0.02
HALF = 64
OFFSETS = ((-1, 0), (1, 0), (0, -1), (0, 1), (-1, -1), (1, -1), (-1, 1), (1, 1))
ROUND_FIELDS = (4, 3, 3, 1, 1, 1, 1, 1)


def roll(values, shift, axis):
    shift = shift % values.shape[axis]
    return values if shift == 0 else pltpu.roll(values, shift, axis)


def div(value, by):
    return value // by if isinstance(value, (int, np.ndarray)) else lax.div(value, np.int32(by))


def rem(value, by):
    return value % by if isinstance(value, (int, np.ndarray)) else lax.rem(value, np.int32(by))


def tables():
    half = np.array([0.2092992179024788687, 0.5917001814331423022, 0.8717401485096066153, 1.0])
    points = np.concatenate([-half[::-1], half])
    earlier, current = points * 0.0 + 1.0, points
    for degree in range(1, 7):
        earlier, current = current, ((2 * degree + 1) * points * current - degree * earlier) / (degree + 1)
    w = 2.0 / (56.0 * current**2)
    spacing = points[:, None] - points[None, :] + np.eye(8)
    d = current[:, None] / current[None, :] / spacing * (1.0 - np.eye(8))
    d[0, 0] = -14.0
    d[7, 7] = 14.0
    k = d.T @ np.diag(w) @ d
    lane = np.arange(128)
    c, b, a_lo = lane % 8, (lane // 8) % 8, lane // 64
    rows = {}

    def put(name, values):
        rows[name] = (len(stack), len(values))
        stack.extend(values)

    stack = []

    def along_a(matrix, scale):
        return [matrix[2 * j + a_lo, q] * scale for j in range(4) for q in range(8)]

    def shifts(matrix, index, scale):
        out = []
        for s in range(-7, 8):
            source = index - s
            inside = (source >= 0) & (source <= 7)
            out.append(np.where(inside, matrix[index, np.clip(source, 0, 7)], 0.0) * scale)
        return out

    one = np.ones(128)
    put("da", along_a(d, one))
    put("db", shifts(d, b, one))
    put("dc", shifts(d, c, one))
    put("ka", along_a(k, w[b] * w[c]))
    put("kb", shifts(k, b, w[c]))
    put("kc", shifts(k, c, w[b]))
    put("wa", [w[2 * i + a_lo] for i in range(4)])
    mass = [w[2 * i + a_lo] * w[b] * w[c] for i in range(4)]
    put("mass", mass)
    put("tend", [STEP / m for m in mass])
    s = (w[:, None] * d * d).sum(0)
    put("diag", [s[2 * i + a_lo] * w[b] * w[c] + w[2 * i + a_lo] * s[b] * w[c] + w[2 * i + a_lo] * w[b] * s[c] for i in range(4)])
    table = np.stack(stack).astype(np.float32)
    return np.ascontiguousarray(np.broadcast_to(table[:, None, :], (len(stack), 8, 128))), rows


TABLE, ROWS = tables()


def owner_of(axial, depth):
    y, core = div(axial, 2), rem(axial, 2)
    z, turn = div(depth, 4), rem(depth, 4)
    x = turn + rem(z, 2) * (3 - 2 * turn)
    return (div(y, 4) * 8 + x * 2 + core, rem(y, 4), z)


class Place:
    def __init__(self, gx, gy, gz):
        self.gx, self.gy, self.gz = gx, gy, gz
        self.core, self.x, self.y_hi = rem(gx, 2), rem(div(gx, 2), 4), div(gx, 8)
        self.y, self.z = self.y_hi * 4 + gy, gz
        self.axial = self.y * 2 + self.core
        self.turn = self.x + rem(gz, 2) * (3 - 2 * self.x)
        self.depth = self.z * 4 + self.turn

    def mesh_id(self, x, y, z, core):
        return (div(y, 4) * 8 + x * 2 + core, rem(y, 4), z)

    def neighbour(self, dx, dz):
        return owner_of(rem(self.axial + dx + 16, 16), rem(self.depth + dz + 32, 32))

    def worker(self, i):
        x = rem(self.x + i, 4)
        return self.mesh_id(x, self.y_hi * 4 + self.x, self.z, self.core), x + rem(self.z, 2) * (3 - 2 * x)

    def home(self, i):
        cross = rem(self.gy + i, 4)
        return self.mesh_id(self.gy, self.y_hi * 4 + cross, self.z, self.core), cross

    def group(self, stage, i):
        if stage == 0:
            me = self.x * 2 + self.core
            other = rem(me + i, 8)
            return self.mesh_id(div(other, 2), self.y, self.z, rem(other, 2)), me
        if stage == 1:
            return self.mesh_id(self.x, rem(self.y + i, 8), self.z, self.core), self.y
        return self.mesh_id(self.x, self.y, rem(self.z + i, 8), self.core), self.z


class Masks:
    def __init__(self, depth):
        lane = lax.broadcasted_iota(jnp.int32, (8, 128), 1)
        row = lax.broadcasted_iota(jnp.int32, (8, 128), 0)
        c, b = lane & 7, (lane >> 3) & 7
        cross = row >> 1
        self.low = lane < HALF
        self.even = (row & 1) == 0
        odd = (row & 1) == 1
        high = lane >= HALF
        self.b0 = (b == 0) & (cross > 0)
        self.b7 = (b == 7) & (cross < 3)
        self.in0 = odd & self.low
        self.in3 = self.even & high
        self.out0 = self.even & self.low
        self.out3 = odd & high
        self.c = c
        self.c0, self.c7 = c == 0, c == 7
        self.slot_low = c < 4
        self.edge0 = self.out0 & ((c & 3) == 0)
        self.edge3 = self.out3 & ((c & 3) == 3)
        up = (depth < 31).astype(jnp.float32)
        down = (depth > 0).astype(jnp.float32)
        self.zmask = jnp.where(self.slot_low, up, down)
        one = jnp.ones((8, 128), jnp.float32)
        iy = jnp.where(self.b0 | self.b7, 0.5, one)
        iz = jnp.where(self.c0, 1.0 - 0.5 * down, jnp.where(self.c7, 1.0 - 0.5 * up, one))
        iyz = iy * iz
        self.inverse = [iyz * jnp.where(self.low, 0.5, one), iyz, iyz, iyz * jnp.where(self.low, one, 0.5)]
        wall_y = ((b == 0) & (cross == 0)) | ((b == 7) & (cross == 3))
        self.interior = jnp.where(wall_y, 0.0, jnp.where(self.c0, down, jnp.where(self.c7, up, one)))


def join_block(v, m):
    out = []
    for x in v:
        g = roll(roll(x, 2, 1), -56, 2)
        h = roll(roll(x, -2, 1), 56, 2)
        out.append(x + jnp.where(m.b0, g, jnp.where(m.b7, h, 0.0)))
    first = roll(roll(out[3], 1, 1), HALF, 2)
    last = roll(roll(out[0], -1, 1), HALF, 2)
    out[0] = out[0] + jnp.where(m.in0, first, 0.0)
    out[3] = out[3] + jnp.where(m.in3, last, 0.0)
    return out


def pack(v, m):
    axial = jnp.where(m.low, v[0], v[3])
    depth = v[0]
    for i in range(1, 4):
        depth = jnp.where(m.c == i, roll(v[i], i, 2), depth)
    for i in range(4):
        depth = jnp.where(m.c == 4 + i, roll(v[i], i - 3, 2), depth)
    return axial, depth


def unpack(v, got, m):
    v = list(v)
    v[0] = v[0] + jnp.where(m.out0, roll(roll(got[0], -1, 1), HALF, 2), 0.0)
    v[3] = v[3] + jnp.where(m.out3, roll(roll(got[1], 1, 1), HALF, 2), 0.0)
    centre = jnp.where(m.slot_low, got[3], got[2])
    before = jnp.where(m.slot_low, got[6], got[4])
    after = jnp.where(m.slot_low, got[7], got[5])
    face = centre + jnp.where(m.edge0, roll(roll(before, -1, 1), -67, 2), 0.0)
    face = face + jnp.where(m.edge3, roll(roll(after, 1, 1), 67, 2), 0.0)
    face = face * m.zmask
    return [
        v[i] + jnp.where(m.c7, roll(face, 7 - i, 2), jnp.where(m.c0, roll(face, -4 - i, 2), 0.0))
        for i in range(4)
    ]


def along_a(v, get, name, m):
    parts = []
    for x in v:
        turned = roll(x, HALF, 2)
        parts.append(jnp.where(m.low, x, turned))
        parts.append(jnp.where(m.low, turned, x))
    start = ROWS[name][0]
    return [sum_of([get(start + j * 8 + q) * parts[q] for q in range(8)]) for j in range(4)]


def along_lanes(v, get, name, stride):
    start = ROWS[name][0]
    return [sum_of([get(start + s + 7) * roll(x, s * stride, 2) for s in range(-7, 8)]) for x in v]


def sum_of(terms):
    while len(terms) > 1:
        terms = [terms[i] + terms[i + 1] if i + 1 < len(terms) else terms[i] for i in range(0, len(terms), 2)]
    return terms[0]


def constant(get, name):
    return [get(ROWS[name][0] + i) for i in range(4)]


def transport(u, get, m):
    da = along_a(u, get, "da", m)
    db = along_lanes(u, get, "db", 8)
    dc = along_lanes(u, get, "dc", 1)
    mass = constant(get, "mass")
    return [mass[i] * (u[i][0:1] * da[i] + u[i][1:2] * db[i] + u[i][2:3] * dc[i]) for i in range(4)]


def divergence(u, get, m):
    da = along_a([x[0:1] for x in u], get, "da", m)
    db = along_lanes([x[1:2] for x in u], get, "db", 8)
    dc = along_lanes([x[2:3] for x in u], get, "dc", 1)
    mass = constant(get, "mass")
    return [-mass[i] * (da[i] + db[i] + dc[i]) for i in range(4)]


def stiffness(p, scaled, get, m):
    ka = along_a(p, get, "ka", m)
    kb = along_lanes(p, get, "kb", 8)
    kc = along_lanes(p, get, "kc", 1)
    wa = constant(get, "wa")
    return [ka[i] + wa[i] * (kb[i] + kc[i]) + scaled[i] * p[i] for i in range(4)]


def moment(f, g, weight=None):
    total = sum_of([f[i][0] * g[i][0] if weight is None else f[i][0] * g[i][0] * weight[i] for i in range(4)])
    return jnp.sum(total, axis=0, keepdims=True)


def solve(n, e):
    g = [[(n[i + j] + n[i + j + 1]) if i + j < 6 else e for j in range(4)] for i in range(4)]
    rhs = [n[i] for i in range(4)]
    inverse = []
    for i in range(4):
        inverse.append(1.0 / g[i][i])
        for r in range(i + 1, 4):
            factor = g[r][i] * inverse[i]
            for j in range(i + 1, 4):
                g[r][j] = g[r][j] - factor * g[i][j]
            rhs[r] = rhs[r] - factor * rhs[i]
    out = [None] * 4
    for i in range(3, -1, -1):
        total = rhs[i]
        for j in range(i + 1, 4):
            total = total - g[i][j] * out[j]
        out[i] = total * inverse[i]
    return out


def kernel(vel_hbm, react_hbm, table_hbm, velo_ref, press_ref, resid_ref, vel, react, tab, load_sem,
           send0, recv0, sem0, *rest):
    rounds = len(ROUND_FIELDS)
    send_x, send_z = rest[0:rounds], rest[rounds:2 * rounds]
    got_refs = rest[2 * rounds:3 * rounds]
    (round_sem, sums, part, sum_sem, back_send, back_recv, back_sem, scratch) = rest[3 * rounds:]
    place = Place(lax.axis_index("gx"), lax.axis_index("gy"), lax.axis_index("gz"))

    def push(pairs, device, send_sem, recv_sem, own=None):
        def remote():
            for source, target in pairs:
                pltpu.make_async_remote_copy(source, target, send_sem, recv_sem,
                                             device_id=device, device_id_type=MESH).start()

        if own is None:
            remote()
            return
        pl.when(jnp.logical_not(own))(remote)

        @pl.when(own)
        def _():
            for source, target in pairs:
                pltpu.make_async_copy(source, target, recv_sem).start()

    def greet(device):
        pl.semaphore_signal(barrier, inc=1, device_id=device, device_id_type=MESH)

    barrier = pltpu.get_barrier_semaphore()
    count = 0
    for i in range(4):
        greet(place.worker(i)[0])
        greet(place.home(i)[0])
        count += 2
    for dx, dz in OFFSETS:
        greet(place.neighbour(dx, dz))
        count += 1
    for stage in range(3):
        for i in range(1, 8):
            greet(place.group(stage, i)[0])
            count += 1

    loads = [pltpu.make_async_copy(s, d, load_sem.at[k]) for k, (s, d) in
             enumerate(((vel_hbm, vel), (react_hbm, react), (table_hbm, tab)))]
    for copy in loads:
        copy.start()
    m = Masks(place.depth)
    loads[0].wait()
    loads[1].wait()
    for f in range(4):
        for x in range(2):
            for i in range(4):
                lanes = slice(i * 128, (i + 1) * 128)
                piece = vel[2 * f + x, :, lanes] if f < 3 else react[x, :, lanes]
                send0[pl.ds(f * 8 + x * 4 + i, 4, stride=32), :] = piece
    pl.semaphore_wait(barrier, count)

    own = place.x == place.gy
    into = pl.ds(pl.multiple_of(place.gy * 8, 8), 8)
    for i in range(4):
        device, turn = place.worker(i)
        pairs = [(send0.at[pl.ds(pl.multiple_of(turn * 32 + f * 8, 8), 8)], recv0.at[f, into]) for f in range(4)]
        push(pairs, device, sem0.at[i], sem0.at[4], None if i else own)

    loads[2].wait()

    def get(row):
        return tab[row]

    pltpu.make_async_copy(recv0, recv0, sem0.at[4]).wait()
    fields = [jnp.stack([recv0[f, pl.ds(i, 8, stride=4), :] for f in range(4)]) for i in range(4)]

    def begin(r, v):
        v = join_block(v, m)
        axial, depth = pack(v, m)
        send_x[r][...] = axial
        send_z[r][...] = depth
        for k, (dx, dz) in enumerate(OFFSETS):
            slot = OFFSETS.index((-dx, -dz))
            pltpu.make_async_remote_copy(
                send_x[r] if dz == 0 else send_z[r], got_refs[r].at[slot],
                round_sem.at[0, r], round_sem.at[1, r],
                device_id=place.neighbour(dx, dz), device_id_type=MESH).start()
        return v

    def finish(r, v):
        pltpu.make_async_copy(got_refs[r], got_refs[r], round_sem.at[1, r]).wait()
        return unpack(v, [got_refs[r][k] for k in range(8)], m)

    def assemble(r, v):
        return finish(r, begin(r, v))

    groups = ((0, 4), (4, 3), (7, 1), (8, 1))

    def give_back(g):
        first, number = groups[g]
        into = pl.ds(pl.multiple_of(place.turn * 8, 8), 8)
        for i in range(4):
            device, cross = place.home(i)
            rows = pl.ds(pl.multiple_of(cross * 8, 8), 8)
            pairs = [(back_send.at[f, rows], back_recv.at[f, into]) for f in range(first, first + number)]
            push(pairs, device, back_sem.at[i, g], back_sem.at[4, g], None if i else own)

    def returned(g):
        first, number = groups[g]
        ref = back_recv.at[pl.ds(first, number)]
        pltpu.make_async_copy(ref, ref, back_sem.at[4, g]).wait()

    def keep(f, v):
        for i in range(4):
            back_send[f, pl.ds(i, 8, stride=4), :] = v[i]

    mass = constant(get, "mass")
    scaled = [fields[i][3:4] * mass[i] for i in range(4)]
    diag_local = constant(get, "diag")
    v = [jnp.concatenate([fields[i][0:3], scaled[i] + diag_local[i]], axis=0) for i in range(4)]
    v = assemble(0, v)
    diag = [x[3:4] for x in v]
    inverse_diag = [1.0 / x for x in diag]
    u = [v[i][0:3] * m.inverse[i] for i in range(4)]
    keep(3, [x[0] for x in diag])
    tend = constant(get, "tend")
    tend = [tend[i] * m.inverse[i] * m.interior for i in range(4)]
    for r in (1, 2):
        t = assemble(r, transport(u, get, m))
        u = [m.interior * u[i] - tend[i] * t[i] for i in range(4)]
    for k in range(3):
        keep(k, [x[k] for x in u])
    source = begin(3, divergence(u, get, m))
    give_back(0)
    source = finish(3, source)

    q = [[source[i] * inverse_diag[i] for i in range(4)]]
    weight = [diag[i][0] * m.inverse[i] for i in range(4)]
    part[0, 0:1, :] = moment(q[0], source, m.inverse)
    keep(4, [x[0] for x in q[0]])
    for j in range(3):
        w = begin(4 + j, stiffness(q[j], scaled, get, m))
        if j == 1:
            part[0, 2:3, :] = moment(q[1], q[1], weight)
        if j == 2:
            give_back(1)
            part[0, 3:4, :] = moment(q[1], q[2], weight)
            part[0, 4:5, :] = moment(q[2], q[2], weight)
        if j == 1:
            part[0, 1:2, :] = moment(q[0], q[1], weight)
        w = finish(4 + j, w)
        q.append([w[i] * inverse_diag[i] - q[j][i] for i in range(4)])
        keep(5 + j, [x[0] for x in q[j + 1]])
    w = stiffness(q[3], scaled, get, m)
    part[0, 5:6, :] = moment(q[2], q[3], weight)
    part[0, 6:7, :] = moment(q[3], q[3], weight)
    part[0, 7:8, :] = moment(q[3], w)

    def send_sum(stage):
        for i in range(1, 8):
            device, me = place.group(stage, i)
            pltpu.make_async_remote_copy(part.at[stage], sums.at[stage, 7 - i], sum_sem.at[0, stage],
                                         sum_sem.at[1, stage], device_id=device, device_id_type=MESH).start()

    def take_sum(stage):
        pltpu.make_async_copy(sums.at[stage], sums.at[stage], sum_sem.at[1, stage]).wait()
        return sum_of([part[stage]] + [sums[stage, i] for i in range(7)])

    send_sum(0)
    w = begin(7, w)
    give_back(2)
    part[1] = take_sum(0)
    send_sum(1)
    w = finish(7, w)
    keep(8, [x[0] for x in w])
    give_back(3)

    returned(0)
    for f in range(3):
        for x in range(2):
            for i in range(4):
                velo_ref[2 * f + x, :, i * 128:(i + 1) * 128] = back_recv[f, pl.ds(x * 4 + i, 4, stride=8), :]

    part[2] = take_sum(1)
    send_sum(2)
    total = take_sum(2)
    n = jnp.broadcast_to(jnp.sum(total, axis=1, keepdims=True), (8, 128))
    c = solve([n[i:i + 1, :] for i in range(7)], n[7:8, :])

    for g in (1, 2, 3):
        returned(g)
    d, q0, q1, q2, q3, w3 = [back_recv[f] for f in range(3, 9)]
    scratch[0] = c[0] * q0 + c[1] * q1 + c[2] * q2 + c[3] * q3
    scratch[1] = d * (q0 - c[0] * (q0 + q1) - c[1] * (q1 + q2) - c[2] * (q2 + q3)) - c[3] * w3
    for f, ref in ((0, press_ref), (1, resid_ref)):
        for x in range(2):
            for i in range(4):
                ref[x, :, i * 128:(i + 1) * 128] = scratch[f, pl.ds(x * 4 + i, 4, stride=8), :]

    for r in range(rounds):
        pltpu.make_async_copy(got_refs[r], got_refs[r], round_sem.at[0, r]).wait()
    for stage in range(3):
        pltpu.make_async_copy(sums.at[stage], sums.at[stage], sum_sem.at[0, stage]).wait()

    def sent(i):
        ref = recv0.at[:, pl.ds(0, 8)]
        pltpu.make_async_copy(ref, ref, sem0.at[i]).wait()
        for g, (first, number) in enumerate(groups):
            ref = back_recv.at[pl.ds(first, number), pl.ds(0, 8)]
            pltpu.make_async_copy(ref, ref, back_sem.at[i, g]).wait()

    for i in range(1, 4):
        sent(i)

    @pl.when(jnp.logical_not(own))
    def _():
        sent(0)


def body(velocity, reaction, table):
    f32 = jnp.float32
    spec = pl.BlockSpec(memory_space=pl.ANY)
    vmem = pl.BlockSpec(memory_space=pltpu.VMEM)
    scratch = [
        pltpu.VMEM((6, 4, 512), f32), pltpu.VMEM((2, 4, 512), f32), pltpu.VMEM(table.shape, f32),
        pltpu.SemaphoreType.DMA((3,)),
        pltpu.VMEM((128, 128), f32), pltpu.VMEM((4, 32, 128), f32), pltpu.SemaphoreType.DMA((5,)),
    ]
    scratch += [pltpu.VMEM((n, 8, 128), f32) for n in ROUND_FIELDS] * 2
    scratch += [pltpu.VMEM((8, n, 8, 128), f32) for n in ROUND_FIELDS]
    scratch += [
        pltpu.SemaphoreType.DMA((2, len(ROUND_FIELDS))),
        pltpu.VMEM((3, 7, 8, 128), f32), pltpu.VMEM((3, 8, 128), f32), pltpu.SemaphoreType.DMA((2, 3)),
        pltpu.VMEM((9, 32, 128), f32), pltpu.VMEM((9, 32, 128), f32), pltpu.SemaphoreType.DMA((5, 4)),
        pltpu.VMEM((2, 32, 128), f32),
    ]
    velo, press, resid = pl.pallas_call(
        kernel,
        out_shape=[jax.ShapeDtypeStruct((6, 4, 512), f32)] + [jax.ShapeDtypeStruct((2, 4, 512), f32)] * 2,
        in_specs=[spec] * 3,
        out_specs=[vmem] * 3,
        scratch_shapes=scratch,
        compiler_params=pltpu.CompilerParams(collective_id=0, has_side_effects=True),
        name="duct_step",
    )(velocity.reshape(6, 4, 512), reaction.reshape(2, 4, 512), table)
    return velo.reshape(velocity.shape), press.reshape(reaction.shape), resid.reshape(reaction.shape)


def solution(mesh):
    specs = (P(None, "gx", "gy", "gz", None), P("gx", "gy", "gz", None))

    def step(velocity, reaction):
        return body(velocity, reaction, jnp.asarray(TABLE))

    return jax.shard_map(
        step, mesh=mesh, in_specs=specs, out_specs=(specs[0], specs[1], specs[1]), check_vma=False
    )
```

```python
import jax
import jax.numpy as jnp
import numpy as np
from jax import lax
from jax.experimental import pallas as pl
from jax.experimental.pallas import tpu as pltpu
from jax.sharding import PartitionSpec as P

MESH = pl.DeviceIdType.MESH
STEP = 0.02
HALF = 64
OFFSETS = ((-1, 0), (1, 0), (0, -1), (0, 1), (-1, -1), (1, -1), (-1, 1), (1, 1))
ROUND_FIELDS = (3, 3, 3, 2, 1, 1, 1, 1)
GROUPS = ((0, 3), (3, 4), (7, 1), (8, 1))


def roll(values, shift, axis):
    shift = shift % values.shape[axis]
    return values if shift == 0 else pltpu.roll(values, shift, axis)


def div(value, by):
    return value // by if isinstance(value, (int, np.ndarray)) else lax.div(value, np.int32(by))


def rem(value, by):
    return value % by if isinstance(value, (int, np.ndarray)) else lax.rem(value, np.int32(by))


def tables():
    half = np.array([0.2092992179024788687, 0.5917001814331423022, 0.8717401485096066153, 1.0])
    points = np.concatenate([-half[::-1], half])
    earlier, current = points * 0.0 + 1.0, points
    for degree in range(1, 7):
        earlier, current = current, ((2 * degree + 1) * points * current - degree * earlier) / (degree + 1)
    w = 2.0 / (56.0 * current**2)
    spacing = points[:, None] - points[None, :] + np.eye(8)
    d = current[:, None] / current[None, :] / spacing * (1.0 - np.eye(8))
    d[0, 0] = -14.0
    d[7, 7] = 14.0
    k = d.T @ np.diag(w) @ d
    lane = np.arange(128)
    c, b, a_lo = lane % 8, (lane // 8) % 8, lane // 64
    rows = {}

    def put(name, values):
        rows[name] = (len(stack), len(values))
        stack.extend(values)

    stack = []

    def along_a(matrix, scale):
        return [matrix[2 * j + a_lo, q] * scale for j in range(4) for q in range(8)]

    def shifts(matrix, index, scale):
        out = []
        for s in range(-7, 8):
            source = index - s
            inside = (source >= 0) & (source <= 7)
            out.append(np.where(inside, matrix[index, np.clip(source, 0, 7)], 0.0) * scale)
        return out

    one = np.ones(128)
    put("da", along_a(d, one))
    put("db", shifts(d, b, one))
    put("dc", shifts(d, c, one))
    put("ka", along_a(k, w[b] * w[c]))
    put("kb", shifts(k, b, w[c]))
    put("kc", shifts(k, c, w[b]))
    put("wa", [w[2 * i + a_lo] for i in range(4)])
    mass = [w[2 * i + a_lo] * w[b] * w[c] for i in range(4)]
    put("mass", mass)
    put("tend", [STEP / m for m in mass])
    s = (w[:, None] * d * d).sum(0)
    put("diag", [s[2 * i + a_lo] * w[b] * w[c] + w[2 * i + a_lo] * s[b] * w[c] + w[2 * i + a_lo] * w[b] * s[c] for i in range(4)])
    table = np.stack(stack).astype(np.float32)
    return np.ascontiguousarray(np.broadcast_to(table[:, None, :], (len(stack), 8, 128))), rows


TABLE, ROWS = tables()


def owner_of(axial, depth):
    y, core = div(axial, 2), rem(axial, 2)
    z, turn = div(depth, 4), rem(depth, 4)
    x = turn + rem(z, 2) * (3 - 2 * turn)
    return (div(y, 4) * 8 + x * 2 + core, rem(y, 4), z)


class Place:
    def __init__(self, gx, gy, gz):
        self.gx, self.gy, self.gz = gx, gy, gz
        self.core, self.x, self.y_hi = rem(gx, 2), rem(div(gx, 2), 4), div(gx, 8)
        self.y, self.z = self.y_hi * 4 + gy, gz
        self.axial = self.y * 2 + self.core
        self.turn = self.x + rem(gz, 2) * (3 - 2 * self.x)
        self.depth = self.z * 4 + self.turn

    def mesh_id(self, x, y, z, core):
        return (div(y, 4) * 8 + x * 2 + core, rem(y, 4), z)

    def neighbour(self, dx, dz):
        return owner_of(rem(self.axial + dx + 16, 16), rem(self.depth + dz + 32, 32))

    def worker(self, i):
        x = rem(self.x + i, 4)
        return self.mesh_id(x, self.y_hi * 4 + self.x, self.z, self.core), x + rem(self.z, 2) * (3 - 2 * x)

    def home(self, i):
        cross = rem(self.gy + i, 4)
        return self.mesh_id(self.gy, self.y_hi * 4 + cross, self.z, self.core), cross

    def group(self, stage, i):
        if stage == 0:
            return self.mesh_id(self.x, self.y, rem(self.z + i // 2, 8), rem(self.core + i % 2, 2))
        return self.mesh_id(rem(self.x + i // 8, 4), rem(self.y + i % 8, 8), self.z, self.core)


MEMBERS = (16, 32)


def far_first(stage):
    def hops(i):
        if stage == 0:
            return (min(i // 2, 8 - i // 2), i % 2)
        return (min(i // 8, 4 - i // 8) + min(i % 8, 8 - i % 8), 0)

    return sorted(range(1, MEMBERS[stage]), key=hops, reverse=True)


def mirror(stage, i):
    if stage == 0:
        return (8 - i // 2) % 8 * 2 + i % 2
    return (4 - i // 8) % 4 * 8 + (8 - i % 8) % 8


class Masks:
    def __init__(self, depth):
        lane = lax.broadcasted_iota(jnp.int32, (8, 128), 1)
        row = lax.broadcasted_iota(jnp.int32, (8, 128), 0)
        c, b = lane & 7, (lane >> 3) & 7
        cross = row >> 1
        self.low = lane < HALF
        self.even = (row & 1) == 0
        odd = (row & 1) == 1
        high = lane >= HALF
        self.b0 = (b == 0) & (cross > 0)
        self.b7 = (b == 7) & (cross < 3)
        self.in0 = odd & self.low
        self.in3 = self.even & high
        self.out0 = self.even & self.low
        self.out3 = odd & high
        self.c = c
        self.c0, self.c7 = c == 0, c == 7
        self.slot_low = c < 4
        self.edge0 = self.out0 & ((c & 3) == 0)
        self.edge3 = self.out3 & ((c & 3) == 3)
        up = (depth < 31).astype(jnp.float32)
        down = (depth > 0).astype(jnp.float32)
        self.zmask = jnp.where(self.slot_low, up, down)
        one = jnp.ones((8, 128), jnp.float32)
        iy = jnp.where(self.b0 | self.b7, 0.5, one)
        iz = jnp.where(self.c0, 1.0 - 0.5 * down, jnp.where(self.c7, 1.0 - 0.5 * up, one))
        iyz = iy * iz
        self.inverse = [iyz * jnp.where(self.low, 0.5, one), iyz, iyz, iyz * jnp.where(self.low, one, 0.5)]
        wall_y = ((b == 0) & (cross == 0)) | ((b == 7) & (cross == 3))
        self.interior = jnp.where(wall_y, 0.0, jnp.where(self.c0, down, jnp.where(self.c7, up, one)))


def join_block(v, m):
    out = []
    for x in v:
        g = roll(roll(x, 2, 1), -56, 2)
        h = roll(roll(x, -2, 1), 56, 2)
        out.append(x + jnp.where(m.b0, g, jnp.where(m.b7, h, 0.0)))
    first = roll(roll(out[3], 1, 1), HALF, 2)
    last = roll(roll(out[0], -1, 1), HALF, 2)
    out[0] = out[0] + jnp.where(m.in0, first, 0.0)
    out[3] = out[3] + jnp.where(m.in3, last, 0.0)
    return out


def pack(v, m):
    axial = jnp.where(m.low, v[0], v[3])
    depth = v[0]
    for i in range(1, 4):
        depth = jnp.where(m.c == i, roll(v[i], i, 2), depth)
    for i in range(4):
        depth = jnp.where(m.c == 4 + i, roll(v[i], i - 3, 2), depth)
    return axial, depth


def unpack(v, got, m):
    v = list(v)
    v[0] = v[0] + jnp.where(m.out0, roll(roll(got[0], -1, 1), HALF, 2), 0.0)
    v[3] = v[3] + jnp.where(m.out3, roll(roll(got[1], 1, 1), HALF, 2), 0.0)
    centre = jnp.where(m.slot_low, got[3], got[2])
    before = jnp.where(m.slot_low, got[6], got[4])
    after = jnp.where(m.slot_low, got[7], got[5])
    face = centre + jnp.where(m.edge0, roll(roll(before, -1, 1), -67, 2), 0.0)
    face = face + jnp.where(m.edge3, roll(roll(after, 1, 1), 67, 2), 0.0)
    face = face * m.zmask
    return [
        v[i] + jnp.where(m.c7, roll(face, 7 - i, 2), jnp.where(m.c0, roll(face, -4 - i, 2), 0.0))
        for i in range(4)
    ]


def along_a(v, get, name, m):
    parts = []
    for x in v:
        turned = roll(x, HALF, 2)
        parts.append(jnp.where(m.low, x, turned))
        parts.append(jnp.where(m.low, turned, x))
    start = ROWS[name][0]
    return [sum_of([get(start + j * 8 + q) * parts[q] for q in range(8)]) for j in range(4)]


def along_lanes(v, get, name, stride):
    start = ROWS[name][0]
    return [sum_of([get(start + s + 7) * roll(x, s * stride, 2) for s in range(-7, 8)]) for x in v]


def sum_of(terms):
    while len(terms) > 1:
        terms = [terms[i] + terms[i + 1] if i + 1 < len(terms) else terms[i] for i in range(0, len(terms), 2)]
    return terms[0]


def constant(get, name):
    return [get(ROWS[name][0] + i) for i in range(4)]


def transport(u, get, m):
    da = along_a(u, get, "da", m)
    db = along_lanes(u, get, "db", 8)
    dc = along_lanes(u, get, "dc", 1)
    mass = constant(get, "mass")
    return [mass[i] * (u[i][0:1] * da[i] + u[i][1:2] * db[i] + u[i][2:3] * dc[i]) for i in range(4)]


def divergence(u, get, m):
    da = along_a([x[0:1] for x in u], get, "da", m)
    db = along_lanes([x[1:2] for x in u], get, "db", 8)
    dc = along_lanes([x[2:3] for x in u], get, "dc", 1)
    mass = constant(get, "mass")
    return [-mass[i] * (da[i] + db[i] + dc[i]) for i in range(4)]


def stiffness(p, scaled, get, m):
    ka = along_a(p, get, "ka", m)
    kb = along_lanes(p, get, "kb", 8)
    kc = along_lanes(p, get, "kc", 1)
    wa = constant(get, "wa")
    return [ka[i] + wa[i] * (kb[i] + kc[i]) + scaled[i] * p[i] for i in range(4)]


def moment(k, f, g, weight=None):
    total = sum_of([f[i][0] * g[i][0] if weight is None else f[i][0] * g[i][0] * weight[i] for i in range(4)])
    total = jnp.sum(total, axis=0, keepdims=True)
    for shift in (64, 32, 16):
        total = total + roll(total, shift, 1)
    lane = lax.broadcasted_iota(jnp.int32, (1, 128), 1)
    return jnp.where((lane >> 4) == k, total, 0.0)


def solve(n, e):
    g = [[(n[i + j] + n[i + j + 1]) if i + j < 6 else e for j in range(4)] for i in range(4)]
    rhs = [n[i] for i in range(4)]
    inverse = []
    for i in range(4):
        inverse.append(1.0 / g[i][i])
        for r in range(i + 1, 4):
            factor = g[r][i] * inverse[i]
            for j in range(i + 1, 4):
                g[r][j] = g[r][j] - factor * g[i][j]
            rhs[r] = rhs[r] - factor * rhs[i]
    out = [None] * 4
    for i in range(3, -1, -1):
        total = rhs[i]
        for j in range(i + 1, 4):
            total = total - g[i][j] * out[j]
        out[i] = total * inverse[i]
    return out


def kernel(vel_hbm, react_hbm, table_hbm, home_ref, total_ref, vel, react, tab, load_sem,
           send0, recv0, sem0, *rest):
    rounds = len(ROUND_FIELDS)
    send_x, send_z = rest[0:rounds], rest[rounds:2 * rounds]
    got_refs = rest[2 * rounds:3 * rounds]
    (round_sem, part, sums0, sums1, sum_sem, back_send, back_recv, back_sem) = rest[3 * rounds:]
    sums = (sums0, sums1)
    place = Place(lax.axis_index("gx"), lax.axis_index("gy"), lax.axis_index("gz"))

    def push(source, target, device, send_sem, recv_sem, own=None):
        def remote():
            pltpu.make_async_remote_copy(source, target, send_sem, recv_sem, device_id=device, device_id_type=MESH).start()

        if own is None:
            remote()
            return
        pl.when(jnp.logical_not(own))(remote)

        @pl.when(own)
        def _():
            pltpu.make_async_copy(source, target, recv_sem).start()

    def greet(device):
        pl.semaphore_signal(barrier, inc=1, device_id=device, device_id_type=MESH)

    barrier = pltpu.get_barrier_semaphore()
    count = 0
    for i in range(4):
        greet(place.worker(i)[0])
        greet(place.home(i)[0])
        count += 2
    for dx, dz in OFFSETS:
        greet(place.neighbour(dx, dz))
        count += 1
    for stage in range(2):
        for i in far_first(stage):
            greet(place.group(stage, i))
            count += 1

    loads = [pltpu.make_async_copy(s, d, load_sem.at[k]) for k, (s, d) in
             enumerate(((vel_hbm, vel), (react_hbm, react), (table_hbm, tab)))]
    for copy in loads:
        copy.start()
    m = Masks(place.depth)
    loads[0].wait()
    loads[1].wait()
    for f in range(4):
        for x in range(2):
            for i in range(4):
                lanes = slice(i * 128, (i + 1) * 128)
                piece = vel[2 * f + x, :, lanes] if f < 3 else react[x, :, lanes]
                send0.reshape(128, 128)[pl.ds(f * 8 + x * 4 + i, 4, stride=32), :] = piece
    pl.semaphore_wait(barrier, count)

    own = place.x == place.gy
    into = pl.ds(pl.multiple_of(place.gy * 8, 8), 8)
    for i in (2, 1, 3, 0):
        device, turn = place.worker(i)
        push(send0.at[turn], recv0.at[:, into], device, sem0.at[i], sem0.at[4], None if i else own)

    loads[2].wait()

    def get(row):
        return tab[row]

    pltpu.make_async_copy(recv0, recv0, sem0.at[4]).wait()
    fields = [jnp.stack([recv0[f, pl.ds(i, 8, stride=4), :] for f in range(4)]) for i in range(4)]

    def begin(r, v):
        v = join_block(v, m)
        axial, depth = pack(v, m)
        send_x[r][...] = axial
        send_z[r][...] = depth
        for dx, dz in OFFSETS[4:] + OFFSETS[:4]:
            slot = OFFSETS.index((-dx, -dz))
            pltpu.make_async_remote_copy(
                send_x[r] if dz == 0 else send_z[r], got_refs[r].at[slot],
                round_sem.at[0, r], round_sem.at[1, r],
                device_id=place.neighbour(dx, dz), device_id_type=MESH).start()
        return v

    def finish(r, v):
        pltpu.make_async_copy(got_refs[r], got_refs[r], round_sem.at[1, r]).wait()
        return unpack(v, [got_refs[r][k] for k in range(8)], m)

    def assemble(r, v):
        return finish(r, begin(r, v))

    def give_back(g):
        first, number = GROUPS[g]
        fields = pl.ds(first, number)
        into = pl.ds(pl.multiple_of(place.turn * 8, 8), 8)
        for i in (2, 1, 3, 0):
            device, cross = place.home(i)
            rows = pl.ds(pl.multiple_of(cross * 8, 8), 8)
            push(back_send.at[fields, rows], back_recv.at[fields, into], device,
                 back_sem.at[i, g], back_sem.at[4, g], None if i else own)

    def keep(f, v):
        for i in range(4):
            back_send[f, pl.ds(i, 8, stride=4), :] = v[i]

    mass = constant(get, "mass")
    scaled = [fields[i][3:4] * mass[i] for i in range(4)]
    diag_local = constant(get, "diag")
    v = assemble(0, [x[0:3] for x in fields])
    u = [v[i] * m.inverse[i] for i in range(4)]
    tend = constant(get, "tend")
    tend = [tend[i] * m.inverse[i] * m.interior for i in range(4)]
    for r in (1, 2):
        t = assemble(r, transport(u, get, m))
        u = [m.interior * u[i] - tend[i] * t[i] for i in range(4)]
    v = divergence(u, get, m)
    v = begin(3, [jnp.concatenate([v[i], scaled[i] + diag_local[i]], axis=0) for i in range(4)])
    for k in range(3):
        keep(k, [x[k] for x in u])
    give_back(0)
    v = finish(3, v)
    source, diag = [x[0:1] for x in v], [x[1:2] for x in v]
    inverse_diag = [1.0 / x for x in diag]

    q = [[source[i] * inverse_diag[i] for i in range(4)]]
    weight = [diag[i][0] * m.inverse[i] for i in range(4)]
    for j in range(3):
        w = begin(4 + j, stiffness(q[j], scaled, get, m))
        if j == 0:
            sums_early = moment(0, q[0], source, m.inverse)
            keep(3, [x[0] for x in diag])
        if j == 1:
            sums_early = sums_early + moment(1, q[0], q[1], weight) + moment(2, q[1], q[1], weight)
        if j == 2:
            sums_early = sums_early + moment(3, q[1], q[2], weight) + moment(4, q[2], q[2], weight)
        keep(4 + j, [x[0] for x in q[j]])
        if j == 2:
            give_back(1)
        w = finish(4 + j, w)
        q.append([w[i] * inverse_diag[i] - q[j][i] for i in range(4)])
    w = stiffness(q[3], scaled, get, m)
    part[0] = (sums_early + moment(5, q[2], q[3], weight)) + (moment(6, q[3], q[3], weight) + moment(7, q[3], w))

    def send_sum(stage):
        for i in far_first(stage):
            pltpu.make_async_remote_copy(part.at[stage], sums[stage].at[mirror(stage, i) - 1], sum_sem.at[0, stage],
                                         sum_sem.at[1, stage], device_id=place.group(stage, i), device_id_type=MESH).start()

    def take_sum(stage):
        pltpu.make_async_copy(sums[stage], sums[stage], sum_sem.at[1, stage]).wait()
        return sum_of([part[stage]] + [sums[stage][i] for i in range(MEMBERS[stage] - 1)])

    send_sum(0)
    w = begin(7, w)
    keep(7, [x[0] for x in q[3]])
    give_back(2)
    part[1] = take_sum(0)
    send_sum(1)
    w = finish(7, w)
    keep(8, [x[0] for x in w])
    give_back(3)
    for g, (first, number) in enumerate(GROUPS):
        ref = back_recv.at[pl.ds(first, number)]
        pltpu.make_async_copy(ref, ref, back_sem.at[4, g]).wait()
    home_ref[...] = back_recv[...]

    for r in range(rounds):
        pltpu.make_async_copy(got_refs[r], got_refs[r], round_sem.at[0, r]).wait()
    for stage in range(2):
        pltpu.make_async_copy(sums[stage], sums[stage], sum_sem.at[0, stage]).wait()

    def sent(i):
        ref = recv0.at[:, pl.ds(0, 8)]
        pltpu.make_async_copy(ref, ref, sem0.at[i]).wait()
        for g, (first, number) in enumerate(GROUPS):
            ref = back_recv.at[pl.ds(first, number), pl.ds(0, 8)]
            pltpu.make_async_copy(ref, ref, back_sem.at[i, g]).wait()

    for i in range(1, 4):
        sent(i)

    @pl.when(jnp.logical_not(own))
    def _():
        sent(0)

    total_ref[...] = take_sum(1)


def combine(home, total_ref, velo_ref, press_ref, resid_ref, scratch):
    lane = lax.broadcasted_iota(jnp.int32, (8, 128), 1)
    row = lax.broadcasted_iota(jnp.int32, (8, 128), 0)
    n = jnp.sum(jnp.where((lane >> 4) == row, total_ref[...], 0.0), axis=1, keepdims=True)
    n = jnp.broadcast_to(n, (8, 128))
    c = solve([n[i:i + 1, :] for i in range(7)], n[7:8, :])
    d, q0, q1, q2, q3, w3 = [home[f] for f in range(3, 9)]
    scratch[0] = c[0] * q0 + c[1] * q1 + c[2] * q2 + c[3] * q3
    scratch[1] = d * (q0 - c[0] * (q0 + q1) - c[1] * (q1 + q2) - c[2] * (q2 + q3)) - c[3] * w3
    for x in range(2):
        for i in range(4):
            rows, lanes = pl.ds(x * 4 + i, 4, stride=8), slice(i * 128, (i + 1) * 128)
            press_ref[x, :, lanes] = scratch[0, rows, :]
            resid_ref[x, :, lanes] = scratch[1, rows, :]
            for f in range(3):
                velo_ref[2 * f + x, :, lanes] = home[f, rows, :]


def body(velocity, reaction, table):
    f32 = jnp.float32
    spec = pl.BlockSpec(memory_space=pl.ANY)
    vmem = pl.BlockSpec(memory_space=pltpu.VMEM)
    scratch = [
        pltpu.VMEM((6, 4, 512), f32), pltpu.VMEM((2, 4, 512), f32), pltpu.VMEM(table.shape, f32),
        pltpu.SemaphoreType.DMA((3,)),
        pltpu.VMEM((4, 4, 8, 128), f32), pltpu.VMEM((4, 32, 128), f32), pltpu.SemaphoreType.DMA((5,)),
    ]
    scratch += [pltpu.VMEM((n, 8, 128), f32) for n in ROUND_FIELDS] * 2
    scratch += [pltpu.VMEM((8, n, 8, 128), f32) for n in ROUND_FIELDS]
    scratch += [
        pltpu.SemaphoreType.DMA((2, len(ROUND_FIELDS))),
        pltpu.VMEM((2, 1, 128), f32), pltpu.VMEM((MEMBERS[0] - 1, 1, 128), f32), pltpu.VMEM((MEMBERS[1] - 1, 1, 128), f32),
        pltpu.SemaphoreType.DMA((2, 2)),
        pltpu.VMEM((9, 32, 128), f32), pltpu.VMEM((9, 32, 128), f32), pltpu.SemaphoreType.DMA((5, 4)),
    ]
    home, total = pl.pallas_call(
        kernel,
        out_shape=[jax.ShapeDtypeStruct((9, 32, 128), f32), jax.ShapeDtypeStruct((1, 128), f32)],
        in_specs=[spec] * 3,
        out_specs=[vmem] * 2,
        scratch_shapes=scratch,
        compiler_params=pltpu.CompilerParams(collective_id=0, has_side_effects=True),
        name="duct_step",
    )(velocity.reshape(6, 4, 512), reaction.reshape(2, 4, 512), table)
    velo, press, resid = pl.pallas_call(
        combine,
        out_shape=[jax.ShapeDtypeStruct((6, 4, 512), f32)] + [jax.ShapeDtypeStruct((2, 4, 512), f32)] * 2,
        in_specs=[vmem] * 2,
        out_specs=[vmem] * 3,
        scratch_shapes=[pltpu.VMEM((2, 32, 128), f32)],
        name="combine",
    )(home, total)
    return velo.reshape(velocity.shape), press.reshape(reaction.shape), resid.reshape(reaction.shape)


def solution(mesh):
    specs = (P(None, "gx", "gy", "gz", None), P("gx", "gy", "gz", None))

    def step(velocity, reaction):
        return body(velocity, reaction, jnp.asarray(TABLE))

    return jax.shard_map(
        step, mesh=mesh, in_specs=specs, out_specs=(specs[0], specs[1], specs[1]), check_vma=False
    )
```

```python
import jax
import jax.numpy as jnp
import numpy as np
from jax import lax
from jax.experimental import pallas as pl
from jax.experimental.pallas import tpu as pltpu
from jax.sharding import PartitionSpec as P

MESH = pl.DeviceIdType.MESH
STEP = 0.02
HALF = 64
OFFSETS = ((-1, 0), (1, 0), (0, -1), (0, 1), (-1, -1), (1, -1), (-1, 1), (1, 1))
ROUNDS = ((3, 8), (1, 8), (3, 4), (3, 4), (1, 4), (1, 4), (1, 4), (1, 4), (1, 4))
GROUPS = ((0, 3), (3, 4), (7, 1), (8, 1))


def roll(values, shift, axis):
    shift = shift % values.shape[axis]
    return values if shift == 0 else pltpu.roll(values, shift, axis)


def div(value, by):
    return value // by if isinstance(value, (int, np.ndarray)) else lax.div(value, np.int32(by))


def rem(value, by):
    return value % by if isinstance(value, (int, np.ndarray)) else lax.rem(value, np.int32(by))


def tables():
    half = np.array([0.2092992179024788687, 0.5917001814331423022, 0.8717401485096066153, 1.0])
    points = np.concatenate([-half[::-1], half])
    earlier, current = points * 0.0 + 1.0, points
    for degree in range(1, 7):
        earlier, current = current, ((2 * degree + 1) * points * current - degree * earlier) / (degree + 1)
    w = 2.0 / (56.0 * current**2)
    spacing = points[:, None] - points[None, :] + np.eye(8)
    d = current[:, None] / current[None, :] / spacing * (1.0 - np.eye(8))
    d[0, 0] = -14.0
    d[7, 7] = 14.0
    k = d.T @ np.diag(w) @ d
    lane = np.arange(128)
    c, b, a_lo = lane % 8, (lane // 8) % 8, lane // 64
    rows = {}

    def put(name, values):
        rows[name] = (len(stack), len(values))
        stack.extend(values)

    stack = []

    def along_a(matrix, scale):
        return [matrix[2 * j + a_lo, q] * scale for j in range(4) for q in range(8)]

    def shifts(matrix, index, scale):
        out = []
        for s in range(-7, 8):
            source = index - s
            inside = (source >= 0) & (source <= 7)
            out.append(np.where(inside, matrix[index, np.clip(source, 0, 7)], 0.0) * scale)
        return out

    one = np.ones(128)
    put("da", along_a(d, one))
    put("db", shifts(d, b, one))
    put("dc", shifts(d, c, one))
    put("ka", along_a(k, one))
    put("kb", shifts(k, b, one))
    put("kc", shifts(k, c, one))
    s = (w[:, None] * d * d).sum(0)
    put("wa", [w[2 * i + a_lo] for i in range(4)])
    put("wb", [w[b]])
    put("wc", [w[c]])
    put("sa", [s[2 * i + a_lo] for i in range(4)])
    put("sb", [s[b]])
    put("sc", [s[c]])
    table = np.stack(stack).astype(np.float32)
    return np.ascontiguousarray(np.broadcast_to(table[:, None, :], (len(stack), 8, 128))), rows


TABLE, ROWS = tables()


def owner_of(axial, depth):
    y, core = div(axial, 2), rem(axial, 2)
    z, turn = div(depth, 4), rem(depth, 4)
    x = turn + rem(z, 2) * (3 - 2 * turn)
    return (div(y, 4) * 8 + x * 2 + core, rem(y, 4), z)


class Place:
    def __init__(self, gx, gy, gz):
        self.gx, self.gy, self.gz = gx, gy, gz
        self.core, self.x, self.y_hi = rem(gx, 2), rem(div(gx, 2), 4), div(gx, 8)
        self.y, self.z = self.y_hi * 4 + gy, gz
        self.axial = self.y * 2 + self.core
        self.turn = self.x + rem(gz, 2) * (3 - 2 * self.x)
        self.depth = self.z * 4 + self.turn

    def mesh_id(self, x, y, z, core):
        return (div(y, 4) * 8 + x * 2 + core, rem(y, 4), z)

    def neighbour(self, dx, dz):
        return owner_of(rem(self.axial + dx + 16, 16), rem(self.depth + dz + 32, 32))

    def worker(self, i):
        x = rem(self.x + i, 4)
        return self.mesh_id(x, self.y_hi * 4 + self.x, self.z, self.core), x + rem(self.z, 2) * (3 - 2 * x)

    def home(self, i):
        cross = rem(self.gy + i, 4)
        return self.mesh_id(self.gy, self.y_hi * 4 + cross, self.z, self.core), cross

    def group(self, stage, i):
        if stage == 0:
            return self.mesh_id(self.x, self.y, rem(self.z + i // 2, 8), rem(self.core + i % 2, 2))
        return self.mesh_id(rem(self.x + i // 8, 4), rem(self.y + i % 8, 8), self.z, self.core)


MEMBERS = (16, 32)


def far_first(stage):
    def hops(i):
        if stage == 0:
            return (min(i // 2, 8 - i // 2), i % 2)
        return (min(i // 8, 4 - i // 8) + min(i % 8, 8 - i % 8), 0)

    return sorted(range(1, MEMBERS[stage]), key=hops, reverse=True)


def mirror(stage, i):
    if stage == 0:
        return (8 - i // 2) % 8 * 2 + i % 2
    return (4 - i // 8) % 4 * 8 + (8 - i % 8) % 8


class Masks:
    def __init__(self, depth):
        lane = lax.broadcasted_iota(jnp.int32, (8, 128), 1)
        row = lax.broadcasted_iota(jnp.int32, (8, 128), 0)
        c, b = lane & 7, (lane >> 3) & 7
        cross = row >> 1
        self.low = lane < HALF
        self.even = (row & 1) == 0
        odd = (row & 1) == 1
        high = lane >= HALF
        self.b0 = (b == 0) & (cross > 0)
        self.b7 = (b == 7) & (cross < 3)
        self.in0 = odd & self.low
        self.in3 = self.even & high
        self.out0 = self.even & self.low
        self.out3 = odd & high
        self.c = c
        self.c0, self.c7 = c == 0, c == 7
        self.slot_low = c < 4
        self.edge0 = self.out0 & ((c & 3) == 0)
        self.edge3 = self.out3 & ((c & 3) == 3)
        up = (depth < 31).astype(jnp.float32)
        down = (depth > 0).astype(jnp.float32)
        self.zmask = jnp.where(self.slot_low, up, down)
        one = jnp.ones((8, 128), jnp.float32)
        first, last = jnp.where(self.low, 0.5, one), jnp.where(self.low, one, 0.5)
        self.hx = [first, one, one, last]
        self.hy = jnp.where(self.b0 | self.b7, 0.5, one)
        self.hz = jnp.where(self.c0, 1.0 - 0.5 * down, jnp.where(self.c7, 1.0 - 0.5 * up, one))
        self.inverse = [x * (self.hy * self.hz) for x in self.hx]
        wall_y = ((b == 0) & (cross == 0)) | ((b == 7) & (cross == 3))
        self.interior = jnp.where(wall_y, 0.0, jnp.where(self.c0, down, jnp.where(self.c7, up, one)))


class Weights:
    def __init__(self, get, m):
        def row(name, i=0):
            return get(ROWS[name][0] + i)

        self.wa, self.wb, self.wc = [row("wa", i) for i in range(4)], row("wb"), row("wc")
        two_x, two_y, two_z = [1.0 / h for h in m.hx], 1.0 / m.hy, 1.0 / m.hz
        self.mx, self.my, self.mz = [x * t for x, t in zip(self.wa, two_x)], self.wb * two_y, self.wc * two_z
        self.yz = self.my * self.mz
        self.xz = [x * self.mz for x in self.mx]
        self.xy = [x * self.my for x in self.mx]
        self.all = [x * self.yz for x in self.mx]
        self.mass = [x * (self.wb * self.wc) for x in self.wa]
        self.diag = [
            row("sa", i) * two_x[i] * self.yz + row("sb") * two_y * self.xz[i] + row("sc") * two_z * self.xy[i]
            for i in range(4)
        ]


def join_cross(v, m):
    out = []
    for x in v:
        g = roll(roll(x, 2, 1), -56, 2)
        h = roll(roll(x, -2, 1), 56, 2)
        out.append(x + jnp.where(m.b0, g, jnp.where(m.b7, h, 0.0)))
    return out


def join_block(v, m):
    out = join_cross(v, m)
    first = roll(roll(out[3], 1, 1), HALF, 2)
    last = roll(roll(out[0], -1, 1), HALF, 2)
    out[0] = out[0] + jnp.where(m.in0, first, 0.0)
    out[3] = out[3] + jnp.where(m.in3, last, 0.0)
    return out


def pack(v, m):
    return jnp.where(m.low, v[0], v[3]), pack_depth(v, m)


def pack_depth(v, m):
    depth = v[0]
    for i in range(1, 4):
        depth = jnp.where(m.c == i, roll(v[i], i, 2), depth)
    for i in range(4):
        depth = jnp.where(m.c == 4 + i, roll(v[i], i - 3, 2), depth)
    return depth


def pack_axial(v, m):
    faces = roll(jnp.where(m.low, v[0], v[3]), HALF, 2)
    return jnp.where(m.even, roll(faces, -1, 1), roll(faces, 1, 1))


def partners(own, got, m):
    across = jnp.where(m.in0 | m.in3, own, jnp.where(m.low, got[0], got[1]))
    face = jnp.where(m.slot_low, got[3], got[2]) * m.zmask
    depth = [jnp.where(m.c7, roll(face, 7 - i, 2), jnp.where(m.c0, roll(face, -4 - i, 2), 0.0)) for i in range(4)]
    return {0: jnp.where(m.low, across, 0.0), 3: jnp.where(m.low, 0.0, across)}, depth


def unpack(v, got, m):
    v = list(v)
    v[0] = v[0] + jnp.where(m.out0, roll(roll(got[0], -1, 1), HALF, 2), 0.0)
    v[3] = v[3] + jnp.where(m.out3, roll(roll(got[1], 1, 1), HALF, 2), 0.0)
    centre = jnp.where(m.slot_low, got[3], got[2])
    before = jnp.where(m.slot_low, got[6], got[4])
    after = jnp.where(m.slot_low, got[7], got[5])
    face = centre + jnp.where(m.edge0, roll(roll(before, -1, 1), -67, 2), 0.0)
    face = face + jnp.where(m.edge3, roll(roll(after, 1, 1), 67, 2), 0.0)
    face = face * m.zmask
    return [
        v[i] + jnp.where(m.c7, roll(face, 7 - i, 2), jnp.where(m.c0, roll(face, -4 - i, 2), 0.0))
        for i in range(4)
    ]


def along_a(v, get, name, m):
    parts = []
    for x in v:
        turned = roll(x, HALF, 2)
        parts.append(jnp.where(m.low, x, turned))
        parts.append(jnp.where(m.low, turned, x))
    start = ROWS[name][0]
    return [sum_of([get(start + j * 8 + q) * parts[q] for q in range(8)]) for j in range(4)]


def along_lanes(v, get, name, stride):
    start = ROWS[name][0]
    return [sum_of([get(start + s + 7) * roll(x, s * stride, 2) for s in range(-7, 8)]) for x in v]


def sum_of(terms):
    while len(terms) > 1:
        terms = [terms[i] + terms[i + 1] if i + 1 < len(terms) else terms[i] for i in range(0, len(terms), 2)]
    return terms[0]


def moment(k, f, g, weight=None):
    total = sum_of([f[i][0] * g[i][0] if weight is None else f[i][0] * g[i][0] * weight[i] for i in range(4)])
    total = jnp.sum(total, axis=0, keepdims=True)
    for shift in (64, 32, 16):
        total = total + roll(total, shift, 1)
    lane = lax.broadcasted_iota(jnp.int32, (1, 128), 1)
    return jnp.where((lane >> 4) == k, total, 0.0)


def solve(n, e):
    g = [[(n[i + j] + n[i + j + 1]) if i + j < 6 else e for j in range(4)] for i in range(4)]
    rhs = [n[i] for i in range(4)]
    inverse = []
    for i in range(4):
        inverse.append(1.0 / g[i][i])
        for r in range(i + 1, 4):
            factor = g[r][i] * inverse[i]
            for j in range(i + 1, 4):
                g[r][j] = g[r][j] - factor * g[i][j]
            rhs[r] = rhs[r] - factor * rhs[i]
    out = [None] * 4
    for i in range(3, -1, -1):
        total = rhs[i]
        for j in range(i + 1, 4):
            total = total - g[i][j] * out[j]
        out[i] = total * inverse[i]
    return out


def kernel(vel_hbm, react_hbm, table_hbm, home_ref, total_ref, vel, react, tab, load_sem,
           send0, recv0, sem0, *rest):
    rounds = len(ROUNDS)
    send_x, send_z = rest[0:rounds], rest[rounds:2 * rounds]
    got_refs = rest[2 * rounds:3 * rounds]
    (round_sem, part, sums0, sums1, sum_sem, back_send, back_recv, back_sem) = rest[3 * rounds:]
    sums = (sums0, sums1)
    place = Place(lax.axis_index("gx"), lax.axis_index("gy"), lax.axis_index("gz"))

    def push(source, target, device, send_sem, recv_sem, own=None):
        def remote():
            pltpu.make_async_remote_copy(source, target, send_sem, recv_sem, device_id=device, device_id_type=MESH).start()

        if own is None:
            remote()
            return
        pl.when(jnp.logical_not(own))(remote)

        @pl.when(own)
        def _():
            pltpu.make_async_copy(source, target, recv_sem).start()

    def greet(device):
        pl.semaphore_signal(barrier, inc=1, device_id=device, device_id_type=MESH)

    barrier = pltpu.get_barrier_semaphore()
    count = 0
    for i in range(4):
        greet(place.worker(i)[0])
        greet(place.home(i)[0])
        count += 2
    for dx, dz in OFFSETS:
        greet(place.neighbour(dx, dz))
        count += 1
    for stage in range(2):
        for i in far_first(stage):
            greet(place.group(stage, i))
            count += 1

    loads = [pltpu.make_async_copy(s, d, load_sem.at[k]) for k, (s, d) in
             enumerate(((vel_hbm, vel), (react_hbm, react), (table_hbm, tab)))]
    for copy in loads:
        copy.start()
    m = Masks(place.depth)
    loads[0].wait()
    loads[1].wait()
    for f in range(4):
        for x in range(2):
            for i in range(4):
                lanes = slice(i * 128, (i + 1) * 128)
                piece = vel[2 * f + x, :, lanes] if f < 3 else react[x, :, lanes]
                send0.reshape(128, 128)[pl.ds(f * 8 + x * 4 + i, 4, stride=32), :] = piece
    pl.semaphore_wait(barrier, count)

    own = place.x == place.gy
    into = pl.ds(pl.multiple_of(place.gy * 8, 8), 8)
    for i in (2, 1, 3, 0):
        device, turn = place.worker(i)
        push(send0.at[turn], recv0.at[:, into], device, sem0.at[i], sem0.at[4], None if i else own)

    loads[2].wait()

    def get(row):
        return tab[row]

    pltpu.make_async_copy(recv0, recv0, sem0.at[4]).wait()
    fields = [jnp.stack([recv0[f, pl.ds(i, 8, stride=4), :] for f in range(4)]) for i in range(4)]

    def send(r, axial, depth):
        send_x[r][...] = axial
        send_z[r][...] = depth
        for dx, dz in OFFSETS[4:ROUNDS[r][1]] + OFFSETS[2:4] + OFFSETS[0:2]:
            slot = OFFSETS.index((-dx, -dz))
            pltpu.make_async_remote_copy(
                send_x[r] if dz == 0 else send_z[r], got_refs[r].at[slot],
                round_sem.at[0, r], round_sem.at[1, r],
                device_id=place.neighbour(dx, dz), device_id_type=MESH).start()

    def receive(r):
        pltpu.make_async_copy(got_refs[r], got_refs[r], round_sem.at[1, r]).wait()
        return [got_refs[r][k] for k in range(ROUNDS[r][1])]

    def send_faces(r, along_axis, along_depth):
        axial = pack_axial(along_axis, m)
        send(r, axial, pack_depth(along_depth, m))
        return axial

    def give_back(g):
        first, number = GROUPS[g]
        fields = pl.ds(first, number)
        into = pl.ds(pl.multiple_of(place.turn * 8, 8), 8)
        for i in (2, 1, 3, 0):
            device, cross = place.home(i)
            rows = pl.ds(pl.multiple_of(cross * 8, 8), 8)
            push(back_send.at[fields, rows], back_recv.at[fields, into], device,
                 back_sem.at[i, g], back_sem.at[4, g], None if i else own)

    def keep(f, v):
        for i in range(4):
            back_send[f, pl.ds(i, 8, stride=4), :] = v[i]

    v = join_block([x[0:3] for x in fields], m)
    send(0, *pack(v, m))
    wt = Weights(get, m)
    scaled = [fields[i][3:4] * wt.mass[i] for i in range(4)]
    react_sum = join_block(scaled, m)
    send(1, *pack(react_sum, m))
    inside = STEP * m.interior
    rate = ([inside * h for h in m.hx], inside * m.hy, inside * m.hz)
    v = unpack(v, receive(0), m)
    u = [v[i] * m.inverse[i] for i in range(4)]

    for r in (2, 3):
        da = along_a(u, get, "da", m)
        dc = along_lanes(u, get, "dc", 1)
        axial = send_faces(r, da, dc)
        db = join_cross(along_lanes(u, get, "db", 8), m)
        first = [rate[0][i] * u[i][0:1] for i in range(4)]
        third = [rate[2] * u[i][2:3] for i in range(4)]
        base = [m.interior * u[i] - (first[i] * da[i] + rate[1] * u[i][1:2] * db[i] + third[i] * dc[i]) for i in range(4)]
        if r == 3:
            react_sum = unpack(react_sum, receive(1), m)
            diag = [wt.diag[i] + react_sum[i] for i in range(4)]
            inverse_diag = [1.0 / x for x in diag]
            step_a = [wt.yz * x for x in inverse_diag]
            step_b = [wt.xz[i] * inverse_diag[i] for i in range(4)]
            step_c = [wt.xy[i] * inverse_diag[i] for i in range(4)]
            step_0 = [react_sum[i] * inverse_diag[i] - 1.0 for i in range(4)]
            weight = [diag[i][0] * m.inverse[i] for i in range(4)]
            keep(3, [x[0] for x in diag])
        across, depth = partners(axial, receive(r), m)
        u = [base[i] - third[i] * depth[i] for i in range(4)]
        for i in across:
            u[i] = u[i] - first[i] * across[i]

    da = along_a([x[0:1] for x in u], get, "da", m)
    dc = along_lanes([x[2:3] for x in u], get, "dc", 1)
    axial = send_faces(4, da, dc)
    for k in range(3):
        keep(k, [x[k] for x in u])
    give_back(0)
    db = join_cross(along_lanes([x[1:2] for x in u], get, "db", 8), m)
    volume = [-x for x in wt.all]
    base = [volume[i] * (m.hx[i] * da[i] + m.hy * db[i] + m.hz * dc[i]) for i in range(4)]
    across, depth = partners(axial, receive(4), m)
    source = [base[i] + volume[i] * m.hz * depth[i] for i in range(4)]
    for i in across:
        source[i] = source[i] + volume[i] * m.hx[i] * across[i]

    q = [[source[i] * inverse_diag[i] for i in range(4)]]
    for j in range(4):
        ka = along_a(q[j], get, "ka", m)
        kc = along_lanes(q[j], get, "kc", 1)
        if j < 3:
            axial = send_faces(5 + j, ka, kc)
        kb = along_lanes(q[j], get, "kb", 8)
        if j == 0:
            early = moment(0, q[0], source, m.inverse)
        if j == 1:
            early = early + moment(1, q[0], q[1], weight) + moment(2, q[1], q[1], weight)
        if j == 2:
            early = early + moment(3, q[1], q[2], weight) + moment(4, q[2], q[2], weight)
        if j == 3:
            break
        kb = join_cross(kb, m)
        base = [step_a[i] * ka[i] + step_b[i] * kb[i] + step_c[i] * kc[i] + step_0[i] * q[j][i] for i in range(4)]
        keep(4 + j, [x[0] for x in q[j]])
        if j == 2:
            give_back(1)
        across, depth = partners(axial, receive(5 + j), m)
        after = [base[i] + step_c[i] * depth[i] for i in range(4)]
        for i in across:
            after[i] = after[i] + step_a[i] * across[i]
        q.append(after)
    energy = [
        wt.wb * wt.wc * ka[i] + wt.wa[i] * (wt.wc * kb[i] + wt.wb * kc[i]) + scaled[i] * q[3][i] for i in range(4)
    ]
    part[0] = (early + moment(5, q[2], q[3], weight)) + (moment(6, q[3], q[3], weight) + moment(7, q[3], energy))

    def send_sum(stage):
        for i in far_first(stage):
            pltpu.make_async_remote_copy(part.at[stage], sums[stage].at[mirror(stage, i) - 1], sum_sem.at[0, stage],
                                         sum_sem.at[1, stage], device_id=place.group(stage, i), device_id_type=MESH).start()

    def take_sum(stage):
        pltpu.make_async_copy(sums[stage], sums[stage], sum_sem.at[1, stage]).wait()
        return sum_of([part[stage]] + [sums[stage][i] for i in range(MEMBERS[stage] - 1)])

    send_sum(0)
    axial = send_faces(8, ka, kc)
    kb = join_cross(kb, m)
    base = [wt.yz * ka[i] + wt.xz[i] * kb[i] + wt.xy[i] * kc[i] + react_sum[i] * q[3][i] for i in range(4)]
    keep(7, [x[0] for x in q[3]])
    give_back(2)
    part[1] = take_sum(0)
    send_sum(1)
    across, depth = partners(axial, receive(8), m)
    w = [base[i] + wt.xy[i] * depth[i] for i in range(4)]
    for i in across:
        w[i] = w[i] + wt.yz * across[i]
    keep(8, [x[0] for x in w])
    give_back(3)
    for g, (first, number) in enumerate(GROUPS):
        ref = back_recv.at[pl.ds(first, number)]
        pltpu.make_async_copy(ref, ref, back_sem.at[4, g]).wait()
    leave = pltpu.make_async_copy(back_recv, home_ref, load_sem.at[0])
    leave.start()

    for r in range(rounds):
        pltpu.make_async_copy(got_refs[r], got_refs[r], round_sem.at[0, r]).wait()
    for stage in range(2):
        pltpu.make_async_copy(sums[stage], sums[stage], sum_sem.at[0, stage]).wait()

    def sent(i):
        ref = recv0.at[:, pl.ds(0, 8)]
        pltpu.make_async_copy(ref, ref, sem0.at[i]).wait()
        for g, (first, number) in enumerate(GROUPS):
            ref = back_recv.at[pl.ds(first, number), pl.ds(0, 8)]
            pltpu.make_async_copy(ref, ref, back_sem.at[i, g]).wait()

    for i in range(1, 4):
        sent(i)

    @pl.when(jnp.logical_not(own))
    def _():
        sent(0)

    total_ref[...] = take_sum(1)
    leave.wait()


def combine(home, total_ref, velo_ref, press_ref, resid_ref, scratch):
    lane = lax.broadcasted_iota(jnp.int32, (8, 128), 1)
    row = lax.broadcasted_iota(jnp.int32, (8, 128), 0)
    n = jnp.sum(jnp.where((lane >> 4) == row, total_ref[...], 0.0), axis=1, keepdims=True)
    n = jnp.broadcast_to(n, (8, 128))
    c = solve([n[i:i + 1, :] for i in range(7)], n[7:8, :])
    d, q0, q1, q2, q3, w3 = [home[f] for f in range(3, 9)]
    scratch[0] = c[0] * q0 + c[1] * q1 + c[2] * q2 + c[3] * q3
    scratch[1] = d * (q0 - c[0] * (q0 + q1) - c[1] * (q1 + q2) - c[2] * (q2 + q3)) - c[3] * w3
    for x in range(2):
        for i in range(4):
            rows, lanes = pl.ds(x * 4 + i, 4, stride=8), slice(i * 128, (i + 1) * 128)
            press_ref[x, :, lanes] = scratch[0, rows, :]
            resid_ref[x, :, lanes] = scratch[1, rows, :]
            for f in range(3):
                velo_ref[2 * f + x, :, lanes] = home[f, rows, :]


def body(velocity, reaction, table):
    f32 = jnp.float32
    spec = pl.BlockSpec(memory_space=pl.ANY)
    vmem = pl.BlockSpec(memory_space=pltpu.VMEM)
    scratch = [
        pltpu.VMEM((6, 4, 512), f32), pltpu.VMEM((2, 4, 512), f32), pltpu.VMEM(table.shape, f32),
        pltpu.SemaphoreType.DMA((3,)),
        pltpu.VMEM((4, 4, 8, 128), f32), pltpu.VMEM((4, 32, 128), f32), pltpu.SemaphoreType.DMA((5,)),
    ]
    scratch += [pltpu.VMEM((n, 8, 128), f32) for n, _ in ROUNDS] * 2
    scratch += [pltpu.VMEM((k, n, 8, 128), f32) for n, k in ROUNDS]
    scratch += [
        pltpu.SemaphoreType.DMA((2, len(ROUNDS))),
        pltpu.VMEM((2, 1, 128), f32), pltpu.VMEM((MEMBERS[0] - 1, 1, 128), f32), pltpu.VMEM((MEMBERS[1] - 1, 1, 128), f32),
        pltpu.SemaphoreType.DMA((2, 2)),
        pltpu.VMEM((9, 32, 128), f32), pltpu.VMEM((9, 32, 128), f32), pltpu.SemaphoreType.DMA((5, 4)),
    ]
    home, total = pl.pallas_call(
        kernel,
        out_shape=[jax.ShapeDtypeStruct((9, 32, 128), f32), jax.ShapeDtypeStruct((1, 128), f32)],
        in_specs=[spec] * 3,
        out_specs=[spec, vmem],
        scratch_shapes=scratch,
        compiler_params=pltpu.CompilerParams(collective_id=0, has_side_effects=True),
        name="duct_step",
    )(velocity.reshape(6, 4, 512), reaction.reshape(2, 4, 512), table)
    velo, press, resid = pl.pallas_call(
        combine,
        out_shape=[jax.ShapeDtypeStruct((6, 4, 512), f32)] + [jax.ShapeDtypeStruct((2, 4, 512), f32)] * 2,
        in_specs=[vmem] * 2,
        out_specs=[vmem] * 3,
        scratch_shapes=[pltpu.VMEM((2, 32, 128), f32)],
        name="combine",
    )(home, total)
    return velo.reshape(velocity.shape), press.reshape(reaction.shape), resid.reshape(reaction.shape)


def solution(mesh):
    specs = (P(None, "gx", "gy", "gz", None), P("gx", "gy", "gz", None))

    def step(velocity, reaction):
        return body(velocity, reaction, jnp.asarray(TABLE))

    return jax.shard_map(
        step, mesh=mesh, in_specs=specs, out_specs=(specs[0], specs[1], specs[1]), check_vma=False
    )
```

```python
import jax
import jax.numpy as jnp
import numpy as np
from jax import lax
from jax.experimental import pallas as pl
from jax.experimental.pallas import tpu as pltpu
from jax.sharding import PartitionSpec as P

MESH = pl.DeviceIdType.MESH
STEP = 0.02
HALF = 64
OFFSETS = ((-1, 0), (1, 0), (0, -1), (0, 1), (-1, -1), (1, -1), (-1, 1), (1, 1), (0, -2), (0, 2))
ROUNDS = ((3, 8), (1, 8), (3, 4), (3, 4), (2, 10), (2, 10), (1, 4))
GROUPS = ((0, 3), (3, 4), (7, 1), (8, 1))


def roll(values, shift, axis):
    shift = shift % values.shape[axis]
    return values if shift == 0 else pltpu.roll(values, shift, axis)


def div(value, by):
    return value // by if isinstance(value, (int, np.ndarray)) else lax.div(value, np.int32(by))


def rem(value, by):
    return value % by if isinstance(value, (int, np.ndarray)) else lax.rem(value, np.int32(by))


def tables():
    half = np.array([0.2092992179024788687, 0.5917001814331423022, 0.8717401485096066153, 1.0])
    points = np.concatenate([-half[::-1], half])
    earlier, current = points * 0.0 + 1.0, points
    for degree in range(1, 7):
        earlier, current = current, ((2 * degree + 1) * points * current - degree * earlier) / (degree + 1)
    w = 2.0 / (56.0 * current**2)
    spacing = points[:, None] - points[None, :] + np.eye(8)
    d = current[:, None] / current[None, :] / spacing * (1.0 - np.eye(8))
    d[0, 0] = -14.0
    d[7, 7] = 14.0
    k = d.T @ np.diag(w) @ d
    lane = np.arange(128)
    c, b, a_lo = lane % 8, (lane // 8) % 8, lane // 64
    rows = {}

    def put(name, values):
        rows[name] = (len(stack), len(values))
        stack.extend(values)

    stack = []

    def along_a(matrix, scale):
        return [matrix[2 * j + a_lo, q] * scale for j in range(4) for q in range(8)]

    def shifts(matrix, index, scale):
        out = []
        for s in range(-7, 8):
            source = index - s
            inside = (source >= 0) & (source <= 7)
            out.append(np.where(inside, matrix[index, np.clip(source, 0, 7)], 0.0) * scale)
        return out

    one = np.ones(128)
    put("da", along_a(d, one))
    put("db", shifts(d, b, one))
    put("dc", shifts(d, c, one))
    put("ka", along_a(k, one))
    put("kb", shifts(k, b, one))
    put("kc", shifts(k, c, one))
    s = (w[:, None] * d * d).sum(0)
    put("wa", [w[2 * i + a_lo] for i in range(4)])
    put("wb", [w[b]])
    put("wc", [w[c]])
    put("sa", [s[2 * i + a_lo] for i in range(4)])
    put("sb", [s[b]])
    put("sc", [s[c]])
    table = np.stack(stack).astype(np.float32)
    whole = np.ascontiguousarray(np.broadcast_to(table[:, None, :], (len(stack), 8, 128)))
    return whole, rows, float(k[0, 0]), float(k[0, 7])


TABLE, ROWS, NEAR, FAR = tables()


def owner_of(axial, depth):
    y, core = div(axial, 2), rem(axial, 2)
    z, turn = div(depth, 4), rem(depth, 4)
    x = turn + rem(z, 2) * (3 - 2 * turn)
    return (div(y, 4) * 8 + x * 2 + core, rem(y, 4), z)


class Place:
    def __init__(self, gx, gy, gz):
        self.gx, self.gy, self.gz = gx, gy, gz
        self.core, self.x, self.y_hi = rem(gx, 2), rem(div(gx, 2), 4), div(gx, 8)
        self.y, self.z = self.y_hi * 4 + gy, gz
        self.axial = self.y * 2 + self.core
        self.turn = self.x + rem(gz, 2) * (3 - 2 * self.x)
        self.depth = self.z * 4 + self.turn

    def mesh_id(self, x, y, z, core):
        return (div(y, 4) * 8 + x * 2 + core, rem(y, 4), z)

    def neighbour(self, dx, dz):
        return owner_of(rem(self.axial + dx + 16, 16), rem(self.depth + dz + 32, 32))

    def worker(self, i):
        x = rem(self.x + i, 4)
        return self.mesh_id(x, self.y_hi * 4 + self.x, self.z, self.core), x + rem(self.z, 2) * (3 - 2 * x)

    def home(self, i):
        cross = rem(self.gy + i, 4)
        return self.mesh_id(self.gy, self.y_hi * 4 + cross, self.z, self.core), cross

    def group(self, stage, i):
        if stage == 0:
            return self.mesh_id(self.x, self.y, rem(self.z + i // 2, 8), rem(self.core + i % 2, 2))
        return self.mesh_id(rem(self.x + i // 8, 4), rem(self.y + i % 8, 8), self.z, self.core)


MEMBERS = (16, 32)


def far_first(stage):
    def hops(i):
        if stage == 0:
            return (min(i // 2, 8 - i // 2), i % 2)
        return (min(i // 8, 4 - i // 8) + min(i % 8, 8 - i % 8), 0)

    return sorted(range(1, MEMBERS[stage]), key=hops, reverse=True)


def mirror(stage, i):
    if stage == 0:
        return (8 - i // 2) % 8 * 2 + i % 2
    return (4 - i // 8) % 4 * 8 + (8 - i % 8) % 8


class Masks:
    def __init__(self, depth):
        lane = lax.broadcasted_iota(jnp.int32, (8, 128), 1)
        row = lax.broadcasted_iota(jnp.int32, (8, 128), 0)
        c, b = lane & 7, (lane >> 3) & 7
        cross = row >> 1
        self.low = lane < HALF
        self.even = (row & 1) == 0
        odd = (row & 1) == 1
        high = lane >= HALF
        self.b0 = (b == 0) & (cross > 0)
        self.b7 = (b == 7) & (cross < 3)
        self.in0 = odd & self.low
        self.in3 = self.even & high
        self.out0 = self.even & self.low
        self.out3 = odd & high
        self.c = c
        self.c0, self.c7 = c == 0, c == 7
        self.slot_low = c < 4
        self.edge0 = self.out0 & ((c & 3) == 0)
        self.edge3 = self.out3 & ((c & 3) == 3)
        up = (depth < 31).astype(jnp.float32)
        down = (depth > 0).astype(jnp.float32)
        self.zmask = jnp.where(self.slot_low, up, down)
        self.far = jnp.where(self.slot_low, (depth < 30).astype(jnp.float32), (depth > 1).astype(jnp.float32)) * FAR
        self.faces = self.c0 | self.c7
        self.zhas = jnp.where(self.c0, down, jnp.where(self.c7, up, 0.0))
        one = jnp.ones((8, 128), jnp.float32)
        first, last = jnp.where(self.low, 0.5, one), jnp.where(self.low, one, 0.5)
        self.hx = [first, one, one, last]
        self.hy = jnp.where(self.b0 | self.b7, 0.5, one)
        self.hz = jnp.where(self.c0, 1.0 - 0.5 * down, jnp.where(self.c7, 1.0 - 0.5 * up, one))
        self.inverse = [x * (self.hy * self.hz) for x in self.hx]
        wall_y = ((b == 0) & (cross == 0)) | ((b == 7) & (cross == 3))
        self.interior = jnp.where(wall_y, 0.0, jnp.where(self.c0, down, jnp.where(self.c7, up, one)))


class Weights:
    def __init__(self, get, m):
        def row(name, i=0):
            return get(ROWS[name][0] + i)

        self.wa, self.wb, self.wc = [row("wa", i) for i in range(4)], row("wb"), row("wc")
        two_x, two_y, two_z = [1.0 / h for h in m.hx], 1.0 / m.hy, 1.0 / m.hz
        self.mx, self.my, self.mz = [x * t for x, t in zip(self.wa, two_x)], self.wb * two_y, self.wc * two_z
        self.yz = self.my * self.mz
        self.xz = [x * self.mz for x in self.mx]
        self.xy = [x * self.my for x in self.mx]
        self.all = [x * self.yz for x in self.mx]
        self.mass = [x * (self.wb * self.wc) for x in self.wa]
        self.diag = [
            row("sa", i) * two_x[i] * self.yz + row("sb") * two_y * self.xz[i] + row("sc") * two_z * self.xy[i]
            for i in range(4)
        ]


def join_cross(v, m):
    out = []
    for x in v:
        g = roll(roll(x, 2, 1), -56, 2)
        h = roll(roll(x, -2, 1), 56, 2)
        out.append(x + jnp.where(m.b0, g, jnp.where(m.b7, h, 0.0)))
    return out


def join_block(v, m):
    out = join_cross(v, m)
    first = roll(roll(out[3], 1, 1), HALF, 2)
    last = roll(roll(out[0], -1, 1), HALF, 2)
    out[0] = out[0] + jnp.where(m.in0, first, 0.0)
    out[3] = out[3] + jnp.where(m.in3, last, 0.0)
    return out


def pack(v, m):
    return jnp.where(m.low, v[0], v[3]), pack_depth(v, m)


def pack_depth(v, m):
    depth = v[0]
    for i in range(1, 4):
        if v[i] is not None:
            depth = jnp.where(m.c == i, roll(v[i], i, 2), depth)
    for i in range(4):
        if v[i] is not None:
            depth = jnp.where(m.c == 4 + i, roll(v[i], i - 3, 2), depth)
    return depth


def pack_axial(v, m):
    faces = roll(jnp.where(m.low, v[0], v[3]), HALF, 2)
    return jnp.where(m.even, roll(faces, -1, 1), roll(faces, 1, 1))


def spread(face, i, m):
    return jnp.where(m.c7, roll(face, 7 - i, 2), jnp.where(m.c0, roll(face, -4 - i, 2), 0.0))


def edges(got, m):
    before = jnp.where(m.slot_low, got[6], got[4])
    after = jnp.where(m.slot_low, got[7], got[5])
    return (jnp.where(m.edge0, roll(roll(before, -1, 1), -67, 2), 0.0)
            + jnp.where(m.edge3, roll(roll(after, 1, 1), 67, 2), 0.0)) * m.zmask


def pair_pack(fa, fc, base, pa, pc, get, m):
    axial = pack_axial(fa, m)
    own = list(base)
    own[0] = own[0] + pa[0] * jnp.where(m.in0, axial, 0.0)
    own[3] = own[3] + pa[3] * jnp.where(m.in3, axial, 0.0)
    ka = along_a(own, get, "ka", m, (0, 3))
    kc = along_lanes(own, get, "kc", 1)
    reach = [pc[i] * fc[i] for i in range(4)]
    ea = along_a([jnp.where(m.faces, x, 0.0) for x in reach], get, "ka", m, (0, 3))
    first, last = along_lanes([jnp.where(m.low, pa[0] * fa[0], 0.0), jnp.where(m.low, 0.0, pa[3] * fa[3])], get, "kc", 1)
    return (jnp.concatenate([axial, pack_axial(ka, m)], axis=0),
            jnp.concatenate([pack_depth(fc, m), pack_depth(kc, m)], axis=0),
            jnp.concatenate([pack_depth(ea, m), pack_depth([first, None, None, last], m)], axis=0),
            jnp.concatenate([pack_depth(reach, m), pack_depth(reach, m)], axis=0))


def pair_unpack(axial, got, fa, fc, base, pa, pc, get, m):
    across, depth = partners(axial, [g[0:1] for g in got], m)
    x = [base[i] + pc[i] * depth[i] for i in range(4)]
    for i in across:
        x[i] = x[i] + pa[i] * across[i]
    ga = edges([g[0:1] for g in got], m)
    second = [g[1:2] for g in got]
    face = jnp.where(m.slot_low, second[3], second[2]) * m.zmask + edges(second, m)
    face = face + jnp.where(m.slot_low, got[9][0:1], got[8][0:1]) * m.far
    depth = [spread(face, i, m) + NEAR * m.zhas * (pc[i] * fc[i]) for i in range(4)]
    across = {0: jnp.where(m.out0, second[0] + NEAR * (pa[0] * fa[0]), 0.0) + spread(ga, 0, m),
              3: jnp.where(m.out3, second[1] + NEAR * (pa[3] * fa[3]), 0.0) + spread(ga, 3, m)}
    return x, across, depth


def operate(x, across, depth, step, get, m):
    ka = along_a(x, get, "ka", m)
    kb = join_cross(along_lanes(x, get, "kb", 8), m)
    kc = along_lanes(x, get, "kc", 1)
    axial = pack_axial(ka, m)
    across = {0: across[0] + jnp.where(m.in0, axial, 0.0), 3: across[3] + jnp.where(m.in3, axial, 0.0)}
    out = [step[1][i] * kb[i] + step[2][i] * (kc[i] + depth[i]) + step[3][i] * x[i] for i in range(4)]
    return [out[i] + step[0][i] * (ka[i] + across[i] if i in across else ka[i]) for i in range(4)]


def partners(own, got, m):
    across = jnp.where(m.in0 | m.in3, own, jnp.where(m.low, got[0], got[1]))
    face = jnp.where(m.slot_low, got[3], got[2]) * m.zmask
    depth = [spread(face, i, m) for i in range(4)]
    return {0: jnp.where(m.low, across, 0.0), 3: jnp.where(m.low, 0.0, across)}, depth


def unpack(v, got, m):
    v = list(v)
    v[0] = v[0] + jnp.where(m.out0, roll(roll(got[0], -1, 1), HALF, 2), 0.0)
    v[3] = v[3] + jnp.where(m.out3, roll(roll(got[1], 1, 1), HALF, 2), 0.0)
    centre = jnp.where(m.slot_low, got[3], got[2])
    before = jnp.where(m.slot_low, got[6], got[4])
    after = jnp.where(m.slot_low, got[7], got[5])
    face = centre + jnp.where(m.edge0, roll(roll(before, -1, 1), -67, 2), 0.0)
    face = face + jnp.where(m.edge3, roll(roll(after, 1, 1), 67, 2), 0.0)
    face = face * m.zmask
    return [
        v[i] + jnp.where(m.c7, roll(face, 7 - i, 2), jnp.where(m.c0, roll(face, -4 - i, 2), 0.0))
        for i in range(4)
    ]


def along_a(v, get, name, m, wanted=range(4)):
    parts = []
    for x in v:
        turned = roll(x, HALF, 2)
        parts.append(jnp.where(m.low, x, turned))
        parts.append(jnp.where(m.low, turned, x))
    start = ROWS[name][0]
    return [sum_of([get(start + j * 8 + q) * parts[q] for q in range(8)]) if j in wanted else None for j in range(4)]


def along_lanes(v, get, name, stride):
    start = ROWS[name][0]
    return [sum_of([get(start + s + 7) * roll(x, s * stride, 2) for s in range(-7, 8)]) for x in v]


def sum_of(terms):
    while len(terms) > 1:
        terms = [terms[i] + terms[i + 1] if i + 1 < len(terms) else terms[i] for i in range(0, len(terms), 2)]
    return terms[0]


def moment(k, f, g, weight=None):
    total = sum_of([f[i][0] * g[i][0] if weight is None else f[i][0] * g[i][0] * weight[i] for i in range(4)])
    total = jnp.sum(total, axis=0, keepdims=True)
    for shift in (64, 32, 16):
        total = total + roll(total, shift, 1)
    lane = lax.broadcasted_iota(jnp.int32, (1, 128), 1)
    return jnp.where((lane >> 4) == k, total, 0.0)


def solve(n, e):
    g = [[(n[i + j] + n[i + j + 1]) if i + j < 6 else e for j in range(4)] for i in range(4)]
    rhs = [n[i] for i in range(4)]
    inverse = []
    for i in range(4):
        inverse.append(1.0 / g[i][i])
        for r in range(i + 1, 4):
            factor = g[r][i] * inverse[i]
            for j in range(i + 1, 4):
                g[r][j] = g[r][j] - factor * g[i][j]
            rhs[r] = rhs[r] - factor * rhs[i]
    out = [None] * 4
    for i in range(3, -1, -1):
        total = rhs[i]
        for j in range(i + 1, 4):
            total = total - g[i][j] * out[j]
        out[i] = total * inverse[i]
    return out


def kernel(vel_hbm, react_hbm, table_hbm, home_ref, total_ref, vel, react, tab, load_sem,
           send0, recv0, sem0, *rest):
    rounds = len(ROUNDS)
    send_x, send_z = rest[0:rounds], rest[rounds:2 * rounds]
    got_refs = rest[2 * rounds:3 * rounds]
    (send_far, round_sem, part, sums0, sums1, sum_sem, back_send, back_recv, back_sem) = rest[3 * rounds:]
    sums = (sums0, sums1)
    place = Place(lax.axis_index("gx"), lax.axis_index("gy"), lax.axis_index("gz"))

    def push(source, target, device, send_sem, recv_sem, own=None):
        def remote():
            pltpu.make_async_remote_copy(source, target, send_sem, recv_sem, device_id=device, device_id_type=MESH).start()

        if own is None:
            remote()
            return
        pl.when(jnp.logical_not(own))(remote)

        @pl.when(own)
        def _():
            pltpu.make_async_copy(source, target, recv_sem).start()

    def greet(device):
        pl.semaphore_signal(barrier, inc=1, device_id=device, device_id_type=MESH)

    barrier = pltpu.get_barrier_semaphore()
    count = 0
    for i in range(4):
        greet(place.worker(i)[0])
        greet(place.home(i)[0])
        count += 2
    for dx, dz in OFFSETS:
        greet(place.neighbour(dx, dz))
        count += 1
    for stage in range(2):
        for i in far_first(stage):
            greet(place.group(stage, i))
            count += 1

    loads = [pltpu.make_async_copy(s, d, load_sem.at[k]) for k, (s, d) in
             enumerate(((vel_hbm, vel), (react_hbm, react), (table_hbm, tab)))]
    for copy in loads:
        copy.start()
    m = Masks(place.depth)
    loads[0].wait()
    loads[1].wait()
    for f in range(4):
        for x in range(2):
            for i in range(4):
                lanes = slice(i * 128, (i + 1) * 128)
                piece = vel[2 * f + x, :, lanes] if f < 3 else react[x, :, lanes]
                send0.reshape(128, 128)[pl.ds(f * 8 + x * 4 + i, 4, stride=32), :] = piece
    pl.semaphore_wait(barrier, count)

    own = place.x == place.gy
    into = pl.ds(pl.multiple_of(place.gy * 8, 8), 8)
    for i in (2, 1, 3, 0):
        device, turn = place.worker(i)
        push(send0.at[turn], recv0.at[:, into], device, sem0.at[i], sem0.at[4], None if i else own)

    loads[2].wait()

    def get(row):
        return tab[row]

    pltpu.make_async_copy(recv0, recv0, sem0.at[4]).wait()
    fields = [jnp.stack([recv0[f, pl.ds(i, 8, stride=4), :] for f in range(4)]) for i in range(4)]

    def send(r, axial, depth, edge=None, far=None):
        send_x[r][...] = axial
        send_z[r][...] = depth
        if edge is not None:
            send_far[r % 2, 0] = edge
            send_far[r % 2, 1] = far
        for dx, dz in OFFSETS[4:ROUNDS[r][1]] + OFFSETS[2:4] + OFFSETS[0:2]:
            slot = OFFSETS.index((-dx, -dz))
            source = send_x[r] if dz == 0 else send_z[r]
            if edge is not None and abs(dx) + abs(dz) == 2:
                source = send_far.at[r % 2, 0 if dx else 1]
            pltpu.make_async_remote_copy(
                source, got_refs[r].at[slot], round_sem.at[0, r], round_sem.at[1, r],
                device_id=place.neighbour(dx, dz), device_id_type=MESH).start()

    def receive(r):
        pltpu.make_async_copy(got_refs[r], got_refs[r], round_sem.at[1, r]).wait()
        return [got_refs[r][k] for k in range(ROUNDS[r][1])]

    def send_faces(r, along_axis, along_depth):
        axial = pack_axial(along_axis, m)
        send(r, axial, pack_depth(along_depth, m))
        return axial

    def give_back(g):
        first, number = GROUPS[g]
        fields = pl.ds(first, number)
        into = pl.ds(pl.multiple_of(place.turn * 8, 8), 8)
        for i in (2, 1, 3, 0):
            device, cross = place.home(i)
            rows = pl.ds(pl.multiple_of(cross * 8, 8), 8)
            push(back_send.at[fields, rows], back_recv.at[fields, into], device,
                 back_sem.at[i, g], back_sem.at[4, g], None if i else own)

    def keep(f, v):
        for i in range(4):
            back_send[f, pl.ds(i, 8, stride=4), :] = v[i]

    v = join_block([x[0:3] for x in fields], m)
    send(0, *pack(v, m))
    wt = Weights(get, m)
    scaled = [fields[i][3:4] * wt.mass[i] for i in range(4)]
    react_sum = join_block(scaled, m)
    send(1, *pack(react_sum, m))
    inside = STEP * m.interior
    rate = ([inside * h for h in m.hx], inside * m.hy, inside * m.hz)
    v = unpack(v, receive(0), m)
    u = [v[i] * m.inverse[i] for i in range(4)]

    for r in (2, 3):
        da = along_a(u, get, "da", m)
        dc = along_lanes(u, get, "dc", 1)
        axial = send_faces(r, da, dc)
        db = join_cross(along_lanes(u, get, "db", 8), m)
        first = [rate[0][i] * u[i][0:1] for i in range(4)]
        third = [rate[2] * u[i][2:3] for i in range(4)]
        base = [m.interior * u[i] - (first[i] * da[i] + rate[1] * u[i][1:2] * db[i] + third[i] * dc[i]) for i in range(4)]
        if r == 3:
            react_sum = unpack(react_sum, receive(1), m)
            diag = [wt.diag[i] + react_sum[i] for i in range(4)]
            inverse_diag = [1.0 / x for x in diag]
            step = ([wt.yz * x for x in inverse_diag],
                    [wt.xz[i] * inverse_diag[i] for i in range(4)],
                    [wt.xy[i] * inverse_diag[i] for i in range(4)],
                    [react_sum[i] * inverse_diag[i] - 1.0 for i in range(4)])
            volume = [-wt.all[i] * inverse_diag[i] for i in range(4)]
            weight = [diag[i][0] * m.inverse[i] for i in range(4)]
            keep(3, [x[0] for x in diag])
        across, depth = partners(axial, receive(r), m)
        u = [base[i] - third[i] * depth[i] for i in range(4)]
        for i in across:
            u[i] = u[i] - first[i] * across[i]

    da = along_a([x[0:1] for x in u], get, "da", m)
    dc = along_lanes([x[2:3] for x in u], get, "dc", 1)
    db = join_cross(along_lanes([x[1:2] for x in u], get, "db", 8), m)
    base = [volume[i] * (m.hx[i] * da[i] + m.hy * db[i] + m.hz * dc[i]) for i in range(4)]
    pa, pc = [volume[i] * m.hx[i] for i in range(4)], [volume[i] * m.hz for i in range(4)]
    tiles = pair_pack(da, dc, base, pa, pc, get, m)
    send(4, *tiles)
    for k in range(3):
        keep(k, [x[k] for x in u])
    give_back(0)
    x, across, depth = pair_unpack(tiles[0][0:1], receive(4), da, dc, base, pa, pc, get, m)
    q = [x, operate(x, across, depth, step, get, m)]

    ka, kb, kc = along_a(q[1], get, "ka", m), along_lanes(q[1], get, "kb", 8), along_lanes(q[1], get, "kc", 1)
    kb = join_cross(kb, m)
    base = [step[0][i] * ka[i] + step[1][i] * kb[i] + step[2][i] * kc[i] + step[3][i] * q[1][i] for i in range(4)]
    tiles = pair_pack(ka, kc, base, step[0], step[2], get, m)
    send(5, *tiles)
    early = moment(0, q[0], q[0], weight) + moment(1, q[0], q[1], weight) + moment(2, q[1], q[1], weight)
    for j in range(2):
        keep(4 + j, [x[0] for x in q[j]])
    x, across, depth = pair_unpack(tiles[0][0:1], receive(5), ka, kc, base, step[0], step[2], get, m)
    q += [x, operate(x, across, depth, step, get, m)]

    early = early + moment(3, q[1], q[2], weight) + moment(4, q[2], q[2], weight)
    ka, kb, kc = along_a(q[3], get, "ka", m), along_lanes(q[3], get, "kb", 8), along_lanes(q[3], get, "kc", 1)
    energy = [
        wt.wb * wt.wc * ka[i] + wt.wa[i] * (wt.wc * kb[i] + wt.wb * kc[i]) + scaled[i] * q[3][i] for i in range(4)
    ]
    part[0] = (early + moment(5, q[2], q[3], weight)) + (moment(6, q[3], q[3], weight) + moment(7, q[3], energy))

    def send_sum(stage):
        for i in far_first(stage):
            pltpu.make_async_remote_copy(part.at[stage], sums[stage].at[mirror(stage, i) - 1], sum_sem.at[0, stage],
                                         sum_sem.at[1, stage], device_id=place.group(stage, i), device_id_type=MESH).start()

    def take_sum(stage):
        pltpu.make_async_copy(sums[stage], sums[stage], sum_sem.at[1, stage]).wait()
        return sum_of([part[stage]] + [sums[stage][i] for i in range(MEMBERS[stage] - 1)])

    send_sum(0)
    axial = send_faces(6, ka, kc)
    kb = join_cross(kb, m)
    base = [wt.yz * ka[i] + wt.xz[i] * kb[i] + wt.xy[i] * kc[i] + react_sum[i] * q[3][i] for i in range(4)]
    for j in (2, 3):
        keep(4 + j, [x[0] for x in q[j]])
    give_back(1)
    give_back(2)
    part[1] = take_sum(0)
    send_sum(1)
    across, depth = partners(axial, receive(6), m)
    w = [base[i] + wt.xy[i] * depth[i] for i in range(4)]
    for i in across:
        w[i] = w[i] + wt.yz * across[i]
    keep(8, [x[0] for x in w])
    give_back(3)
    for g, (first, number) in enumerate(GROUPS):
        ref = back_recv.at[pl.ds(first, number)]
        pltpu.make_async_copy(ref, ref, back_sem.at[4, g]).wait()
    leave = pltpu.make_async_copy(back_recv, home_ref, load_sem.at[0])
    leave.start()

    for r in range(rounds):
        pltpu.make_async_copy(got_refs[r], got_refs[r], round_sem.at[0, r]).wait()
    for stage in range(2):
        pltpu.make_async_copy(sums[stage], sums[stage], sum_sem.at[0, stage]).wait()

    def sent(i):
        ref = recv0.at[:, pl.ds(0, 8)]
        pltpu.make_async_copy(ref, ref, sem0.at[i]).wait()
        for g, (first, number) in enumerate(GROUPS):
            ref = back_recv.at[pl.ds(first, number), pl.ds(0, 8)]
            pltpu.make_async_copy(ref, ref, back_sem.at[i, g]).wait()

    for i in range(1, 4):
        sent(i)

    @pl.when(jnp.logical_not(own))
    def _():
        sent(0)

    total_ref[...] = take_sum(1)
    leave.wait()


def combine(home, total_ref, velo_ref, press_ref, resid_ref, scratch):
    lane = lax.broadcasted_iota(jnp.int32, (8, 128), 1)
    row = lax.broadcasted_iota(jnp.int32, (8, 128), 0)
    n = jnp.sum(jnp.where((lane >> 4) == row, total_ref[...], 0.0), axis=1, keepdims=True)
    n = jnp.broadcast_to(n, (8, 128))
    c = solve([n[i:i + 1, :] for i in range(7)], n[7:8, :])
    d, q0, q1, q2, q3, w3 = [home[f] for f in range(3, 9)]
    scratch[0] = c[0] * q0 + c[1] * q1 + c[2] * q2 + c[3] * q3
    scratch[1] = d * (q0 - c[0] * (q0 + q1) - c[1] * (q1 + q2) - c[2] * (q2 + q3)) - c[3] * w3
    for x in range(2):
        for i in range(4):
            rows, lanes = pl.ds(x * 4 + i, 4, stride=8), slice(i * 128, (i + 1) * 128)
            press_ref[x, :, lanes] = scratch[0, rows, :]
            resid_ref[x, :, lanes] = scratch[1, rows, :]
            for f in range(3):
                velo_ref[2 * f + x, :, lanes] = home[f, rows, :]


def body(velocity, reaction, table):
    f32 = jnp.float32
    spec = pl.BlockSpec(memory_space=pl.ANY)
    vmem = pl.BlockSpec(memory_space=pltpu.VMEM)
    scratch = [
        pltpu.VMEM((6, 4, 512), f32), pltpu.VMEM((2, 4, 512), f32), pltpu.VMEM(table.shape, f32),
        pltpu.SemaphoreType.DMA((3,)),
        pltpu.VMEM((4, 4, 8, 128), f32), pltpu.VMEM((4, 32, 128), f32), pltpu.SemaphoreType.DMA((5,)),
    ]
    scratch += [pltpu.VMEM((n, 8, 128), f32) for n, _ in ROUNDS] * 2
    scratch += [pltpu.VMEM((k, n, 8, 128), f32) for n, k in ROUNDS]
    scratch += [
        pltpu.VMEM((2, 2, 2, 8, 128), f32), pltpu.SemaphoreType.DMA((2, len(ROUNDS))),
        pltpu.VMEM((2, 1, 128), f32), pltpu.VMEM((MEMBERS[0] - 1, 1, 128), f32), pltpu.VMEM((MEMBERS[1] - 1, 1, 128), f32),
        pltpu.SemaphoreType.DMA((2, 2)),
        pltpu.VMEM((9, 32, 128), f32), pltpu.VMEM((9, 32, 128), f32), pltpu.SemaphoreType.DMA((5, 4)),
    ]
    home, total = pl.pallas_call(
        kernel,
        out_shape=[jax.ShapeDtypeStruct((9, 32, 128), f32), jax.ShapeDtypeStruct((1, 128), f32)],
        in_specs=[spec] * 3,
        out_specs=[spec, vmem],
        scratch_shapes=scratch,
        compiler_params=pltpu.CompilerParams(collective_id=0, has_side_effects=True),
        name="duct_step",
    )(velocity.reshape(6, 4, 512), reaction.reshape(2, 4, 512), table)
    velo, press, resid = pl.pallas_call(
        combine,
        out_shape=[jax.ShapeDtypeStruct((6, 4, 512), f32)] + [jax.ShapeDtypeStruct((2, 4, 512), f32)] * 2,
        in_specs=[vmem] * 2,
        out_specs=[vmem] * 3,
        scratch_shapes=[pltpu.VMEM((2, 32, 128), f32)],
        name="combine",
    )(home, total)
    return velo.reshape(velocity.shape), press.reshape(reaction.shape), resid.reshape(reaction.shape)


def solution(mesh):
    specs = (P(None, "gx", "gy", "gz", None), P("gx", "gy", "gz", None))

    def step(velocity, reaction):
        return body(velocity, reaction, jnp.asarray(TABLE))

    return jax.shard_map(
        step, mesh=mesh, in_specs=specs, out_specs=(specs[0], specs[1], specs[1]), check_vma=False
    )
```

```python
import jax
import jax.numpy as jnp
import numpy as np
from jax import lax
from jax.experimental import pallas as pl
from jax.experimental.pallas import tpu as pltpu
from jax.sharding import PartitionSpec as P

MESH = pl.DeviceIdType.MESH
STEP = 0.02
HALF = 64
OFFSETS = ((-1, 0), (1, 0), (0, -1), (0, 1), (-1, -1), (1, -1), (-1, 1), (1, 1), (0, -2), (0, 2))
ROUNDS = ((3, 8), (1, 8), (3, 4), (3, 4), (2, 10), (2, 10), (1, 4))
GROUPS = ((0, 3), (3, 4), (7, 1), (8, 1))


def roll(values, shift, axis):
    shift = shift % values.shape[axis]
    return values if shift == 0 else pltpu.roll(values, shift, axis)


def div(value, by):
    return value // by if isinstance(value, (int, np.ndarray)) else lax.div(value, np.int32(by))


def rem(value, by):
    return value % by if isinstance(value, (int, np.ndarray)) else lax.rem(value, np.int32(by))


def tables():
    half = np.array([0.2092992179024788687, 0.5917001814331423022, 0.8717401485096066153, 1.0])
    points = np.concatenate([-half[::-1], half])
    earlier, current = points * 0.0 + 1.0, points
    for degree in range(1, 7):
        earlier, current = current, ((2 * degree + 1) * points * current - degree * earlier) / (degree + 1)
    w = 2.0 / (56.0 * current**2)
    spacing = points[:, None] - points[None, :] + np.eye(8)
    d = current[:, None] / current[None, :] / spacing * (1.0 - np.eye(8))
    d[0, 0] = -14.0
    d[7, 7] = 14.0
    k = d.T @ np.diag(w) @ d
    lane = np.arange(128)
    c, b, a_lo = lane % 8, (lane // 8) % 8, lane // 64
    rows = {}

    def put(name, values):
        rows[name] = (len(stack), len(values))
        stack.extend(values)

    stack = []

    def along_a(matrix, scale):
        return [matrix[2 * j + a_lo, q] * scale for j in range(4) for q in range(8)]

    def shifts(matrix, index, scale):
        out = []
        for s in range(-7, 8):
            source = index - s
            inside = (source >= 0) & (source <= 7)
            out.append(np.where(inside, matrix[index, np.clip(source, 0, 7)], 0.0) * scale)
        return out

    one = np.ones(128)
    put("da", along_a(d, one))
    put("db", shifts(d, b, one))
    put("dc", shifts(d, c, one))
    put("ka", along_a(k, one))
    put("kb", shifts(k, b, one))
    put("kc", shifts(k, c, one))
    s = (w[:, None] * d * d).sum(0)
    put("wa", [w[2 * i + a_lo] for i in range(4)])
    put("wb", [w[b]])
    put("wc", [w[c]])
    put("sa", [s[2 * i + a_lo] for i in range(4)])
    put("sb", [s[b]])
    put("sc", [s[c]])
    table = np.stack(stack).astype(np.float32)
    whole = np.ascontiguousarray(np.broadcast_to(table[:, None, :], (len(stack), 8, 128)))
    return whole, rows, float(k[0, 0]), float(k[0, 7])


TABLE, ROWS, NEAR, FAR = tables()


def owner_of(axial, depth):
    y, core = div(axial, 2), rem(axial, 2)
    z, turn = div(depth, 4), rem(depth, 4)
    x = turn + rem(z, 2) * (3 - 2 * turn)
    return (div(y, 4) * 8 + x * 2 + core, rem(y, 4), z)


class Place:
    def __init__(self, gx, gy, gz):
        self.gx, self.gy, self.gz = gx, gy, gz
        self.core, self.x, self.y_hi = rem(gx, 2), rem(div(gx, 2), 4), div(gx, 8)
        self.y, self.z = self.y_hi * 4 + gy, gz
        self.axial = self.y * 2 + self.core
        self.turn = self.x + rem(gz, 2) * (3 - 2 * self.x)
        self.depth = self.z * 4 + self.turn

    def mesh_id(self, x, y, z, core):
        return (div(y, 4) * 8 + x * 2 + core, rem(y, 4), z)

    def neighbour(self, dx, dz):
        return owner_of(rem(self.axial + dx + 16, 16), rem(self.depth + dz + 32, 32))

    def worker(self, i):
        x = rem(self.x + i, 4)
        return self.mesh_id(x, self.y_hi * 4 + self.x, self.z, self.core), x + rem(self.z, 2) * (3 - 2 * x)

    def home(self, i):
        cross = rem(self.gy + i, 4)
        return self.mesh_id(self.gy, self.y_hi * 4 + cross, self.z, self.core), cross

    def group(self, stage, i):
        if stage == 0:
            return self.mesh_id(self.x, self.y, rem(self.z + i // 2, 8), rem(self.core + i % 2, 2))
        return self.mesh_id(rem(self.x + i // 8, 4), rem(self.y + i % 8, 8), self.z, self.core)


MEMBERS = (16, 32)


def far_first(stage):
    def hops(i):
        if stage == 0:
            return (min(i // 2, 8 - i // 2), i % 2)
        return (min(i // 8, 4 - i // 8) + min(i % 8, 8 - i % 8), 0)

    return sorted(range(1, MEMBERS[stage]), key=hops, reverse=True)


def mirror(stage, i):
    if stage == 0:
        return (8 - i // 2) % 8 * 2 + i % 2
    return (4 - i // 8) % 4 * 8 + (8 - i % 8) % 8


class Masks:
    def __init__(self, depth):
        lane = lax.broadcasted_iota(jnp.int32, (8, 128), 1)
        row = lax.broadcasted_iota(jnp.int32, (8, 128), 0)
        c, b = lane & 7, (lane >> 3) & 7
        cross = row >> 1
        self.low = lane < HALF
        self.even = (row & 1) == 0
        odd = (row & 1) == 1
        high = lane >= HALF
        self.b0 = (b == 0) & (cross > 0)
        self.b7 = (b == 7) & (cross < 3)
        self.in0 = odd & self.low
        self.in3 = self.even & high
        self.out0 = self.even & self.low
        self.out3 = odd & high
        self.c = c
        self.c0, self.c7 = c == 0, c == 7
        self.slot_low = c < 4
        self.edge0 = self.out0 & ((c & 3) == 0)
        self.edge3 = self.out3 & ((c & 3) == 3)
        up = (depth < 31).astype(jnp.float32)
        down = (depth > 0).astype(jnp.float32)
        self.zmask = jnp.where(self.slot_low, up, down)
        self.far = jnp.where(self.slot_low, (depth < 30).astype(jnp.float32), (depth > 1).astype(jnp.float32)) * FAR
        self.faces = self.c0 | self.c7
        self.zhas = jnp.where(self.c0, down, jnp.where(self.c7, up, 0.0))
        one = jnp.ones((8, 128), jnp.float32)
        first, last = jnp.where(self.low, 0.5, one), jnp.where(self.low, one, 0.5)
        self.hx = [first, one, one, last]
        self.hy = jnp.where(self.b0 | self.b7, 0.5, one)
        self.hz = jnp.where(self.c0, 1.0 - 0.5 * down, jnp.where(self.c7, 1.0 - 0.5 * up, one))
        self.inverse = [x * (self.hy * self.hz) for x in self.hx]
        wall_y = ((b == 0) & (cross == 0)) | ((b == 7) & (cross == 3))
        self.interior = jnp.where(wall_y, 0.0, jnp.where(self.c0, down, jnp.where(self.c7, up, one)))


class Weights:
    def __init__(self, get, m):
        def row(name, i=0):
            return get(ROWS[name][0] + i)

        self.wa, self.wb, self.wc = [row("wa", i) for i in range(4)], row("wb"), row("wc")
        two_x, two_y, two_z = [1.0 / h for h in m.hx], 1.0 / m.hy, 1.0 / m.hz
        self.mx, self.my, self.mz = [x * t for x, t in zip(self.wa, two_x)], self.wb * two_y, self.wc * two_z
        self.yz = self.my * self.mz
        self.xz = [x * self.mz for x in self.mx]
        self.xy = [x * self.my for x in self.mx]
        self.all = [x * self.yz for x in self.mx]
        self.mass = [x * (self.wb * self.wc) for x in self.wa]
        self.diag = [
            row("sa", i) * two_x[i] * self.yz + row("sb") * two_y * self.xz[i] + row("sc") * two_z * self.xy[i]
            for i in range(4)
        ]


def join_cross(v, m):
    out = []
    for x in v:
        g = roll(roll(x, 2, 1), -56, 2)
        h = roll(roll(x, -2, 1), 56, 2)
        out.append(x + jnp.where(m.b0, g, jnp.where(m.b7, h, 0.0)))
    return out


def join_block(v, m):
    out = join_cross(v, m)
    first = roll(roll(out[3], 1, 1), HALF, 2)
    last = roll(roll(out[0], -1, 1), HALF, 2)
    out[0] = out[0] + jnp.where(m.in0, first, 0.0)
    out[3] = out[3] + jnp.where(m.in3, last, 0.0)
    return out


def pack(v, m):
    return jnp.where(m.low, v[0], v[3]), pack_depth(v, m)


def pack_depth(v, m):
    depth = v[0]
    for i in range(1, 4):
        if v[i] is not None:
            depth = jnp.where(m.c == i, roll(v[i], i, 2), depth)
    for i in range(4):
        if v[i] is not None:
            depth = jnp.where(m.c == 4 + i, roll(v[i], i - 3, 2), depth)
    return depth


def pack_axial(v, m):
    faces = roll(jnp.where(m.low, v[0], v[3]), HALF, 2)
    return jnp.where(m.even, roll(faces, -1, 1), roll(faces, 1, 1))


def spread(face, i, m):
    return jnp.where(m.c7, roll(face, 7 - i, 2), jnp.where(m.c0, roll(face, -4 - i, 2), 0.0))


def edges(got, m):
    before = jnp.where(m.slot_low, got[6], got[4])
    after = jnp.where(m.slot_low, got[7], got[5])
    return (jnp.where(m.edge0, roll(roll(before, -1, 1), -67, 2), 0.0)
            + jnp.where(m.edge3, roll(roll(after, 1, 1), 67, 2), 0.0)) * m.zmask


def pair_pack(fa, fc, base, pa, pc, get, m):
    axial = pack_axial(fa, m)
    own = list(base)
    own[0] = own[0] + pa[0] * jnp.where(m.in0, axial, 0.0)
    own[3] = own[3] + pa[3] * jnp.where(m.in3, axial, 0.0)
    ka = along_a(own, get, "ka", m, (0, 3))
    kc = along_lanes(own, get, "kc", 1)
    reach = [pc[i] * fc[i] for i in range(4)]
    ea = along_a([jnp.where(m.faces, x, 0.0) for x in reach], get, "ka", m, (0, 3))
    first, last = along_lanes([jnp.where(m.low, pa[0] * fa[0], 0.0), jnp.where(m.low, 0.0, pa[3] * fa[3])], get, "kc", 1)
    return (jnp.concatenate([axial, pack_axial(ka, m)], axis=0),
            jnp.concatenate([pack_depth(fc, m), pack_depth(kc, m)], axis=0),
            jnp.concatenate([pack_depth(ea, m), pack_depth([first, None, None, last], m)], axis=0),
            jnp.concatenate([pack_depth(reach, m), pack_depth(reach, m)], axis=0))


def pair_unpack(axial, got, fa, fc, base, pa, pc, get, m):
    across, depth = partners(axial, [g[0:1] for g in got], m)
    x = [base[i] + pc[i] * depth[i] for i in range(4)]
    for i in across:
        x[i] = x[i] + pa[i] * across[i]
    ga = edges([g[0:1] for g in got], m)
    second = [g[1:2] for g in got]
    face = jnp.where(m.slot_low, second[3], second[2]) * m.zmask + edges(second, m)
    face = face + jnp.where(m.slot_low, got[9][0:1], got[8][0:1]) * m.far
    depth = [spread(face, i, m) + NEAR * m.zhas * (pc[i] * fc[i]) for i in range(4)]
    across = {0: jnp.where(m.out0, second[0] + NEAR * (pa[0] * fa[0]), 0.0) + spread(ga, 0, m),
              3: jnp.where(m.out3, second[1] + NEAR * (pa[3] * fa[3]), 0.0) + spread(ga, 3, m)}
    return x, across, depth


def operate(x, across, depth, step, get, m):
    ka = along_a(x, get, "ka", m)
    kb = join_cross(along_lanes(x, get, "kb", 8), m)
    kc = along_lanes(x, get, "kc", 1)
    axial = pack_axial(ka, m)
    across = {0: across[0] + jnp.where(m.in0, axial, 0.0), 3: across[3] + jnp.where(m.in3, axial, 0.0)}
    out = [step[1][i] * kb[i] + step[2][i] * (kc[i] + depth[i]) + step[3][i] * x[i] for i in range(4)]
    return [out[i] + step[0][i] * (ka[i] + across[i] if i in across else ka[i]) for i in range(4)]


def partners(own, got, m):
    across = jnp.where(m.in0 | m.in3, own, jnp.where(m.low, got[0], got[1]))
    face = jnp.where(m.slot_low, got[3], got[2]) * m.zmask
    depth = [spread(face, i, m) for i in range(4)]
    return {0: jnp.where(m.low, across, 0.0), 3: jnp.where(m.low, 0.0, across)}, depth


def unpack(v, got, m):
    v = list(v)
    v[0] = v[0] + jnp.where(m.out0, roll(roll(got[0], -1, 1), HALF, 2), 0.0)
    v[3] = v[3] + jnp.where(m.out3, roll(roll(got[1], 1, 1), HALF, 2), 0.0)
    centre = jnp.where(m.slot_low, got[3], got[2])
    before = jnp.where(m.slot_low, got[6], got[4])
    after = jnp.where(m.slot_low, got[7], got[5])
    face = centre + jnp.where(m.edge0, roll(roll(before, -1, 1), -67, 2), 0.0)
    face = face + jnp.where(m.edge3, roll(roll(after, 1, 1), 67, 2), 0.0)
    face = face * m.zmask
    return [
        v[i] + jnp.where(m.c7, roll(face, 7 - i, 2), jnp.where(m.c0, roll(face, -4 - i, 2), 0.0))
        for i in range(4)
    ]


def along_a(v, get, name, m, wanted=range(4)):
    parts = []
    for x in v:
        turned = roll(x, HALF, 2)
        parts.append(jnp.where(m.low, x, turned))
        parts.append(jnp.where(m.low, turned, x))
    start = ROWS[name][0]
    return [sum_of([get(start + j * 8 + q) * parts[q] for q in range(8)]) if j in wanted else None for j in range(4)]


def along_lanes(v, get, name, stride):
    start = ROWS[name][0]
    return [sum_of([get(start + s + 7) * roll(x, s * stride, 2) for s in range(-7, 8)]) for x in v]


def sum_of(terms):
    while len(terms) > 1:
        terms = [terms[i] + terms[i + 1] if i + 1 < len(terms) else terms[i] for i in range(0, len(terms), 2)]
    return terms[0]


def moment(k, f, g, weight=None):
    total = sum_of([f[i][0] * g[i][0] if weight is None else f[i][0] * g[i][0] * weight[i] for i in range(4)])
    total = jnp.sum(total, axis=0, keepdims=True)
    for shift in (64, 32, 16):
        total = total + roll(total, shift, 1)
    lane = lax.broadcasted_iota(jnp.int32, (1, 128), 1)
    return jnp.where((lane >> 4) == k, total, 0.0)


def solve(n, e):
    g = [[(n[i + j] + n[i + j + 1]) if i + j < 6 else e for j in range(4)] for i in range(4)]
    rhs = [n[i] for i in range(4)]
    inverse = []
    for i in range(4):
        inverse.append(1.0 / g[i][i])
        for r in range(i + 1, 4):
            factor = g[r][i] * inverse[i]
            for j in range(i + 1, 4):
                g[r][j] = g[r][j] - factor * g[i][j]
            rhs[r] = rhs[r] - factor * rhs[i]
    out = [None] * 4
    for i in range(3, -1, -1):
        total = rhs[i]
        for j in range(i + 1, 4):
            total = total - g[i][j] * out[j]
        out[i] = total * inverse[i]
    return out


def kernel(vel_hbm, react_hbm, table_hbm, home_ref, total_ref, vel, react, tab, load_sem,
           send0, recv0, sem0, *rest):
    rounds = len(ROUNDS)
    send_x, send_z = rest[0:rounds], rest[rounds:2 * rounds]
    got_refs = rest[2 * rounds:3 * rounds]
    (send_far, round_sem, part, sums0, sums1, sum_sem, back_send, back_recv, back_sem) = rest[3 * rounds:]
    sums = (sums0, sums1)
    place = Place(lax.axis_index("gx"), lax.axis_index("gy"), lax.axis_index("gz"))

    def push(source, target, device, send_sem, recv_sem, own=None):
        def remote():
            pltpu.make_async_remote_copy(source, target, send_sem, recv_sem, device_id=device, device_id_type=MESH).start()

        if own is None:
            remote()
            return
        pl.when(jnp.logical_not(own))(remote)

        @pl.when(own)
        def _():
            pltpu.make_async_copy(source, target, recv_sem).start()

    def greet(device):
        pl.semaphore_signal(barrier, inc=1, device_id=device, device_id_type=MESH)

    barrier = pltpu.get_barrier_semaphore()
    count = 0
    for i in range(4):
        greet(place.worker(i)[0])
        greet(place.home(i)[0])
        count += 2
    loads = [pltpu.make_async_copy(s, d, load_sem.at[k]) for k, (s, d) in
             enumerate(((vel_hbm, vel), (react_hbm, react), (table_hbm, tab)))]
    for copy in loads:
        copy.start()
    for dx, dz in OFFSETS:
        greet(place.neighbour(dx, dz))
        count += 1
    for stage in range(2):
        for i in far_first(stage):
            greet(place.group(stage, i))
            count += 1

    m = Masks(place.depth)
    loads[0].wait()
    loads[1].wait()
    for f in range(4):
        for x in range(2):
            for i in range(4):
                lanes = slice(i * 128, (i + 1) * 128)
                piece = vel[2 * f + x, :, lanes] if f < 3 else react[x, :, lanes]
                send0.reshape(128, 128)[pl.ds(f * 8 + x * 4 + i, 4, stride=32), :] = piece
    pl.semaphore_wait(barrier, count)

    own = place.x == place.gy
    into = pl.ds(pl.multiple_of(place.gy * 8, 8), 8)
    for part_of, fields in ((0, pl.ds(0, 3)), (1, pl.ds(3, 1))):
        for i in (2, 1, 3, 0):
            device, turn = place.worker(i)
            push(send0.at[turn, fields], recv0.at[fields, into], device,
                 sem0.at[part_of, i], sem0.at[part_of, 4], None if i else own)

    loads[2].wait()

    def get(row):
        return tab[row]

    def taken(first, number):
        ref = recv0.at[pl.ds(first, number)]
        pltpu.make_async_copy(ref, ref, sem0.at[0 if number == 3 else 1, 4]).wait()
        return [jnp.stack([recv0[f, pl.ds(i, 8, stride=4), :] for f in range(first, first + number)]) for i in range(4)]


    def send(r, axial, depth, edge=None, far=None):
        send_x[r][...] = axial
        send_z[r][...] = depth
        if edge is not None:
            send_far[r % 2, 0] = edge
            send_far[r % 2, 1] = far
        for dx, dz in OFFSETS[4:ROUNDS[r][1]] + OFFSETS[2:4] + OFFSETS[0:2]:
            slot = OFFSETS.index((-dx, -dz))
            source = send_x[r] if dz == 0 else send_z[r]
            if edge is not None and abs(dx) + abs(dz) == 2:
                source = send_far.at[r % 2, 0 if dx else 1]
            pltpu.make_async_remote_copy(
                source, got_refs[r].at[slot], round_sem.at[0, r], round_sem.at[1, r],
                device_id=place.neighbour(dx, dz), device_id_type=MESH).start()

    def receive(r):
        pltpu.make_async_copy(got_refs[r], got_refs[r], round_sem.at[1, r]).wait()
        return [got_refs[r][k] for k in range(ROUNDS[r][1])]

    def send_faces(r, along_axis, along_depth):
        axial = pack_axial(along_axis, m)
        send(r, axial, pack_depth(along_depth, m))
        return axial

    def give_back(g):
        first, number = GROUPS[g]
        fields = pl.ds(first, number)
        into = pl.ds(pl.multiple_of(place.turn * 8, 8), 8)
        for i in (2, 1, 3, 0):
            device, cross = place.home(i)
            rows = pl.ds(pl.multiple_of(cross * 8, 8), 8)
            push(back_send.at[fields, rows], back_recv.at[fields, into], device,
                 back_sem.at[i, g], back_sem.at[4, g], None if i else own)

    def keep(f, v):
        for i in range(4):
            back_send[f, pl.ds(i, 8, stride=4), :] = v[i]

    v = join_block(taken(0, 3), m)
    send(0, *pack(v, m))
    wt = Weights(get, m)
    scaled = [x * mass for x, mass in zip(taken(3, 1), wt.mass)]
    react_sum = join_block(scaled, m)
    send(1, *pack(react_sum, m))
    inside = STEP * m.interior
    rate = ([inside * h for h in m.hx], inside * m.hy, inside * m.hz)
    v = unpack(v, receive(0), m)
    u = [v[i] * m.inverse[i] for i in range(4)]

    for r in (2, 3):
        da = along_a(u, get, "da", m)
        dc = along_lanes(u, get, "dc", 1)
        axial = send_faces(r, da, dc)
        db = join_cross(along_lanes(u, get, "db", 8), m)
        first = [rate[0][i] * u[i][0:1] for i in range(4)]
        third = [rate[2] * u[i][2:3] for i in range(4)]
        base = [m.interior * u[i] - (first[i] * da[i] + rate[1] * u[i][1:2] * db[i] + third[i] * dc[i]) for i in range(4)]
        if r == 3:
            react_sum = unpack(react_sum, receive(1), m)
            diag = [wt.diag[i] + react_sum[i] for i in range(4)]
            inverse_diag = [1.0 / x for x in diag]
            step = ([wt.yz * x for x in inverse_diag],
                    [wt.xz[i] * inverse_diag[i] for i in range(4)],
                    [wt.xy[i] * inverse_diag[i] for i in range(4)],
                    [react_sum[i] * inverse_diag[i] - 1.0 for i in range(4)])
            volume = [-wt.all[i] * inverse_diag[i] for i in range(4)]
            weight = [diag[i][0] * m.inverse[i] for i in range(4)]
            keep(3, [x[0] for x in diag])
        across, depth = partners(axial, receive(r), m)
        u = [base[i] - third[i] * depth[i] for i in range(4)]
        for i in across:
            u[i] = u[i] - first[i] * across[i]

    da = along_a([x[0:1] for x in u], get, "da", m)
    dc = along_lanes([x[2:3] for x in u], get, "dc", 1)
    db = join_cross(along_lanes([x[1:2] for x in u], get, "db", 8), m)
    base = [volume[i] * (m.hx[i] * da[i] + m.hy * db[i] + m.hz * dc[i]) for i in range(4)]
    pa, pc = [volume[i] * m.hx[i] for i in range(4)], [volume[i] * m.hz for i in range(4)]
    tiles = pair_pack(da, dc, base, pa, pc, get, m)
    send(4, *tiles)
    for k in range(3):
        keep(k, [x[k] for x in u])
    give_back(0)
    x, across, depth = pair_unpack(tiles[0][0:1], receive(4), da, dc, base, pa, pc, get, m)
    q = [x, operate(x, across, depth, step, get, m)]

    ka, kb, kc = along_a(q[1], get, "ka", m), along_lanes(q[1], get, "kb", 8), along_lanes(q[1], get, "kc", 1)
    kb = join_cross(kb, m)
    base = [step[0][i] * ka[i] + step[1][i] * kb[i] + step[2][i] * kc[i] + step[3][i] * q[1][i] for i in range(4)]
    tiles = pair_pack(ka, kc, base, step[0], step[2], get, m)
    send(5, *tiles)
    early = moment(0, q[0], q[0], weight) + moment(1, q[0], q[1], weight) + moment(2, q[1], q[1], weight)
    for j in range(2):
        keep(4 + j, [x[0] for x in q[j]])
    x, across, depth = pair_unpack(tiles[0][0:1], receive(5), ka, kc, base, step[0], step[2], get, m)
    q += [x, operate(x, across, depth, step, get, m)]

    early = early + moment(3, q[1], q[2], weight) + moment(4, q[2], q[2], weight)
    ka, kb, kc = along_a(q[3], get, "ka", m), along_lanes(q[3], get, "kb", 8), along_lanes(q[3], get, "kc", 1)
    energy = [
        wt.wb * wt.wc * ka[i] + wt.wa[i] * (wt.wc * kb[i] + wt.wb * kc[i]) + scaled[i] * q[3][i] for i in range(4)
    ]
    part[0] = (early + moment(5, q[2], q[3], weight)) + (moment(6, q[3], q[3], weight) + moment(7, q[3], energy))

    def send_sum(stage):
        for i in far_first(stage):
            pltpu.make_async_remote_copy(part.at[stage], sums[stage].at[mirror(stage, i) - 1], sum_sem.at[0, stage],
                                         sum_sem.at[1, stage], device_id=place.group(stage, i), device_id_type=MESH).start()

    def take_sum(stage):
        pltpu.make_async_copy(sums[stage], sums[stage], sum_sem.at[1, stage]).wait()
        return sum_of([part[stage]] + [sums[stage][i] for i in range(MEMBERS[stage] - 1)])

    send_sum(0)
    axial = send_faces(6, ka, kc)
    kb = join_cross(kb, m)
    base = [wt.yz * ka[i] + wt.xz[i] * kb[i] + wt.xy[i] * kc[i] + react_sum[i] * q[3][i] for i in range(4)]
    for j in (2, 3):
        keep(4 + j, [x[0] for x in q[j]])
    give_back(1)
    give_back(2)
    part[1] = take_sum(0)
    send_sum(1)
    across, depth = partners(axial, receive(6), m)
    w = [base[i] + wt.xy[i] * depth[i] for i in range(4)]
    for i in across:
        w[i] = w[i] + wt.yz * across[i]
    keep(8, [x[0] for x in w])
    give_back(3)
    for g, (first, number) in enumerate(GROUPS):
        ref = back_recv.at[pl.ds(first, number)]
        pltpu.make_async_copy(ref, ref, back_sem.at[4, g]).wait()
    home_ref[...] = back_recv[...]

    for r in range(rounds):
        pltpu.make_async_copy(got_refs[r], got_refs[r], round_sem.at[0, r]).wait()
    for stage in range(2):
        pltpu.make_async_copy(sums[stage], sums[stage], sum_sem.at[0, stage]).wait()

    def sent(i):
        for part_of, number in ((0, 3), (1, 1)):
            ref = recv0.at[pl.ds(0, number), pl.ds(0, 8)]
            pltpu.make_async_copy(ref, ref, sem0.at[part_of, i]).wait()
        for g, (first, number) in enumerate(GROUPS):
            ref = back_recv.at[pl.ds(first, number), pl.ds(0, 8)]
            pltpu.make_async_copy(ref, ref, back_sem.at[i, g]).wait()

    for i in range(1, 4):
        sent(i)

    @pl.when(jnp.logical_not(own))
    def _():
        sent(0)

    total_ref[...] = take_sum(1)


def combine(home, total_ref, velo_ref, press_ref, resid_ref, scratch):
    lane = lax.broadcasted_iota(jnp.int32, (8, 128), 1)
    row = lax.broadcasted_iota(jnp.int32, (8, 128), 0)
    n = jnp.sum(jnp.where((lane >> 4) == row, total_ref[...], 0.0), axis=1, keepdims=True)
    n = jnp.broadcast_to(n, (8, 128))
    c = solve([n[i:i + 1, :] for i in range(7)], n[7:8, :])
    d, q0, q1, q2, q3, w3 = [home[f] for f in range(3, 9)]
    scratch[0] = c[0] * q0 + c[1] * q1 + c[2] * q2 + c[3] * q3
    scratch[1] = d * (q0 - c[0] * (q0 + q1) - c[1] * (q1 + q2) - c[2] * (q2 + q3)) - c[3] * w3
    for x in range(2):
        for i in range(4):
            rows, lanes = pl.ds(x * 4 + i, 4, stride=8), slice(i * 128, (i + 1) * 128)
            press_ref[x, :, lanes] = scratch[0, rows, :]
            resid_ref[x, :, lanes] = scratch[1, rows, :]
            for f in range(3):
                velo_ref[2 * f + x, :, lanes] = home[f, rows, :]


def body(velocity, reaction, table):
    f32 = jnp.float32
    spec = pl.BlockSpec(memory_space=pl.ANY)
    vmem = pl.BlockSpec(memory_space=pltpu.VMEM)
    scratch = [
        pltpu.VMEM((6, 4, 512), f32), pltpu.VMEM((2, 4, 512), f32), pltpu.VMEM(table.shape, f32),
        pltpu.SemaphoreType.DMA((3,)),
        pltpu.VMEM((4, 4, 8, 128), f32), pltpu.VMEM((4, 32, 128), f32), pltpu.SemaphoreType.DMA((2, 5)),
    ]
    scratch += [pltpu.VMEM((n, 8, 128), f32) for n, _ in ROUNDS] * 2
    scratch += [pltpu.VMEM((k, n, 8, 128), f32) for n, k in ROUNDS]
    scratch += [
        pltpu.VMEM((2, 2, 2, 8, 128), f32), pltpu.SemaphoreType.DMA((2, len(ROUNDS))),
        pltpu.VMEM((2, 1, 128), f32), pltpu.VMEM((MEMBERS[0] - 1, 1, 128), f32), pltpu.VMEM((MEMBERS[1] - 1, 1, 128), f32),
        pltpu.SemaphoreType.DMA((2, 2)),
        pltpu.VMEM((9, 32, 128), f32), pltpu.VMEM((9, 32, 128), f32), pltpu.SemaphoreType.DMA((5, 4)),
    ]
    home, total = pl.pallas_call(
        kernel,
        out_shape=[pltpu.VMEM((9, 32, 128), f32), pltpu.VMEM((1, 128), f32)],
        in_specs=[spec] * 3,
        out_specs=[vmem] * 2,
        scratch_shapes=scratch,
        compiler_params=pltpu.CompilerParams(collective_id=0, has_side_effects=True),
        name="duct_step",
    )(velocity.reshape(6, 4, 512), reaction.reshape(2, 4, 512), table)
    velo, press, resid = pl.pallas_call(
        combine,
        out_shape=[jax.ShapeDtypeStruct((6, 4, 512), f32)] + [jax.ShapeDtypeStruct((2, 4, 512), f32)] * 2,
        in_specs=[vmem] * 2,
        out_specs=[vmem] * 3,
        scratch_shapes=[pltpu.VMEM((2, 32, 128), f32)],
        name="combine",
    )(pltpu.with_memory_space_constraint(home, pltpu.VMEM), pltpu.with_memory_space_constraint(total, pltpu.VMEM))
    return velo.reshape(velocity.shape), press.reshape(reaction.shape), resid.reshape(reaction.shape)


def solution(mesh):
    specs = (P(None, "gx", "gy", "gz", None), P("gx", "gy", "gz", None))

    def step(velocity, reaction):
        return body(velocity, reaction, jnp.asarray(TABLE))

    return jax.shard_map(
        step, mesh=mesh, in_specs=specs, out_specs=(specs[0], specs[1], specs[1]), check_vma=False
    )
```

```python
import jax
import jax.numpy as jnp
import numpy as np
from jax import lax
from jax.experimental import pallas as pl
from jax.experimental.pallas import tpu as pltpu
from jax.sharding import PartitionSpec as P

MESH = pl.DeviceIdType.MESH
STEP = 0.02
HALF = 64
OFFSETS = ((-1, 0), (1, 0), (0, -1), (0, 1), (-1, -1), (1, -1), (-1, 1), (1, 1), (0, -2), (0, 2))
ROUNDS = ((3, 8), (1, 8), (3, 4), (3, 4), (2, 10), (2, 10), (1, 4))
GROUPS = ((0, 3), (3, 4), (7, 1), (8, 1))


def roll(values, shift, axis):
    shift = shift % values.shape[axis]
    return values if shift == 0 else pltpu.roll(values, shift, axis)


def div(value, by):
    return value // by if isinstance(value, (int, np.ndarray)) else lax.div(value, np.int32(by))


def rem(value, by):
    return value % by if isinstance(value, (int, np.ndarray)) else lax.rem(value, np.int32(by))


def tables():
    half = np.array([0.2092992179024788687, 0.5917001814331423022, 0.8717401485096066153, 1.0])
    points = np.concatenate([-half[::-1], half])
    earlier, current = points * 0.0 + 1.0, points
    for degree in range(1, 7):
        earlier, current = current, ((2 * degree + 1) * points * current - degree * earlier) / (degree + 1)
    w = 2.0 / (56.0 * current**2)
    spacing = points[:, None] - points[None, :] + np.eye(8)
    d = current[:, None] / current[None, :] / spacing * (1.0 - np.eye(8))
    d[0, 0] = -14.0
    d[7, 7] = 14.0
    k = d.T @ np.diag(w) @ d
    lane = np.arange(128)
    c, b, a_lo = lane % 8, (lane // 8) % 8, lane // 64
    rows = {}

    def put(name, values):
        rows[name] = (len(stack), len(values))
        stack.extend(values)

    stack = []

    def along_a(matrix, scale):
        return [matrix[2 * j + a_lo, q] * scale for j in range(4) for q in range(8)]

    def shifts(matrix, index, scale):
        out = []
        for s in range(-7, 8):
            source = index - s
            inside = (source >= 0) & (source <= 7)
            out.append(np.where(inside, matrix[index, np.clip(source, 0, 7)], 0.0) * scale)
        return out

    one = np.ones(128)
    put("da", along_a(d, one))
    put("db", shifts(d, b, one))
    put("dc", shifts(d, c, one))
    put("ka", along_a(k, one))
    put("kb", shifts(k, b, one))
    put("kc", shifts(k, c, one))
    s = (w[:, None] * d * d).sum(0)
    put("wa", [w[2 * i + a_lo] for i in range(4)])
    put("wb", [w[b]])
    put("wc", [w[c]])
    put("sa", [s[2 * i + a_lo] for i in range(4)])
    put("sb", [s[b]])
    put("sc", [s[c]])
    table = np.stack(stack).astype(np.float32)
    whole = np.ascontiguousarray(np.broadcast_to(table[:, None, :], (len(stack), 8, 128)))
    return whole, rows, float(k[0, 0]), float(k[0, 7])


TABLE, ROWS, NEAR, FAR = tables()


def owner_of(axial, depth):
    y, core = div(axial, 2), rem(axial, 2)
    z, turn = div(depth, 4), rem(depth, 4)
    x = turn + rem(z, 2) * (3 - 2 * turn)
    return (div(y, 4) * 8 + x * 2 + core, rem(y, 4), z)


class Place:
    def __init__(self, gx, gy, gz):
        self.gx, self.gy, self.gz = gx, gy, gz
        self.core, self.x, self.y_hi = rem(gx, 2), rem(div(gx, 2), 4), div(gx, 8)
        self.y, self.z = self.y_hi * 4 + gy, gz
        self.axial = self.y * 2 + self.core
        self.turn = self.x + rem(gz, 2) * (3 - 2 * self.x)
        self.depth = self.z * 4 + self.turn

    def mesh_id(self, x, y, z, core):
        return (div(y, 4) * 8 + x * 2 + core, rem(y, 4), z)

    def neighbour(self, dx, dz):
        return owner_of(rem(self.axial + dx + 16, 16), rem(self.depth + dz + 32, 32))

    def worker(self, i):
        x = rem(self.x + i, 4)
        return self.mesh_id(x, self.y_hi * 4 + self.x, self.z, self.core), x + rem(self.z, 2) * (3 - 2 * x)

    def home(self, i):
        cross = rem(self.gy + i, 4)
        return self.mesh_id(self.gy, self.y_hi * 4 + cross, self.z, self.core), cross

    def group(self, stage, i):
        if stage == 0:
            return self.mesh_id(self.x, self.y, rem(self.z + i // 2, 8), rem(self.core + i % 2, 2))
        return self.mesh_id(rem(self.x + i // 8, 4), rem(self.y + i % 8, 8), self.z, self.core)


MEMBERS = (16, 32)


def far_first(stage):
    def hops(i):
        if stage == 0:
            return (min(i // 2, 8 - i // 2), i % 2)
        return (min(i // 8, 4 - i // 8) + min(i % 8, 8 - i % 8), 0)

    return sorted(range(1, MEMBERS[stage]), key=hops, reverse=True)


def mirror(stage, i):
    if stage == 0:
        return (8 - i // 2) % 8 * 2 + i % 2
    return (4 - i // 8) % 4 * 8 + (8 - i % 8) % 8


class Masks:
    def __init__(self, depth):
        lane = lax.broadcasted_iota(jnp.int32, (8, 128), 1)
        row = lax.broadcasted_iota(jnp.int32, (8, 128), 0)
        c, b = lane & 7, (lane >> 3) & 7
        cross = row >> 1
        self.low = lane < HALF
        self.even = (row & 1) == 0
        odd = (row & 1) == 1
        high = lane >= HALF
        self.b0 = (b == 0) & (cross > 0)
        self.b7 = (b == 7) & (cross < 3)
        self.in0 = odd & self.low
        self.in3 = self.even & high
        self.out0 = self.even & self.low
        self.out3 = odd & high
        self.c = c
        self.c0, self.c7 = c == 0, c == 7
        self.slot_low = c < 4
        self.edge0 = self.out0 & ((c & 3) == 0)
        self.edge3 = self.out3 & ((c & 3) == 3)
        up = (depth < 31).astype(jnp.float32)
        down = (depth > 0).astype(jnp.float32)
        self.zmask = jnp.where(self.slot_low, up, down)
        self.far = jnp.where(self.slot_low, (depth < 30).astype(jnp.float32), (depth > 1).astype(jnp.float32)) * FAR
        self.faces = self.c0 | self.c7
        self.zhas = jnp.where(self.c0, down, jnp.where(self.c7, up, 0.0))
        one = jnp.ones((8, 128), jnp.float32)
        first, last = jnp.where(self.low, 0.5, one), jnp.where(self.low, one, 0.5)
        self.hx = [first, one, one, last]
        self.hy = jnp.where(self.b0 | self.b7, 0.5, one)
        self.hz = jnp.where(self.c0, 1.0 - 0.5 * down, jnp.where(self.c7, 1.0 - 0.5 * up, one))
        self.inverse = [x * (self.hy * self.hz) for x in self.hx]
        wall_y = ((b == 0) & (cross == 0)) | ((b == 7) & (cross == 3))
        self.interior = jnp.where(wall_y, 0.0, jnp.where(self.c0, down, jnp.where(self.c7, up, one)))


class Weights:
    def __init__(self, get, m):
        def row(name, i=0):
            return get(ROWS[name][0] + i)

        self.wa, self.wb, self.wc = [row("wa", i) for i in range(4)], row("wb"), row("wc")
        two_x, two_y, two_z = [1.0 / h for h in m.hx], 1.0 / m.hy, 1.0 / m.hz
        self.mx, self.my, self.mz = [x * t for x, t in zip(self.wa, two_x)], self.wb * two_y, self.wc * two_z
        self.yz = self.my * self.mz
        self.xz = [x * self.mz for x in self.mx]
        self.xy = [x * self.my for x in self.mx]
        self.all = [x * self.yz for x in self.mx]
        self.mass = [x * (self.wb * self.wc) for x in self.wa]
        self.diag = [
            row("sa", i) * two_x[i] * self.yz + row("sb") * two_y * self.xz[i] + row("sc") * two_z * self.xy[i]
            for i in range(4)
        ]


def join_cross(v, m):
    out = []
    for x in v:
        g = roll(roll(x, 2, 1), -56, 2)
        h = roll(roll(x, -2, 1), 56, 2)
        out.append(x + jnp.where(m.b0, g, jnp.where(m.b7, h, 0.0)))
    return out


def join_block(v, m):
    out = join_cross(v, m)
    first = roll(roll(out[3], 1, 1), HALF, 2)
    last = roll(roll(out[0], -1, 1), HALF, 2)
    out[0] = out[0] + jnp.where(m.in0, first, 0.0)
    out[3] = out[3] + jnp.where(m.in3, last, 0.0)
    return out


def pack(v, m):
    return jnp.where(m.low, v[0], v[3]), pack_depth(v, m)


def pack_depth(v, m):
    depth = v[0]
    for i in range(1, 4):
        if v[i] is not None:
            depth = jnp.where(m.c == i, roll(v[i], i, 2), depth)
    for i in range(4):
        if v[i] is not None:
            depth = jnp.where(m.c == 4 + i, roll(v[i], i - 3, 2), depth)
    return depth


def pack_edges(depth, m):
    out = depth[0:1]
    for k in range(1, depth.shape[0]):
        moved = jnp.where(m.even, roll(depth[k:k + 1], k, 2), roll(depth[k:k + 1], -k, 2))
        out = jnp.where((m.c & 3) == jnp.where(m.even, k, 3 - k), moved, out)
    return out


def pack_axial(v, m):
    faces = roll(jnp.where(m.low, v[0], v[3]), HALF, 2)
    return jnp.where(m.even, roll(faces, -1, 1), roll(faces, 1, 1))


def spread(face, i, m):
    return jnp.where(m.c7, roll(face, 7 - i, 2), jnp.where(m.c0, roll(face, -4 - i, 2), 0.0))


def edges(got, m):
    before = jnp.where(m.slot_low, got[6], got[4])
    after = jnp.where(m.slot_low, got[7], got[5])
    return (jnp.where(m.edge0, roll(roll(before, -1, 1), -67, 2), 0.0)
            + jnp.where(m.edge3, roll(roll(after, 1, 1), 67, 2), 0.0)) * m.zmask


def pair_pack(fa, fc, base, pa, pc, get, m):
    axial = pack_axial(fa, m)
    own = list(base)
    own[0] = own[0] + pa[0] * jnp.where(m.in0, axial, 0.0)
    own[3] = own[3] + pa[3] * jnp.where(m.in3, axial, 0.0)
    ka = along_a(own, get, "ka", m, (0, 3))
    kc = along_lanes(own, get, "kc", 1)
    reach = [pc[i] * fc[i] for i in range(4)]
    ea = along_a([jnp.where(m.faces, x, 0.0) for x in reach], get, "ka", m, (0, 3))
    first, last = along_lanes([jnp.where(m.low, pa[0] * fa[0], 0.0), jnp.where(m.low, 0.0, pa[3] * fa[3])], get, "kc", 1)
    return (jnp.concatenate([axial, pack_axial(ka, m)], axis=0),
            jnp.concatenate([pack_depth(fc, m), pack_depth(kc, m)], axis=0),
            jnp.concatenate([pack_depth(ea, m), pack_depth([first, None, None, last], m)], axis=0),
            jnp.concatenate([pack_depth(reach, m), pack_depth(reach, m)], axis=0))


def pair_unpack(axial, got, fa, fc, base, pa, pc, get, m):
    across, depth = partners(axial, [g[0:1] for g in got], m)
    x = [base[i] + pc[i] * depth[i] for i in range(4)]
    for i in across:
        x[i] = x[i] + pa[i] * across[i]
    ga = edges([g[0:1] for g in got], m)
    second = [g[1:2] for g in got]
    face = jnp.where(m.slot_low, second[3], second[2]) * m.zmask + edges(second, m)
    face = face + jnp.where(m.slot_low, got[9][0:1], got[8][0:1]) * m.far
    depth = [spread(face, i, m) + NEAR * m.zhas * (pc[i] * fc[i]) for i in range(4)]
    across = {0: jnp.where(m.out0, second[0] + NEAR * (pa[0] * fa[0]), 0.0) + spread(ga, 0, m),
              3: jnp.where(m.out3, second[1] + NEAR * (pa[3] * fa[3]), 0.0) + spread(ga, 3, m)}
    return x, across, depth


def operate(x, across, depth, step, get, m):
    ka = along_a(x, get, "ka", m)
    kb = join_cross(along_lanes(x, get, "kb", 8), m)
    kc = along_lanes(x, get, "kc", 1)
    axial = pack_axial(ka, m)
    across = {0: across[0] + jnp.where(m.in0, axial, 0.0), 3: across[3] + jnp.where(m.in3, axial, 0.0)}
    out = [step[1][i] * kb[i] + step[2][i] * (kc[i] + depth[i]) + step[3][i] * x[i] for i in range(4)]
    return [out[i] + step[0][i] * (ka[i] + across[i] if i in across else ka[i]) for i in range(4)]


def partners(own, got, m):
    across = jnp.where(m.in0 | m.in3, own, jnp.where(m.low, got[0], got[1]))
    face = jnp.where(m.slot_low, got[3], got[2]) * m.zmask
    depth = [spread(face, i, m) for i in range(4)]
    return {0: jnp.where(m.low, across, 0.0), 3: jnp.where(m.low, 0.0, across)}, depth


def unpack(v, got, m):
    v = list(v)
    v[0] = v[0] + jnp.where(m.out0, roll(roll(got[0], -1, 1), HALF, 2), 0.0)
    v[3] = v[3] + jnp.where(m.out3, roll(roll(got[1], 1, 1), HALF, 2), 0.0)
    centre = jnp.where(m.slot_low, got[3], got[2])
    before = roll(jnp.where(m.slot_low, got[6], got[4]), -1, 1)
    after = roll(jnp.where(m.slot_low, got[7], got[5]), 1, 1)
    fields = range(v[0].shape[0])
    face = centre + jnp.where(m.edge0, jnp.concatenate([roll(before, k - 67, 2) for k in fields], axis=0), 0.0)
    face = face + jnp.where(m.edge3, jnp.concatenate([roll(after, 67 - k, 2) for k in fields], axis=0), 0.0)
    face = face * m.zmask
    return [
        v[i] + jnp.where(m.c7, roll(face, 7 - i, 2), jnp.where(m.c0, roll(face, -4 - i, 2), 0.0))
        for i in range(4)
    ]


def along_a(v, get, name, m, wanted=range(4)):
    parts = []
    for x in v:
        turned = roll(x, HALF, 2)
        parts.append(jnp.where(m.low, x, turned))
        parts.append(jnp.where(m.low, turned, x))
    start = ROWS[name][0]
    return [sum_of([get(start + j * 8 + q) * parts[q] for q in range(8)]) if j in wanted else None for j in range(4)]


def along_lanes(v, get, name, stride):
    start = ROWS[name][0]
    return [sum_of([get(start + s + 7) * roll(x, s * stride, 2) for s in range(-7, 8)]) for x in v]


def sum_of(terms):
    while len(terms) > 1:
        terms = [terms[i] + terms[i + 1] if i + 1 < len(terms) else terms[i] for i in range(0, len(terms), 2)]
    return terms[0]


def moment(k, f, g, weight=None):
    total = sum_of([f[i][0] * g[i][0] if weight is None else f[i][0] * g[i][0] * weight[i] for i in range(4)])
    total = jnp.sum(total, axis=0, keepdims=True)
    for shift in (64, 32, 16):
        total = total + roll(total, shift, 1)
    lane = lax.broadcasted_iota(jnp.int32, (1, 128), 1)
    return jnp.where((lane >> 4) == k, total, 0.0)


def solve(n, e):
    g = [[(n[i + j] + n[i + j + 1]) if i + j < 6 else e for j in range(4)] for i in range(4)]
    rhs = [n[i] for i in range(4)]
    inverse = []
    for i in range(4):
        inverse.append(1.0 / g[i][i])
        for r in range(i + 1, 4):
            factor = g[r][i] * inverse[i]
            for j in range(i + 1, 4):
                g[r][j] = g[r][j] - factor * g[i][j]
            rhs[r] = rhs[r] - factor * rhs[i]
    out = [None] * 4
    for i in range(3, -1, -1):
        total = rhs[i]
        for j in range(i + 1, 4):
            total = total - g[i][j] * out[j]
        out[i] = total * inverse[i]
    return out


def kernel(vel_hbm, react_hbm, table_hbm, home_ref, total_ref, vel, react, tab, load_sem,
           send0, recv0, sem0, *rest):
    rounds = len(ROUNDS)
    send_x, send_z = rest[0:rounds], rest[rounds:2 * rounds]
    got_refs = rest[2 * rounds:3 * rounds]
    (send_edge, send_far, round_sem, part, sums0, sums1, sum_sem, back_send, back_recv, back_sem) = rest[3 * rounds:]
    sums = (sums0, sums1)
    place = Place(lax.axis_index("gx"), lax.axis_index("gy"), lax.axis_index("gz"))

    def push(source, target, device, send_sem, recv_sem, own=None):
        def remote():
            pltpu.make_async_remote_copy(source, target, send_sem, recv_sem, device_id=device, device_id_type=MESH).start()

        if own is None:
            remote()
            return
        pl.when(jnp.logical_not(own))(remote)

        @pl.when(own)
        def _():
            pltpu.make_async_copy(source, target, recv_sem).start()

    def greet(device):
        pl.semaphore_signal(barrier, inc=1, device_id=device, device_id_type=MESH)

    barrier = pltpu.get_barrier_semaphore()
    count = 0
    for i in range(4):
        greet(place.worker(i)[0])
        greet(place.home(i)[0])
        count += 2
    loads = [pltpu.make_async_copy(s, d, load_sem.at[k]) for k, (s, d) in
             enumerate(((vel_hbm, vel), (react_hbm, react), (table_hbm, tab)))]
    for copy in loads:
        copy.start()
    for dx, dz in OFFSETS:
        greet(place.neighbour(dx, dz))
        count += 1
    for stage in range(2):
        for i in far_first(stage):
            greet(place.group(stage, i))
            count += 1

    m = Masks(place.depth)
    loads[0].wait()
    loads[1].wait()
    for f in range(4):
        for x in range(2):
            for i in range(4):
                lanes = slice(i * 128, (i + 1) * 128)
                piece = vel[2 * f + x, :, lanes] if f < 3 else react[x, :, lanes]
                send0.reshape(128, 128)[pl.ds(f * 8 + x * 4 + i, 4, stride=32), :] = piece
    pl.semaphore_wait(barrier, count)

    own = place.x == place.gy
    into = pl.ds(pl.multiple_of(place.gy * 8, 8), 8)
    for part_of, fields in ((0, pl.ds(0, 3)), (1, pl.ds(3, 1))):
        for i in (2, 1, 3, 0):
            device, turn = place.worker(i)
            push(send0.at[turn, fields], recv0.at[fields, into], device,
                 sem0.at[part_of, i], sem0.at[part_of, 4], None if i else own)

    loads[2].wait()

    def get(row):
        return tab[row]

    def taken(first, number):
        ref = recv0.at[pl.ds(first, number)]
        pltpu.make_async_copy(ref, ref, sem0.at[0 if number == 3 else 1, 4]).wait()
        return [jnp.stack([recv0[f, pl.ds(i, 8, stride=4), :] for f in range(first, first + number)]) for i in range(4)]


    def send(r, axial, depth, edge=None, far=None):
        send_x[r][...] = axial
        send_z[r][...] = depth
        if edge is not None:
            send_far[r % 2, 0] = edge
            send_far[r % 2, 1] = far
        for dx, dz in OFFSETS[4:ROUNDS[r][1]] + OFFSETS[2:4] + OFFSETS[0:2]:
            slot = OFFSETS.index((-dx, -dz))
            source = send_x[r] if dz == 0 else send_z[r]
            target = got_refs[r].at[slot]
            if edge is not None and abs(dx) + abs(dz) == 2:
                source = send_far.at[r % 2, 0 if dx else 1]
            if r == 0:
                target = got_refs[0].at[pl.ds(3 * slot, 3) if slot < 4 else pl.ds(8 + slot, 1)]
                source = source if slot < 4 else send_edge
            pltpu.make_async_remote_copy(
                source, target, round_sem.at[0, r], round_sem.at[1, r],
                device_id=place.neighbour(dx, dz), device_id_type=MESH).start()

    def receive(r):
        pltpu.make_async_copy(got_refs[r], got_refs[r], round_sem.at[1, r]).wait()
        if r == 0:
            return [got_refs[0][3 * k:3 * k + 3] if k < 4 else got_refs[0][8 + k:9 + k] for k in range(8)]
        return [got_refs[r][k] for k in range(ROUNDS[r][1])]

    def send_faces(r, along_axis, along_depth):
        axial = pack_axial(along_axis, m)
        send(r, axial, pack_depth(along_depth, m))
        return axial

    def give_back(g):
        first, number = GROUPS[g]
        fields = pl.ds(first, number)
        into = pl.ds(pl.multiple_of(place.turn * 8, 8), 8)
        for i in (2, 1, 3, 0):
            device, cross = place.home(i)
            rows = pl.ds(pl.multiple_of(cross * 8, 8), 8)
            push(back_send.at[fields, rows], back_recv.at[fields, into], device,
                 back_sem.at[i, g], back_sem.at[4, g], None if i else own)

    def keep(f, v):
        for i in range(4):
            back_send[f, pl.ds(i, 8, stride=4), :] = v[i]

    v = join_block(taken(0, 3), m)
    axial, depth = pack(v, m)
    send_edge[...] = pack_edges(depth, m)
    send(0, axial, depth)
    wt = Weights(get, m)
    scaled = [x * mass for x, mass in zip(taken(3, 1), wt.mass)]
    react_sum = join_block(scaled, m)
    send(1, *pack(react_sum, m))
    inside = STEP * m.interior
    rate = ([inside * h for h in m.hx], inside * m.hy, inside * m.hz)
    v = unpack(v, receive(0), m)
    u = [v[i] * m.inverse[i] for i in range(4)]

    for r in (2, 3):
        da = along_a(u, get, "da", m)
        dc = along_lanes(u, get, "dc", 1)
        axial = send_faces(r, da, dc)
        db = join_cross(along_lanes(u, get, "db", 8), m)
        first = [rate[0][i] * u[i][0:1] for i in range(4)]
        third = [rate[2] * u[i][2:3] for i in range(4)]
        base = [m.interior * u[i] - (first[i] * da[i] + rate[1] * u[i][1:2] * db[i] + third[i] * dc[i]) for i in range(4)]
        if r == 3:
            react_sum = unpack(react_sum, receive(1), m)
            diag = [wt.diag[i] + react_sum[i] for i in range(4)]
            inverse_diag = [1.0 / x for x in diag]
            step = ([wt.yz * x for x in inverse_diag],
                    [wt.xz[i] * inverse_diag[i] for i in range(4)],
                    [wt.xy[i] * inverse_diag[i] for i in range(4)],
                    [react_sum[i] * inverse_diag[i] - 1.0 for i in range(4)])
            volume = [-wt.all[i] * inverse_diag[i] for i in range(4)]
            weight = [diag[i][0] * m.inverse[i] for i in range(4)]
            keep(3, [x[0] for x in diag])
        across, depth = partners(axial, receive(r), m)
        u = [base[i] - third[i] * depth[i] for i in range(4)]
        for i in across:
            u[i] = u[i] - first[i] * across[i]

    da = along_a([x[0:1] for x in u], get, "da", m)
    dc = along_lanes([x[2:3] for x in u], get, "dc", 1)
    db = join_cross(along_lanes([x[1:2] for x in u], get, "db", 8), m)
    base = [volume[i] * (m.hx[i] * da[i] + m.hy * db[i] + m.hz * dc[i]) for i in range(4)]
    pa, pc = [volume[i] * m.hx[i] for i in range(4)], [volume[i] * m.hz for i in range(4)]
    tiles = pair_pack(da, dc, base, pa, pc, get, m)
    send(4, *tiles)
    for k in range(3):
        keep(k, [x[k] for x in u])
    give_back(0)
    x, across, depth = pair_unpack(tiles[0][0:1], receive(4), da, dc, base, pa, pc, get, m)
    q = [x, operate(x, across, depth, step, get, m)]

    ka, kb, kc = along_a(q[1], get, "ka", m), along_lanes(q[1], get, "kb", 8), along_lanes(q[1], get, "kc", 1)
    kb = join_cross(kb, m)
    base = [step[0][i] * ka[i] + step[1][i] * kb[i] + step[2][i] * kc[i] + step[3][i] * q[1][i] for i in range(4)]
    tiles = pair_pack(ka, kc, base, step[0], step[2], get, m)
    send(5, *tiles)
    early = moment(0, q[0], q[0], weight) + moment(1, q[0], q[1], weight) + moment(2, q[1], q[1], weight)
    for j in range(2):
        keep(4 + j, [x[0] for x in q[j]])
    x, across, depth = pair_unpack(tiles[0][0:1], receive(5), ka, kc, base, step[0], step[2], get, m)
    q += [x, operate(x, across, depth, step, get, m)]

    early = early + moment(3, q[1], q[2], weight) + moment(4, q[2], q[2], weight)
    ka, kb, kc = along_a(q[3], get, "ka", m), along_lanes(q[3], get, "kb", 8), along_lanes(q[3], get, "kc", 1)
    energy = [
        wt.wb * wt.wc * ka[i] + wt.wa[i] * (wt.wc * kb[i] + wt.wb * kc[i]) + scaled[i] * q[3][i] for i in range(4)
    ]
    part[0] = (early + moment(5, q[2], q[3], weight)) + (moment(6, q[3], q[3], weight) + moment(7, q[3], energy))

    def send_sum(stage):
        for i in far_first(stage):
            pltpu.make_async_remote_copy(part.at[stage], sums[stage].at[mirror(stage, i) - 1], sum_sem.at[0, stage],
                                         sum_sem.at[1, stage], device_id=place.group(stage, i), device_id_type=MESH).start()

    def take_sum(stage):
        pltpu.make_async_copy(sums[stage], sums[stage], sum_sem.at[1, stage]).wait()
        return sum_of([part[stage]] + [sums[stage][i] for i in range(MEMBERS[stage] - 1)])

    send_sum(0)
    axial = send_faces(6, ka, kc)
    kb = join_cross(kb, m)
    base = [wt.yz * ka[i] + wt.xz[i] * kb[i] + wt.xy[i] * kc[i] + react_sum[i] * q[3][i] for i in range(4)]
    for j in (2, 3):
        keep(4 + j, [x[0] for x in q[j]])
    give_back(1)
    give_back(2)
    part[1] = take_sum(0)
    send_sum(1)
    across, depth = partners(axial, receive(6), m)
    w = [base[i] + wt.xy[i] * depth[i] for i in range(4)]
    for i in across:
        w[i] = w[i] + wt.yz * across[i]
    keep(8, [x[0] for x in w])
    give_back(3)
    for g, (first, number) in enumerate(GROUPS):
        ref = back_recv.at[pl.ds(first, number)]
        pltpu.make_async_copy(ref, ref, back_sem.at[4, g]).wait()
    home_ref[...] = back_recv[...]

    for r in range(rounds):
        pltpu.make_async_copy(got_refs[r], got_refs[r], round_sem.at[0, r]).wait()
    for stage in range(2):
        pltpu.make_async_copy(sums[stage], sums[stage], sum_sem.at[0, stage]).wait()

    def sent(i):
        for part_of, number in ((0, 3), (1, 1)):
            ref = recv0.at[pl.ds(0, number), pl.ds(0, 8)]
            pltpu.make_async_copy(ref, ref, sem0.at[part_of, i]).wait()
        for g, (first, number) in enumerate(GROUPS):
            ref = back_recv.at[pl.ds(first, number), pl.ds(0, 8)]
            pltpu.make_async_copy(ref, ref, back_sem.at[i, g]).wait()

    for i in range(1, 4):
        sent(i)

    @pl.when(jnp.logical_not(own))
    def _():
        sent(0)

    total_ref[...] = take_sum(1)


def combine(home, total_ref, velo_ref, press_ref, resid_ref, scratch):
    lane = lax.broadcasted_iota(jnp.int32, (8, 128), 1)
    row = lax.broadcasted_iota(jnp.int32, (8, 128), 0)
    n = jnp.sum(jnp.where((lane >> 4) == row, total_ref[...], 0.0), axis=1, keepdims=True)
    n = jnp.broadcast_to(n, (8, 128))
    c = solve([n[i:i + 1, :] for i in range(7)], n[7:8, :])
    d, q0, q1, q2, q3, w3 = [home[f] for f in range(3, 9)]
    scratch[0] = c[0] * q0 + c[1] * q1 + c[2] * q2 + c[3] * q3
    scratch[1] = d * (q0 - c[0] * (q0 + q1) - c[1] * (q1 + q2) - c[2] * (q2 + q3)) - c[3] * w3
    for x in range(2):
        for i in range(4):
            rows, lanes = pl.ds(x * 4 + i, 4, stride=8), slice(i * 128, (i + 1) * 128)
            press_ref[x, :, lanes] = scratch[0, rows, :]
            resid_ref[x, :, lanes] = scratch[1, rows, :]
            for f in range(3):
                velo_ref[2 * f + x, :, lanes] = home[f, rows, :]


def body(velocity, reaction, table):
    f32 = jnp.float32
    spec = pl.BlockSpec(memory_space=pl.ANY)
    vmem = pl.BlockSpec(memory_space=pltpu.VMEM)
    scratch = [
        pltpu.VMEM((6, 4, 512), f32), pltpu.VMEM((2, 4, 512), f32), pltpu.VMEM(table.shape, f32),
        pltpu.SemaphoreType.DMA((3,)),
        pltpu.VMEM((4, 4, 8, 128), f32), pltpu.VMEM((4, 32, 128), f32), pltpu.SemaphoreType.DMA((2, 5)),
    ]
    scratch += [pltpu.VMEM((n, 8, 128), f32) for n, _ in ROUNDS] * 2
    scratch += [pltpu.VMEM((k, n, 8, 128) if r else (16, 8, 128), f32) for r, (n, k) in enumerate(ROUNDS)]
    scratch += [
        pltpu.VMEM((1, 8, 128), f32), pltpu.VMEM((2, 2, 2, 8, 128), f32), pltpu.SemaphoreType.DMA((2, len(ROUNDS))),
        pltpu.VMEM((2, 1, 128), f32), pltpu.VMEM((MEMBERS[0] - 1, 1, 128), f32), pltpu.VMEM((MEMBERS[1] - 1, 1, 128), f32),
        pltpu.SemaphoreType.DMA((2, 2)),
        pltpu.VMEM((9, 32, 128), f32), pltpu.VMEM((9, 32, 128), f32), pltpu.SemaphoreType.DMA((5, 4)),
    ]
    home, total = pl.pallas_call(
        kernel,
        out_shape=[pltpu.VMEM((9, 32, 128), f32), pltpu.VMEM((1, 128), f32)],
        in_specs=[spec] * 3,
        out_specs=[vmem] * 2,
        scratch_shapes=scratch,
        compiler_params=pltpu.CompilerParams(collective_id=0, has_side_effects=True),
        name="duct_step",
    )(velocity.reshape(6, 4, 512), reaction.reshape(2, 4, 512), table)
    velo, press, resid = pl.pallas_call(
        combine,
        out_shape=[jax.ShapeDtypeStruct((6, 4, 512), f32)] + [jax.ShapeDtypeStruct((2, 4, 512), f32)] * 2,
        in_specs=[vmem] * 2,
        out_specs=[vmem] * 3,
        scratch_shapes=[pltpu.VMEM((2, 32, 128), f32)],
        name="combine",
    )(pltpu.with_memory_space_constraint(home, pltpu.VMEM), pltpu.with_memory_space_constraint(total, pltpu.VMEM))
    return velo.reshape(velocity.shape), press.reshape(reaction.shape), resid.reshape(reaction.shape)


def solution(mesh):
    specs = (P(None, "gx", "gy", "gz", None), P("gx", "gy", "gz", None))

    def step(velocity, reaction):
        return body(velocity, reaction, jnp.asarray(TABLE))

    return jax.shard_map(
        step, mesh=mesh, in_specs=specs, out_specs=(specs[0], specs[1], specs[1]), check_vma=False
    )
```

```python
import jax
import jax.numpy as jnp
import numpy as np
from jax import lax
from jax.experimental import pallas as pl
from jax.experimental.pallas import tpu as pltpu
from jax.sharding import PartitionSpec as P

MESH = pl.DeviceIdType.MESH
STEP = 0.02
HALF = 64
OFFSETS = ((-1, 0), (1, 0), (0, -1), (0, 1), (-1, -1), (1, -1), (-1, 1), (1, 1), (0, -2), (0, 2))
ROUNDS = ((3, 8), (1, 8), (3, 4), (3, 4), (2, 10), (2, 10), (1, 4))
GROUPS = ((0, 3), (3, 4), (7, 1), (8, 1))


def roll(values, shift, axis):
    shift = shift % values.shape[axis]
    return values if shift == 0 else pltpu.roll(values, shift, axis)


def div(value, by):
    return value // by if isinstance(value, (int, np.ndarray)) else lax.div(value, np.int32(by))


def rem(value, by):
    return value % by if isinstance(value, (int, np.ndarray)) else lax.rem(value, np.int32(by))


def tables():
    half = np.array([0.2092992179024788687, 0.5917001814331423022, 0.8717401485096066153, 1.0])
    points = np.concatenate([-half[::-1], half])
    earlier, current = points * 0.0 + 1.0, points
    for degree in range(1, 7):
        earlier, current = current, ((2 * degree + 1) * points * current - degree * earlier) / (degree + 1)
    w = 2.0 / (56.0 * current**2)
    spacing = points[:, None] - points[None, :] + np.eye(8)
    d = current[:, None] / current[None, :] / spacing * (1.0 - np.eye(8))
    d[0, 0] = -14.0
    d[7, 7] = 14.0
    k = d.T @ np.diag(w) @ d
    lane = np.arange(128)
    c, b, a_lo = lane % 8, (lane // 8) % 8, lane // 64
    rows = {}

    def put(name, values):
        rows[name] = (len(stack), len(values))
        stack.extend(values)

    stack = []

    def along_a(matrix, scale):
        return [matrix[2 * j + a_lo, q] * scale for j in range(4) for q in range(8)]

    def shifts(matrix, index, scale):
        out = []
        for s in range(-7, 8):
            source = index - s
            inside = (source >= 0) & (source <= 7)
            out.append(np.where(inside, matrix[index, np.clip(source, 0, 7)], 0.0) * scale)
        return out

    one = np.ones(128)
    put("da", along_a(d, one))
    put("db", shifts(d, b, one))
    put("dc", shifts(d, c, one))
    put("ka", along_a(k, one))
    put("kb", shifts(k, b, one))
    put("kc", shifts(k, c, one))
    s = (w[:, None] * d * d).sum(0)
    put("wa", [w[2 * i + a_lo] for i in range(4)])
    put("wb", [w[b]])
    put("wc", [w[c]])
    put("sa", [s[2 * i + a_lo] for i in range(4)])
    put("sb", [s[b]])
    put("sc", [s[c]])
    table = np.stack(stack).astype(np.float32)
    whole = np.ascontiguousarray(np.broadcast_to(table[:, None, :], (len(stack), 8, 128)))
    return whole, rows, float(k[0, 0]), float(k[0, 7])


TABLE, ROWS, NEAR, FAR = tables()


def owner_of(axial, depth):
    y, core = div(axial, 2), rem(axial, 2)
    z, turn = div(depth, 4), rem(depth, 4)
    x = turn + rem(z, 2) * (3 - 2 * turn)
    return (div(y, 4) * 8 + x * 2 + core, rem(y, 4), z)


class Place:
    def __init__(self, gx, gy, gz):
        self.gx, self.gy, self.gz = gx, gy, gz
        self.core, self.x, self.y_hi = rem(gx, 2), rem(div(gx, 2), 4), div(gx, 8)
        self.y, self.z = self.y_hi * 4 + gy, gz
        self.axial = self.y * 2 + self.core
        self.turn = self.x + rem(gz, 2) * (3 - 2 * self.x)
        self.depth = self.z * 4 + self.turn

    def mesh_id(self, x, y, z, core):
        return (div(y, 4) * 8 + x * 2 + core, rem(y, 4), z)

    def neighbour(self, dx, dz):
        return owner_of(rem(self.axial + dx + 16, 16), rem(self.depth + dz + 32, 32))

    def worker(self, i):
        x = rem(self.x + i, 4)
        return self.mesh_id(x, self.y_hi * 4 + self.x, self.z, self.core), x + rem(self.z, 2) * (3 - 2 * x)

    def home(self, i):
        cross = rem(self.gy + i, 4)
        return self.mesh_id(self.gy, self.y_hi * 4 + cross, self.z, self.core), cross

    def group(self, stage, i):
        if stage == 0:
            return self.mesh_id(self.x, self.y, rem(self.z + i // 2, 8), rem(self.core + i % 2, 2))
        return self.mesh_id(rem(self.x + i // 8, 4), rem(self.y + i % 8, 8), self.z, self.core)


MEMBERS = (16, 32)


def far_first(stage):
    def hops(i):
        if stage == 0:
            return (min(i // 2, 8 - i // 2), i % 2)
        return (min(i // 8, 4 - i // 8) + min(i % 8, 8 - i % 8), 0)

    return sorted(range(1, MEMBERS[stage]), key=hops, reverse=True)


def mirror(stage, i):
    if stage == 0:
        return (8 - i // 2) % 8 * 2 + i % 2
    return (4 - i // 8) % 4 * 8 + (8 - i % 8) % 8


class Masks:
    def __init__(self, depth):
        lane = lax.broadcasted_iota(jnp.int32, (8, 128), 1)
        row = lax.broadcasted_iota(jnp.int32, (8, 128), 0)
        c, b = lane & 7, (lane >> 3) & 7
        cross = row >> 1
        self.low = lane < HALF
        self.even = (row & 1) == 0
        odd = (row & 1) == 1
        high = lane >= HALF
        self.b0 = (b == 0) & (cross > 0)
        self.b7 = (b == 7) & (cross < 3)
        self.in0 = odd & self.low
        self.in3 = self.even & high
        self.out0 = self.even & self.low
        self.out3 = odd & high
        self.c = c
        self.c0, self.c7 = c == 0, c == 7
        self.slot_low = c < 4
        self.edge0 = self.out0 & ((c & 3) == 0)
        self.edge3 = self.out3 & ((c & 3) == 3)
        up = (depth < 31).astype(jnp.float32)
        down = (depth > 0).astype(jnp.float32)
        self.zmask = jnp.where(self.slot_low, up, down)
        self.far = jnp.where(self.slot_low, (depth < 30).astype(jnp.float32), (depth > 1).astype(jnp.float32)) * FAR
        self.faces = self.c0 | self.c7
        self.zhas = jnp.where(self.c0, down, jnp.where(self.c7, up, 0.0))
        one = jnp.ones((8, 128), jnp.float32)
        first, last = jnp.where(self.low, 0.5, one), jnp.where(self.low, one, 0.5)
        self.hx = [first, one, one, last]
        self.hy = jnp.where(self.b0 | self.b7, 0.5, one)
        self.hz = jnp.where(self.c0, 1.0 - 0.5 * down, jnp.where(self.c7, 1.0 - 0.5 * up, one))
        self.inverse = [x * (self.hy * self.hz) for x in self.hx]
        wall_y = ((b == 0) & (cross == 0)) | ((b == 7) & (cross == 3))
        self.interior = jnp.where(wall_y, 0.0, jnp.where(self.c0, down, jnp.where(self.c7, up, one)))


class Weights:
    def __init__(self, get, m):
        def row(name, i=0):
            return get(ROWS[name][0] + i)

        self.wa, self.wb, self.wc = [row("wa", i) for i in range(4)], row("wb"), row("wc")
        two_x, two_y, two_z = [1.0 / h for h in m.hx], 1.0 / m.hy, 1.0 / m.hz
        self.mx, self.my, self.mz = [x * t for x, t in zip(self.wa, two_x)], self.wb * two_y, self.wc * two_z
        self.yz = self.my * self.mz
        self.xz = [x * self.mz for x in self.mx]
        self.xy = [x * self.my for x in self.mx]
        self.all = [x * self.yz for x in self.mx]
        self.mass = [x * (self.wb * self.wc) for x in self.wa]
        self.diag = [
            row("sa", i) * two_x[i] * self.yz + row("sb") * two_y * self.xz[i] + row("sc") * two_z * self.xy[i]
            for i in range(4)
        ]


def join_cross(v, m):
    out = []
    for x in v:
        g = roll(roll(x, 2, 1), -56, 2)
        h = roll(roll(x, -2, 1), 56, 2)
        out.append(x + jnp.where(m.b0, g, jnp.where(m.b7, h, 0.0)))
    return out


def join_block(v, m):
    out = join_cross(v, m)
    first = roll(roll(out[3], 1, 1), HALF, 2)
    last = roll(roll(out[0], -1, 1), HALF, 2)
    out[0] = out[0] + jnp.where(m.in0, first, 0.0)
    out[3] = out[3] + jnp.where(m.in3, last, 0.0)
    return out


def pack(v, m):
    return jnp.where(m.low, v[0], v[3]), pack_depth(v, m)


def pack_depth(v, m):
    depth = v[0]
    for i in range(1, 4):
        if v[i] is not None:
            depth = jnp.where(m.c == i, roll(v[i], i, 2), depth)
    for i in range(4):
        if v[i] is not None:
            depth = jnp.where(m.c == 4 + i, roll(v[i], i - 3, 2), depth)
    return depth


def pack_edges(depth, m):
    out = depth[0:1]
    for k in range(1, depth.shape[0]):
        moved = jnp.where(m.even, roll(depth[k:k + 1], k, 2), roll(depth[k:k + 1], -k, 2))
        out = jnp.where((m.c & 3) == jnp.where(m.even, k, 3 - k), moved, out)
    return out


def pack_axial(v, m):
    faces = roll(jnp.where(m.low, v[0], v[3]), HALF, 2)
    return jnp.where(m.even, roll(faces, -1, 1), roll(faces, 1, 1))


def spread(face, i, m):
    return jnp.where(m.c7, roll(face, 7 - i, 2), jnp.where(m.c0, roll(face, -4 - i, 2), 0.0))


def edges(got, m, k):
    before = roll(jnp.where(m.slot_low, got[6], got[4]), -1, 1)
    after = roll(jnp.where(m.slot_low, got[7], got[5]), 1, 1)
    return (jnp.where(m.edge0, roll(before, k - 67, 2), 0.0) + jnp.where(m.edge3, roll(after, 67 - k, 2), 0.0)) * m.zmask


def pair_pack(fa, fc, base, pa, pc, get, m):
    axial = pack_axial(fa, m)
    own = list(base)
    own[0] = own[0] + pa[0] * jnp.where(m.in0, axial, 0.0)
    own[3] = own[3] + pa[3] * jnp.where(m.in3, axial, 0.0)
    ka = along_a(own, get, "ka", m, (0, 3))
    kc = along_lanes(own, get, "kc", 1)
    reach = [pc[i] * fc[i] for i in range(4)]
    ea = along_a([jnp.where(m.faces, x, 0.0) for x in reach], get, "ka", m, (0, 3))
    first, last = along_lanes([jnp.where(m.low, pa[0] * fa[0], 0.0), jnp.where(m.low, 0.0, pa[3] * fa[3])], get, "kc", 1)
    return (jnp.concatenate([axial, pack_axial(ka, m)], axis=0),
            jnp.concatenate([pack_depth(fc, m), pack_depth(kc, m)], axis=0),
            pack_edges(jnp.concatenate([pack_depth(ea, m), pack_depth([first, None, None, last], m)], axis=0), m),
            pack_depth(reach, m))


def pair_unpack(axial, got, fa, fc, base, pa, pc, get, m):
    across, depth = partners(axial, [g[0:1] for g in got[:4]], m)
    x = [base[i] + pc[i] * depth[i] for i in range(4)]
    for i in across:
        x[i] = x[i] + pa[i] * across[i]
    ga = edges(got, m, 0)
    second = [g[1:2] for g in got[:4]]
    face = jnp.where(m.slot_low, second[3], second[2]) * m.zmask + edges(got, m, 1)
    face = face + jnp.where(m.slot_low, got[9][0:1], got[8][0:1]) * m.far
    depth = [spread(face, i, m) + NEAR * m.zhas * (pc[i] * fc[i]) for i in range(4)]
    across = {0: jnp.where(m.out0, second[0] + NEAR * (pa[0] * fa[0]), 0.0) + spread(ga, 0, m),
              3: jnp.where(m.out3, second[1] + NEAR * (pa[3] * fa[3]), 0.0) + spread(ga, 3, m)}
    return x, across, depth


def operate(x, across, depth, step, get, m):
    ka = along_a(x, get, "ka", m)
    kb = join_cross(along_lanes(x, get, "kb", 8), m)
    kc = along_lanes(x, get, "kc", 1)
    axial = pack_axial(ka, m)
    across = {0: across[0] + jnp.where(m.in0, axial, 0.0), 3: across[3] + jnp.where(m.in3, axial, 0.0)}
    out = [step[1][i] * kb[i] + step[2][i] * (kc[i] + depth[i]) + step[3][i] * x[i] for i in range(4)]
    return [out[i] + step[0][i] * (ka[i] + across[i] if i in across else ka[i]) for i in range(4)]


def partners(own, got, m):
    across = jnp.where(m.in0 | m.in3, own, jnp.where(m.low, got[0], got[1]))
    face = jnp.where(m.slot_low, got[3], got[2]) * m.zmask
    depth = [spread(face, i, m) for i in range(4)]
    return {0: jnp.where(m.low, across, 0.0), 3: jnp.where(m.low, 0.0, across)}, depth


def unpack(v, got, m):
    v = list(v)
    v[0] = v[0] + jnp.where(m.out0, roll(roll(got[0], -1, 1), HALF, 2), 0.0)
    v[3] = v[3] + jnp.where(m.out3, roll(roll(got[1], 1, 1), HALF, 2), 0.0)
    centre = jnp.where(m.slot_low, got[3], got[2])
    before = roll(jnp.where(m.slot_low, got[6], got[4]), -1, 1)
    after = roll(jnp.where(m.slot_low, got[7], got[5]), 1, 1)
    fields = range(v[0].shape[0])
    face = centre + jnp.where(m.edge0, jnp.concatenate([roll(before, k - 67, 2) for k in fields], axis=0), 0.0)
    face = face + jnp.where(m.edge3, jnp.concatenate([roll(after, 67 - k, 2) for k in fields], axis=0), 0.0)
    face = face * m.zmask
    return [
        v[i] + jnp.where(m.c7, roll(face, 7 - i, 2), jnp.where(m.c0, roll(face, -4 - i, 2), 0.0))
        for i in range(4)
    ]


def along_a(v, get, name, m, wanted=range(4)):
    parts = []
    for x in v:
        turned = roll(x, HALF, 2)
        parts.append(jnp.where(m.low, x, turned))
        parts.append(jnp.where(m.low, turned, x))
    start = ROWS[name][0]
    return [sum_of([get(start + j * 8 + q) * parts[q] for q in range(8)]) if j in wanted else None for j in range(4)]


def along_lanes(v, get, name, stride):
    start = ROWS[name][0]
    return [sum_of([get(start + s + 7) * roll(x, s * stride, 2) for s in range(-7, 8)]) for x in v]


def sum_of(terms):
    while len(terms) > 1:
        terms = [terms[i] + terms[i + 1] if i + 1 < len(terms) else terms[i] for i in range(0, len(terms), 2)]
    return terms[0]


def moment(k, f, g, weight=None):
    total = sum_of([f[i][0] * g[i][0] if weight is None else f[i][0] * g[i][0] * weight[i] for i in range(4)])
    total = jnp.sum(total, axis=0, keepdims=True)
    for shift in (64, 32, 16):
        total = total + roll(total, shift, 1)
    lane = lax.broadcasted_iota(jnp.int32, (1, 128), 1)
    return jnp.where((lane >> 4) == k, total, 0.0)


def solve(n, e):
    g = [[(n[i + j] + n[i + j + 1]) if i + j < 6 else e for j in range(4)] for i in range(4)]
    rhs = [n[i] for i in range(4)]
    inverse = []
    for i in range(4):
        inverse.append(1.0 / g[i][i])
        for r in range(i + 1, 4):
            factor = g[r][i] * inverse[i]
            for j in range(i + 1, 4):
                g[r][j] = g[r][j] - factor * g[i][j]
            rhs[r] = rhs[r] - factor * rhs[i]
    out = [None] * 4
    for i in range(3, -1, -1):
        total = rhs[i]
        for j in range(i + 1, 4):
            total = total - g[i][j] * out[j]
        out[i] = total * inverse[i]
    return out


def kernel(vel_hbm, react_hbm, table_hbm, home_ref, total_ref, vel, react, tab, load_sem,
           send0, recv0, sem0, *rest):
    rounds = len(ROUNDS)
    send_x, send_z = rest[0:rounds], rest[rounds:2 * rounds]
    got_refs = rest[2 * rounds:3 * rounds]
    (send_edge, send_far, round_sem, part, sums0, sums1, sum_sem, back_send, back_recv, back_sem) = rest[3 * rounds:]
    sums = (sums0, sums1)
    place = Place(lax.axis_index("gx"), lax.axis_index("gy"), lax.axis_index("gz"))

    def push(source, target, device, send_sem, recv_sem, own=None):
        def remote():
            pltpu.make_async_remote_copy(source, target, send_sem, recv_sem, device_id=device, device_id_type=MESH).start()

        if own is None:
            remote()
            return
        pl.when(jnp.logical_not(own))(remote)

        @pl.when(own)
        def _():
            pltpu.make_async_copy(source, target, recv_sem).start()

    def greet(device):
        pl.semaphore_signal(barrier, inc=1, device_id=device, device_id_type=MESH)

    barrier = pltpu.get_barrier_semaphore()
    count = 0
    for i in range(4):
        greet(place.worker(i)[0])
        greet(place.home(i)[0])
        count += 2
    loads = [pltpu.make_async_copy(s, d, load_sem.at[k]) for k, (s, d) in
             enumerate(((vel_hbm, vel), (react_hbm, react), (table_hbm, tab)))]
    for copy in loads:
        copy.start()
    for dx, dz in OFFSETS:
        greet(place.neighbour(dx, dz))
        count += 1
    for stage in range(2):
        for i in far_first(stage):
            greet(place.group(stage, i))
            count += 1

    m = Masks(place.depth)
    loads[0].wait()
    loads[1].wait()
    for f in range(4):
        for x in range(2):
            for i in range(4):
                lanes = slice(i * 128, (i + 1) * 128)
                piece = vel[2 * f + x, :, lanes] if f < 3 else react[x, :, lanes]
                send0.reshape(128, 128)[pl.ds(f * 8 + x * 4 + i, 4, stride=32), :] = piece
    pl.semaphore_wait(barrier, count)

    own = place.x == place.gy
    into = pl.ds(pl.multiple_of(place.gy * 8, 8), 8)
    for part_of, fields in ((0, pl.ds(0, 3)), (1, pl.ds(3, 1))):
        for i in (2, 1, 3, 0):
            device, turn = place.worker(i)
            push(send0.at[turn, fields], recv0.at[fields, into], device,
                 sem0.at[part_of, i], sem0.at[part_of, 4], None if i else own)

    loads[2].wait()

    def get(row):
        return tab[row]

    def taken(first, number):
        ref = recv0.at[pl.ds(first, number)]
        pltpu.make_async_copy(ref, ref, sem0.at[0 if number == 3 else 1, 4]).wait()
        return [jnp.stack([recv0[f, pl.ds(i, 8, stride=4), :] for f in range(first, first + number)]) for i in range(4)]


    def send(r, axial, depth, edge=None, far=None):
        send_x[r][...] = axial
        send_z[r][...] = depth
        if edge is not None:
            send_far[r % 2, 0] = edge
            send_far[r % 2, 1] = far
        for dx, dz in OFFSETS[4:ROUNDS[r][1]] + OFFSETS[2:4] + OFFSETS[0:2]:
            slot = OFFSETS.index((-dx, -dz))
            source = send_x[r] if dz == 0 else send_z[r]
            target = got_refs[r].at[slot]
            if edge is not None:
                target = got_refs[r].at[pl.ds(2 * slot, 2) if slot < 4 else pl.ds(4 + slot, 1)]
                source = source if slot < 4 else send_far.at[r % 2, 0 if dx else 1]
            if r == 0:
                target = got_refs[0].at[pl.ds(3 * slot, 3) if slot < 4 else pl.ds(8 + slot, 1)]
                source = source if slot < 4 else send_edge
            pltpu.make_async_remote_copy(
                source, target, round_sem.at[0, r], round_sem.at[1, r],
                device_id=place.neighbour(dx, dz), device_id_type=MESH).start()

    def receive(r):
        pltpu.make_async_copy(got_refs[r], got_refs[r], round_sem.at[1, r]).wait()
        if r == 0:
            return [got_refs[0][3 * k:3 * k + 3] if k < 4 else got_refs[0][8 + k:9 + k] for k in range(8)]
        if ROUNDS[r][1] == 10:
            return [got_refs[r][2 * k:2 * k + 2] if k < 4 else got_refs[r][4 + k:5 + k] for k in range(10)]
        return [got_refs[r][k] for k in range(ROUNDS[r][1])]

    def send_faces(r, along_axis, along_depth):
        axial = pack_axial(along_axis, m)
        send(r, axial, pack_depth(along_depth, m))
        return axial

    def give_back(g):
        first, number = GROUPS[g]
        fields = pl.ds(first, number)
        into = pl.ds(pl.multiple_of(place.turn * 8, 8), 8)
        for i in (2, 1, 3, 0):
            device, cross = place.home(i)
            rows = pl.ds(pl.multiple_of(cross * 8, 8), 8)
            push(back_send.at[fields, rows], back_recv.at[fields, into], device,
                 back_sem.at[i, g], back_sem.at[4, g], None if i else own)

    def keep(f, v):
        for i in range(4):
            back_send[f, pl.ds(i, 8, stride=4), :] = v[i]

    v = join_block(taken(0, 3), m)
    axial, depth = pack(v, m)
    send_edge[...] = pack_edges(depth, m)
    send(0, axial, depth)
    wt = Weights(get, m)
    scaled = [x * mass for x, mass in zip(taken(3, 1), wt.mass)]
    react_sum = join_block(scaled, m)
    send(1, *pack(react_sum, m))
    inside = STEP * m.interior
    rate = ([inside * h for h in m.hx], inside * m.hy, inside * m.hz)
    v = unpack(v, receive(0), m)
    u = [v[i] * m.inverse[i] for i in range(4)]

    for r in (2, 3):
        da = along_a(u, get, "da", m)
        dc = along_lanes(u, get, "dc", 1)
        axial = send_faces(r, da, dc)
        db = join_cross(along_lanes(u, get, "db", 8), m)
        first = [rate[0][i] * u[i][0:1] for i in range(4)]
        third = [rate[2] * u[i][2:3] for i in range(4)]
        base = [m.interior * u[i] - (first[i] * da[i] + rate[1] * u[i][1:2] * db[i] + third[i] * dc[i]) for i in range(4)]
        if r == 3:
            react_sum = unpack(react_sum, receive(1), m)
            diag = [wt.diag[i] + react_sum[i] for i in range(4)]
            inverse_diag = [1.0 / x for x in diag]
            step = ([wt.yz * x for x in inverse_diag],
                    [wt.xz[i] * inverse_diag[i] for i in range(4)],
                    [wt.xy[i] * inverse_diag[i] for i in range(4)],
                    [react_sum[i] * inverse_diag[i] - 1.0 for i in range(4)])
            volume = [-wt.all[i] * inverse_diag[i] for i in range(4)]
            weight = [diag[i][0] * m.inverse[i] for i in range(4)]
            keep(3, [x[0] for x in diag])
        across, depth = partners(axial, receive(r), m)
        u = [base[i] - third[i] * depth[i] for i in range(4)]
        for i in across:
            u[i] = u[i] - first[i] * across[i]

    da = along_a([x[0:1] for x in u], get, "da", m)
    dc = along_lanes([x[2:3] for x in u], get, "dc", 1)
    db = join_cross(along_lanes([x[1:2] for x in u], get, "db", 8), m)
    base = [volume[i] * (m.hx[i] * da[i] + m.hy * db[i] + m.hz * dc[i]) for i in range(4)]
    pa, pc = [volume[i] * m.hx[i] for i in range(4)], [volume[i] * m.hz for i in range(4)]
    tiles = pair_pack(da, dc, base, pa, pc, get, m)
    send(4, *tiles)
    for k in range(3):
        keep(k, [x[k] for x in u])
    give_back(0)
    x, across, depth = pair_unpack(tiles[0][0:1], receive(4), da, dc, base, pa, pc, get, m)
    q = [x, operate(x, across, depth, step, get, m)]

    ka, kb, kc = along_a(q[1], get, "ka", m), along_lanes(q[1], get, "kb", 8), along_lanes(q[1], get, "kc", 1)
    kb = join_cross(kb, m)
    base = [step[0][i] * ka[i] + step[1][i] * kb[i] + step[2][i] * kc[i] + step[3][i] * q[1][i] for i in range(4)]
    tiles = pair_pack(ka, kc, base, step[0], step[2], get, m)
    send(5, *tiles)
    early = moment(0, q[0], q[0], weight) + moment(1, q[0], q[1], weight) + moment(2, q[1], q[1], weight)
    for j in range(2):
        keep(4 + j, [x[0] for x in q[j]])
    x, across, depth = pair_unpack(tiles[0][0:1], receive(5), ka, kc, base, step[0], step[2], get, m)
    q += [x, operate(x, across, depth, step, get, m)]

    early = early + moment(3, q[1], q[2], weight) + moment(4, q[2], q[2], weight)
    ka, kb, kc = along_a(q[3], get, "ka", m), along_lanes(q[3], get, "kb", 8), along_lanes(q[3], get, "kc", 1)
    energy = [
        wt.wb * wt.wc * ka[i] + wt.wa[i] * (wt.wc * kb[i] + wt.wb * kc[i]) + scaled[i] * q[3][i] for i in range(4)
    ]
    part[0] = (early + moment(5, q[2], q[3], weight)) + (moment(6, q[3], q[3], weight) + moment(7, q[3], energy))

    def send_sum(stage):
        for i in far_first(stage):
            pltpu.make_async_remote_copy(part.at[stage], sums[stage].at[mirror(stage, i) - 1], sum_sem.at[0, stage],
                                         sum_sem.at[1, stage], device_id=place.group(stage, i), device_id_type=MESH).start()

    def take_sum(stage):
        pltpu.make_async_copy(sums[stage], sums[stage], sum_sem.at[1, stage]).wait()
        return sum_of([part[stage]] + [sums[stage][i] for i in range(MEMBERS[stage] - 1)])

    send_sum(0)
    axial = send_faces(6, ka, kc)
    kb = join_cross(kb, m)
    base = [wt.yz * ka[i] + wt.xz[i] * kb[i] + wt.xy[i] * kc[i] + react_sum[i] * q[3][i] for i in range(4)]
    for j in (2, 3):
        keep(4 + j, [x[0] for x in q[j]])
    give_back(1)
    give_back(2)
    part[1] = take_sum(0)
    send_sum(1)
    across, depth = partners(axial, receive(6), m)
    w = [base[i] + wt.xy[i] * depth[i] for i in range(4)]
    for i in across:
        w[i] = w[i] + wt.yz * across[i]
    keep(8, [x[0] for x in w])
    give_back(3)
    for g, (first, number) in enumerate(GROUPS):
        ref = back_recv.at[pl.ds(first, number)]
        pltpu.make_async_copy(ref, ref, back_sem.at[4, g]).wait()
    home_ref[...] = back_recv[...]

    for r in range(rounds):
        pltpu.make_async_copy(got_refs[r], got_refs[r], round_sem.at[0, r]).wait()
    for stage in range(2):
        pltpu.make_async_copy(sums[stage], sums[stage], sum_sem.at[0, stage]).wait()

    def sent(i):
        for part_of, number in ((0, 3), (1, 1)):
            ref = recv0.at[pl.ds(0, number), pl.ds(0, 8)]
            pltpu.make_async_copy(ref, ref, sem0.at[part_of, i]).wait()
        for g, (first, number) in enumerate(GROUPS):
            ref = back_recv.at[pl.ds(first, number), pl.ds(0, 8)]
            pltpu.make_async_copy(ref, ref, back_sem.at[i, g]).wait()

    for i in range(1, 4):
        sent(i)

    @pl.when(jnp.logical_not(own))
    def _():
        sent(0)

    total_ref[...] = take_sum(1)


def combine(home, total_ref, velo_ref, press_ref, resid_ref, scratch):
    lane = lax.broadcasted_iota(jnp.int32, (8, 128), 1)
    row = lax.broadcasted_iota(jnp.int32, (8, 128), 0)
    n = jnp.sum(jnp.where((lane >> 4) == row, total_ref[...], 0.0), axis=1, keepdims=True)
    n = jnp.broadcast_to(n, (8, 128))
    c = solve([n[i:i + 1, :] for i in range(7)], n[7:8, :])
    d, q0, q1, q2, q3, w3 = [home[f] for f in range(3, 9)]
    scratch[0] = c[0] * q0 + c[1] * q1 + c[2] * q2 + c[3] * q3
    scratch[1] = d * (q0 - c[0] * (q0 + q1) - c[1] * (q1 + q2) - c[2] * (q2 + q3)) - c[3] * w3
    for x in range(2):
        for i in range(4):
            rows, lanes = pl.ds(x * 4 + i, 4, stride=8), slice(i * 128, (i + 1) * 128)
            press_ref[x, :, lanes] = scratch[0, rows, :]
            resid_ref[x, :, lanes] = scratch[1, rows, :]
            for f in range(3):
                velo_ref[2 * f + x, :, lanes] = home[f, rows, :]


def body(velocity, reaction, table):
    f32 = jnp.float32
    spec = pl.BlockSpec(memory_space=pl.ANY)
    vmem = pl.BlockSpec(memory_space=pltpu.VMEM)
    scratch = [
        pltpu.VMEM((6, 4, 512), f32), pltpu.VMEM((2, 4, 512), f32), pltpu.VMEM(table.shape, f32),
        pltpu.SemaphoreType.DMA((3,)),
        pltpu.VMEM((4, 4, 8, 128), f32), pltpu.VMEM((4, 32, 128), f32), pltpu.SemaphoreType.DMA((2, 5)),
    ]
    scratch += [pltpu.VMEM((n, 8, 128), f32) for n, _ in ROUNDS] * 2
    packed = {0: (16, 8, 128), 4: (14, 8, 128), 5: (14, 8, 128)}
    scratch += [pltpu.VMEM(packed.get(r, (k, n, 8, 128)), f32) for r, (n, k) in enumerate(ROUNDS)]
    scratch += [
        pltpu.VMEM((1, 8, 128), f32), pltpu.VMEM((2, 2, 1, 8, 128), f32), pltpu.SemaphoreType.DMA((2, len(ROUNDS))),
        pltpu.VMEM((2, 1, 128), f32), pltpu.VMEM((MEMBERS[0] - 1, 1, 128), f32), pltpu.VMEM((MEMBERS[1] - 1, 1, 128), f32),
        pltpu.SemaphoreType.DMA((2, 2)),
        pltpu.VMEM((9, 32, 128), f32), pltpu.VMEM((9, 32, 128), f32), pltpu.SemaphoreType.DMA((5, 4)),
    ]
    home, total = pl.pallas_call(
        kernel,
        out_shape=[pltpu.VMEM((9, 32, 128), f32), pltpu.VMEM((1, 128), f32)],
        in_specs=[spec] * 3,
        out_specs=[vmem] * 2,
        scratch_shapes=scratch,
        compiler_params=pltpu.CompilerParams(collective_id=0, has_side_effects=True),
        name="duct_step",
    )(velocity.reshape(6, 4, 512), reaction.reshape(2, 4, 512), table)
    velo, press, resid = pl.pallas_call(
        combine,
        out_shape=[jax.ShapeDtypeStruct((6, 4, 512), f32)] + [jax.ShapeDtypeStruct((2, 4, 512), f32)] * 2,
        in_specs=[vmem] * 2,
        out_specs=[vmem] * 3,
        scratch_shapes=[pltpu.VMEM((2, 32, 128), f32)],
        name="combine",
    )(pltpu.with_memory_space_constraint(home, pltpu.VMEM), pltpu.with_memory_space_constraint(total, pltpu.VMEM))
    return velo.reshape(velocity.shape), press.reshape(reaction.shape), resid.reshape(reaction.shape)


def solution(mesh):
    specs = (P(None, "gx", "gy", "gz", None), P("gx", "gy", "gz", None))

    def step(velocity, reaction):
        return body(velocity, reaction, jnp.asarray(TABLE))

    return jax.shard_map(
        step, mesh=mesh, in_specs=specs, out_specs=(specs[0], specs[1], specs[1]), check_vma=False
    )
```
